32 devices in a mesh: groups: 2 (over x), seq: 16 (over z, y, core).
Axes of the slice: x: 2, y: 2, z: 4, core: 2. Of those that a mesh axis runs over, the one named last changes fastest.
Arguments:
- query_rows: bfloat16 [8192, 2048], P(('groups', 'seq')), parts along dimension 0, may hold values from -6 to 6
- key_rows: bfloat16 [16384, 2048], P(('groups', 'seq')), parts along dimension 0, may hold values from -6 to 6
- value_rows: bfloat16 [16384, 2048], P(('groups', 'seq')), parts along dimension 0, may hold values from -6 to 6
- write_rate: float32 [16384, 16], P(('groups', 'seq')), parts along dimension 0, may hold values from 0 to 1
- log_gate: float32 [8192, 16], P(('groups', 'seq')), parts along dimension 0, may hold values from -1 to 0
- keep_mask: int32 [256, 4], P(('groups', 'seq')), parts along dimension 0, may hold values 0 or 1
- query_kernel: float32 [4, 2048], replicated, may hold values from -3 to 3
- key_kernel: float32 [4, 2048], replicated, may hold values from -3 to 3
- value_kernel: float32 [4, 2048], replicated, may hold values from -3 to 3
Outputs:
- head_outputs: bfloat16 [8192, 2048], P(('groups', 'seq')), parts along dimension 0
The draws below stay inside these ranges and needn't reach their ends.
There are 2 independent parts, one for each index of `groups`. The reference program is written for one: setup_inputs(seed, part) draws one part's arguments, and reference() takes and returns one part's arrays. A program takes and returns all parts, laid end to end along the dimension named above; an argument that names none is the same for every part. Nothing has to cross between parts.
All inputs are finite; a program needn't handle non-finite values. No bound on the sum of `keep_mask` on one device may be relied on, other than what follows from the above.
Results may differ from the reference program's by a relative error of at most 0.001.
Values may be sent and summed in bfloat16 or wider, within the bound.
No kernel may reach another device: no remote copies, remote signals or barrier semaphores. Data moves between devices by JAX's collectives and lax.ppermute only.
A program may use at most 128 MiB of HBM per device.

```python
import jax
import jax.numpy as jnp
from jax import lax

HEAD_COUNT = 16
DK = 128
NH = 2
SPAN = 64
BLOCK = 16
TOK_DEV = 256
D = 2048
STEPS_DEV = 512
SEQUENCE_TOKENS = 4096
STEPS = 8192
NCHUNKS = 128
SUBS = 4


def head_mixed(key):
    chosen = jax.random.uniform(jax.random.fold_in(key, 7), (HEAD_COUNT,), jnp.float32)
    mixed_share = 0.5
    forced_head = jax.random.randint(jax.random.fold_in(key, 8), (), 0, HEAD_COUNT)
    head_place = jnp.arange(HEAD_COUNT, dtype=jnp.int32)
    return (chosen < mixed_share) | (head_place == forced_head)


def device_quick(key):
    device_total = SEQUENCE_TOKENS // TOK_DEV
    regime = jax.random.uniform(jax.random.fold_in(key, 9), (device_total, HEAD_COUNT), jnp.float32) < 0.4
    forced_device = jax.random.randint(jax.random.fold_in(key, 10), (1, HEAD_COUNT), 2, device_total)
    device_place = jnp.arange(device_total, dtype=jnp.int32)[:, None]
    regime = jnp.where(device_place == forced_device, True, regime)
    regime = jnp.where((device_place == forced_device - 1) | (device_place == forced_device - 2), False, regime)
    return regime & head_mixed(key)[None, :]


def log_range(key, shape, lower, upper):
    return jnp.exp(jax.random.uniform(key, shape, jnp.float32, jnp.log(lower), jnp.log(upper)))


def draw_write_rate(key, part):
    quick = jnp.repeat(device_quick(key), STEPS_DEV, axis=0)
    mixed = head_mixed(key)[None, :]
    quick_low = 0.2
    quick_rate = log_range(jax.random.fold_in(key, 11), (STEPS, HEAD_COUNT), quick_low, 1.0)
    slow_rate = jnp.minimum(log_range(jax.random.fold_in(key, 12), (STEPS, HEAD_COUNT), 0.2, 1.0) * (DK / STEPS), 1.0)
    middle_rate = jnp.minimum(log_range(jax.random.fold_in(key, 13), (STEPS, HEAD_COUNT), 0.1, 0.4) * (DK / STEPS_DEV), 1.0)
    return jnp.where(quick, quick_rate, jnp.where(mixed, middle_rate, slow_rate))


def draw_log_gate(key, part):
    quick = jnp.repeat(device_quick(key), TOK_DEV, axis=0)
    quick_rate = log_range(jax.random.fold_in(key, 21), (HEAD_COUNT,), 0.02, 0.033)
    slow_rate = log_range(jax.random.fold_in(key, 22), (HEAD_COUNT,), 0.1, 1.0) / SEQUENCE_TOKENS
    baseline_rate = jnp.where(quick, quick_rate[None, :], slow_rate[None, :])
    device_multiplier = jnp.repeat(log_range(jax.random.fold_in(key, 23), (SEQUENCE_TOKENS // TOK_DEV, HEAD_COUNT), 0.5, 2.0), TOK_DEV, axis=0)
    coarse_estimate = jax.random.uniform(jax.random.fold_in(key, 24), (SEQUENCE_TOKENS, HEAD_COUNT), jnp.float32, 0.5, 1.5)
    device_positions = jax.random.randint(jax.random.fold_in(key, 25), (4, HEAD_COUNT), 0, SEQUENCE_TOKENS)
    index_of_row = jnp.arange(SEQUENCE_TOKENS, dtype=jnp.int32)[:, None, None]
    spike_amount = jnp.any(index_of_row == device_positions[None, :, :], axis=1)
    spike_penalty = jnp.log(jax.random.uniform(jax.random.fold_in(key, 26), (SEQUENCE_TOKENS, HEAD_COUNT), jnp.float32, 0.5, 0.8))
    return -baseline_rate * device_multiplier * coarse_estimate + jnp.where(spike_amount, spike_penalty, 0.0)


def place_ends(values, key, least, top_value):
    extent = values.shape
    index_at = [jax.random.randint(jax.random.fold_in(key, axis), (), 0, extent[axis]) for axis in range(len(extent))]
    values = values.at[tuple(index_at)].set(least)
    longest = extent.index(max(extent))
    index_at[longest] = (index_at[longest] + 1) % extent[longest]
    return values.at[tuple(index_at)].set(top_value)


def block_scale(key, extent, cuts, least, high):
    level, own = 1.0, jax.random.fold_in(key, 6)
    for dim, shards_of in cuts:
        steps = jnp.exp(jax.random.uniform(jax.random.fold_in(own, dim), (shards_of,), jnp.float32, least / len(cuts), high / len(cuts)))
        level = level * jnp.repeat(steps, extent[dim] // shards_of).reshape([-1 if axis == dim else 1 for axis in range(len(extent))])
    return level


def normal_values(key, extent, width, bound, cuts=(), held_as=jnp.bfloat16):
    level = block_scale(key, extent, cuts, -0.22, 0.18) if cuts else 1.0
    entries = jax.random.normal(key, extent, jnp.float32) * width * level
    return jnp.minimum(jnp.maximum(entries, -bound), bound).astype(held_as)


def setup_inputs(seed: int = 0, part: int = 0) -> dict:
    seeds = jax.random.split(jax.random.key(seed), 10)
    part_splits = jax.random.split(jax.random.fold_in(seeds[9], part), 10)
    query_rows = normal_values(part_splits[0], (SEQUENCE_TOKENS, D), 1.0, 6.0, ((0, 16),))
    key_rows = normal_values(part_splits[1], (STEPS, D), 1.0, 6.0, ((0, 16),))
    value_rows = normal_values(part_splits[2], (STEPS, D), 1.0, 6.0, ((0, 16),))
    write_rate = draw_write_rate(jax.random.fold_in(jax.random.fold_in(seeds[9], part), 71), part)
    log_gate = draw_log_gate(jax.random.fold_in(jax.random.fold_in(seeds[9], part), 71), part)
    keep_mask = place_ends((jax.random.randint(part_splits[5], (NCHUNKS, SUBS), 0, 4) < 3).astype(jnp.int32), jax.random.fold_in(part_splits[5], 1), 0, 1)
    query_kernel = normal_values(seeds[6], (4, D), 0.5, 3.0, (), jnp.float32)
    key_kernel = normal_values(seeds[7], (4, D), 0.5, 3.0, (), jnp.float32)
    value_kernel = normal_values(seeds[8], (4, D), 0.5, 3.0, (), jnp.float32)
    return dict(query_rows=query_rows, key_rows=key_rows, value_rows=value_rows, write_rate=write_rate, log_gate=log_gate, keep_mask=keep_mask, query_kernel=query_kernel, key_kernel=key_kernel, value_kernel=value_kernel)


HIGHEST = lax.Precision.HIGHEST

def conv_silu(leading, current, kernel):
    joined = jnp.concatenate([leading, current], axis=0).astype(jnp.float32)
    length = current.shape[0]
    total = kernel[0] * joined[0:length]
    for offset in range(1, 4):
        total = total + kernel[offset] * joined[offset:offset + length]
    return jax.nn.silu(total)

def unit_heads(rows_in, heads):
    shaped = rows_in.reshape(rows_in.shape[0], heads, -1)
    return shaped * lax.rsqrt(lax.optimization_barrier(jnp.sum(shaped * shaped, axis=-1, keepdims=True)) + 1e-06)

def to_blocks(rows_in, per_block):
    shaped = rows_in.reshape(rows_in.shape[0] // per_block, per_block, rows_in.shape[1], rows_in.shape[2])
    return shaped.transpose(0, 2, 1, 3)

def step_scalars(write_rate, log_gate, keep_mask, heads):
    filler = jnp.zeros((log_gate.shape[0], NH - 1, heads), jnp.float32)
    step_log = jnp.concatenate([log_gate[:, None, :], filler], axis=1).reshape(-1, heads)
    keep_steps = jnp.repeat(keep_mask.astype(jnp.float32), BLOCK, axis=1).reshape(-1)
    rates = write_rate * keep_steps[:, None]
    rate_blocks = rates.reshape(-1, SPAN, heads).transpose(0, 2, 1)
    log_blocks = step_log.reshape(-1, SPAN, heads).transpose(0, 2, 1)
    return (rate_blocks, log_blocks)

def unit_lower_inverse(lower_part, steps_here):
    negated = -lower_part
    inverse = jnp.eye(steps_here, dtype=jnp.float32) + negated
    power = negated
    reach = 2
    while reach < steps_here:
        power = jnp.einsum('...ij,...jk->...ik', power, power, precision=HIGHEST)
        inverse = inverse + jnp.einsum('...ij,...jk->...ik', inverse, power, precision=HIGHEST)
        reach = reach * 2
    return inverse

def span_terms(query_block, key_block, value_block, rate_block, log_block):
    steps_here = key_block.shape[-2]
    head_size = key_block.shape[-1]
    readers = query_block.shape[-2]
    stride = steps_here // readers
    cumlog = jnp.cumsum(log_block, axis=-1)
    index_of_row = lax.broadcasted_iota(jnp.int32, (steps_here, steps_here), 0)
    col_index = lax.broadcasted_iota(jnp.int32, (steps_here, steps_here), 1)
    strictly_below = col_index < index_of_row
    spread = cumlog[..., :, None] - cumlog[..., None, :]
    key_gram = jnp.einsum('...id,...jd->...ij', key_block, key_block, precision=HIGHEST)
    lower_part = jnp.where(strictly_below, rate_block[..., :, None] * jnp.exp(jnp.where(strictly_below, spread, 0.0)) * key_gram, 0.0)
    inverse = unit_lower_inverse(lower_part, steps_here)
    targets = jnp.concatenate([(rate_block * jnp.exp(cumlog))[..., None] * key_block, rate_block[..., None] * value_block], axis=-1)
    solved = jnp.einsum('...ij,...jd->...id', inverse, targets, precision=HIGHEST)
    erase_rows = solved[..., :head_size]
    fresh_rows = solved[..., head_size:]
    final_log = cumlog[..., -1:]
    faded_keys = jnp.exp(final_log - cumlog)[..., None] * key_block
    read_log = cumlog[..., stride - 1::stride]
    read_step = lax.broadcasted_iota(jnp.int32, (readers, steps_here), 0) * stride + stride - 1
    read_col = lax.broadcasted_iota(jnp.int32, (readers, steps_here), 1)
    visible = read_col <= read_step
    read_spread = read_log[..., :, None] - cumlog[..., None, :]
    scores = jnp.einsum('...td,...jd->...tj', query_block, key_block, precision=HIGHEST)
    inner = jnp.where(visible, jnp.exp(jnp.where(visible, read_spread, 0.0)) * scores, 0.0)
    return (erase_rows, fresh_rows, faded_keys, inner, jnp.exp(read_log), jnp.exp(final_log[..., 0]))

def span_read(state, pieces):
    erase_rows, fresh_rows, faded_keys, inner, read_scale, fade, query_block = pieces
    pseudo = fresh_rows - jnp.einsum('hcd,hde->hce', erase_rows, state, precision=HIGHEST)
    carried = read_scale[..., None] * jnp.einsum('htd,hde->hte', query_block, state, precision=HIGHEST)
    output = carried + jnp.einsum('htc,hce->hte', inner, pseudo, precision=HIGHEST)
    state = fade[:, None, None] * state + jnp.einsum('hcd,hce->hde', faded_keys, pseudo, precision=HIGHEST)
    return (state, output)

def reference(query_rows, key_rows, value_rows, write_rate, log_gate, keep_mask, query_kernel, key_kernel, value_kernel):
    heads = write_rate.shape[1]
    model_width = query_rows.shape[1]
    empty_rim = jnp.zeros((3, model_width), jnp.float32)
    query_unit = unit_heads(conv_silu(empty_rim, query_rows, query_kernel), heads)
    key_unit = unit_heads(conv_silu(empty_rim, key_rows, key_kernel), heads)
    value_feat = conv_silu(empty_rim, value_rows, value_kernel).reshape(value_rows.shape[0], heads, -1)
    rate_blocks, log_blocks = step_scalars(write_rate, log_gate, keep_mask, heads)
    query_blocks = to_blocks(query_unit, SPAN // NH)
    key_blocks = to_blocks(key_unit, SPAN)
    value_blocks = to_blocks(value_feat, SPAN)

    def advance(state, pieces):
        query_block, key_block, value_block, rate_block, log_block = pieces
        terms = span_terms(query_block, key_block, value_block, rate_block, log_block)
        return span_read(state, terms + (query_block,))
    initial = jnp.zeros((heads, DK, DK), jnp.float32)
    _, outputs = lax.scan(advance, initial, (query_blocks, key_blocks, value_blocks, rate_blocks, log_blocks))
    return outputs.transpose(0, 2, 1, 3).reshape(-1, heads * DK).astype(jnp.bfloat16)
```

```python
import functools

import jax
import jax.numpy as jnp
from jax import lax
from jax.experimental import pallas as pl
from jax.experimental.pallas import tpu as pltpu
from jax.sharding import PartitionSpec as P

NH = 2
BLOCK = 16
SPAN = 64
DK = 128
CHUNK = 128
HALF = 64
PLANE = 4
HB = 2
VMEM = 56 << 20

F32 = jnp.float32
BF16 = jnp.bfloat16
NN = (((1,), (0,)), ((), ()))
NT = (((1,), (1,)), ((), ()))


def split(x):
    high = x.astype(BF16)
    low = (x - high.astype(F32)).astype(BF16)
    return high, low


def mm(a, b, dims=NN):
    return lax.dot_general(a, b, dims, preferred_element_type=F32)


def mm3(a, b):
    ah, al = a
    bh, bl = b
    return mm(jnp.concatenate([ah, al], axis=1), jnp.concatenate([bh, bh], axis=0)) + mm(ah, bl)


def mm3_nt(a, b):
    ah, al = a
    bh, bl = b
    return mm(jnp.concatenate([ah, al], axis=1), jnp.concatenate([bh, bh], axis=1), NT) + mm(ah, bl, NT)


def lhs_of(x):
    high, low = x
    return jnp.concatenate([high, low], axis=1)


def rhs_of(x):
    high, low = x
    return jnp.concatenate([high, low, high, low], axis=0)


def silu(v):
    return v / (1.0 + jnp.exp(-v))


def conv(scratch, rows_ref, tail, kernel_ref):
    count = rows_ref.shape[0]
    scratch[5:8, :] = tail
    scratch[8 : 8 + count, :] = rows_ref[...].astype(F32)
    total = kernel_ref[0:1, :] * scratch[5 : 5 + count, :]
    for tap in range(1, 4):
        total = total + kernel_ref[tap : tap + 1, :] * scratch[5 + tap : 5 + tap + count, :]
    return silu(total)


def unit(x):
    return x * lax.rsqrt(jnp.sum(x * x, axis=-1, keepdims=True) + 1e-06)


def iota(shape, dim):
    return lax.broadcasted_iota(jnp.int32, shape, dim)


def prep_kernel(rate_ref, log_ref, mask_ref, rate_out, cum_out, dup_out, row_out, read_out):
    heads, steps = rate_ref.shape
    tokens = log_ref.shape[1]
    group = heads // PLANE
    subs, blocks = mask_ref.shape
    row_of = (iota((steps, blocks), 0) // SPAN == iota((steps, blocks), 1)).astype(F32)
    picked = mm(row_of, mask_ref[...].astype(F32), NT)
    sub_of = ((iota((steps, subs), 0) % SPAN) // BLOCK == iota((steps, subs), 1)).astype(F32)
    keep = jnp.sum(picked * sub_of, axis=1, keepdims=True)
    rates = rate_ref[...].T * keep
    turned = log_ref[...]
    logs = turned.T
    window = CHUNK // NH

    def upto(token, last):
        return ((token // window == last // window) & (token <= last)).astype(F32)

    high = lax.Precision.HIGHEST
    cum = jnp.dot(
        upto(iota((steps, tokens), 1), iota((steps, tokens), 0) // NH), logs, precision=high, preferred_element_type=F32
    )
    read = jnp.dot(
        upto(iota((tokens, tokens), 1), iota((tokens, tokens), 0)), logs, precision=high, preferred_element_type=F32
    )
    wide = (steps // HALF) * CHUNK
    lane = iota((tokens, wide), 1)
    dup = jnp.dot(
        turned,
        upto(iota((tokens, wide), 0), ((lane // CHUNK) * HALF + lane % HALF) // NH),
        precision=high,
        preferred_element_type=F32,
    )
    row = jnp.dot(
        turned,
        upto(iota((tokens, steps), 0), iota((tokens, steps), 1) // NH),
        precision=high,
        preferred_element_type=F32,
    )
    for g in range(PLANE):
        rate_out[g] = rates[:, g * group : (g + 1) * group]
        cum_out[g] = cum[:, g * group : (g + 1) * group]
        read_out[g] = read[:, g * group : (g + 1) * group]
    for b in range(steps // HALF):
        dup_out[:, b, :] = dup[:, b * CHUNK : (b + 1) * CHUNK]
    for b in range(steps // CHUNK):
        row_out[:, b, :] = row[:, b * CHUNK : (b + 1) * CHUNK]


def last_rows_kernel(query_ref, key_ref, value_ref, out_ref):
    for i, ref in enumerate((query_ref, key_ref, value_ref)):
        out_ref[3 * i : 3 * i + 3, :] = ref[...].astype(F32)[13:16].astype(BF16)


def last_rows(*arrays):
    width = arrays[0].shape[1]
    return pl.pallas_call(
        last_rows_kernel,
        grid=(1,),
        in_specs=[pl.BlockSpec((16, width), functools.partial(lambda at, i: (at, 0), x.shape[0] // 16 - 1)) for x in arrays],
        out_specs=pl.BlockSpec((9, width), lambda i: (0, 0)),
        out_shape=jax.ShapeDtypeStruct((9, width), BF16),
        name="last_rows",
    )(*arrays)


def prep(write_rate, log_gate, keep_mask):
    steps, heads = write_rate.shape
    tokens = log_gate.shape[0]
    group = heads // PLANE
    return pl.pallas_call(
        prep_kernel,
        out_shape=(
            jax.ShapeDtypeStruct((PLANE, steps, group), F32),
            jax.ShapeDtypeStruct((PLANE, steps, group), F32),
            jax.ShapeDtypeStruct((heads, steps // HALF, CHUNK), F32),
            jax.ShapeDtypeStruct((heads, steps // CHUNK, CHUNK), F32),
            jax.ShapeDtypeStruct((PLANE, tokens, group), F32),
        ),
        compiler_params=pltpu.CompilerParams(vmem_limit_bytes=40 << 20),
        name="prep",
    )(write_rate.T, log_gate.T, keep_mask.T)


def block_inverses(lowers):
    row = iota((HALF, CHUNK), 0)
    col = iota((HALF, CHUNK), 1) % HALF
    eye = (row == col).astype(F32)
    near = row // BLOCK == col // BLOCK
    inner = [jnp.where(near, -x, 0.0) for x in lowers]
    outer = [split(jnp.where(near, 0.0, x)) for x in lowers]
    first = [split(x) for x in inner]
    second = [mm(lhs_of(x), rhs_of(x)) for x in first]
    s2 = [split(x) for x in second]
    fourth = [mm(lhs_of(x), rhs_of(x)) for x in s2]
    a = [eye + x for x in inner]
    a = [x + mm(lhs_of(split(x)), rhs_of(y)) for x, y in zip(a, s2)]
    s4 = [split(x) for x in fourth]
    eighth = [mm(lhs_of(x), rhs_of(x)) for x in s4]
    a = [x + mm(lhs_of(split(x)), rhs_of(y)) for x, y in zip(a, s4)]
    s8 = [split(x) for x in eighth]
    a = [x + mm(lhs_of(split(x)), rhs_of(y)) for x, y in zip(a, s8)]
    sa = [split(x) for x in a]
    m = [mm(lhs_of(x), rhs_of(y)) for x, y in zip(sa, outer)]
    sm = [split(x) for x in m]
    m2 = [mm(lhs_of(x), rhs_of(x)) for x in sm]
    t = [x - mm(lhs_of(y), rhs_of(z)) for x, y, z in zip(a, sm, sa)]
    return [x + mm(lhs_of(split(y)), rhs_of(split(x))) for x, y in zip(t, m2)]


def maps_kernel(
    group_ref,
    key_ref,
    value_ref,
    tail_ref,
    key_kernel_ref,
    value_kernel_ref,
    rate_ref,
    cum_ref,
    dup_ref,
    row_ref,
    map_out,
    ph_out,
    pl_out,
    scratch,
):
    steps = key_ref.shape[0]
    chunks = steps // CHUNK
    at = pl.program_id(0)
    keys = conv(scratch, key_ref, tail_ref[3:6, :].astype(F32), key_kernel_ref)
    keys = jnp.concatenate([unit(keys[:, h * DK : (h + 1) * DK]) for h in range(HB)], axis=1)
    values = conv(scratch, value_ref, tail_ref[6:9, :].astype(F32), value_kernel_ref)
    kh, kl = split(keys)
    group = rate_ref.shape[2]
    rates, cums = rate_ref[0], cum_ref[0]

    def column(x, h):
        out = x[:, h : h + 1]
        for turn in range(1, group // HB):
            out = jnp.where(at == turn, x[:, turn * HB + h : turn * HB + h + 1], out)
        return out

    row = iota((HALF, CHUNK), 0)
    col = iota((HALF, CHUNK), 1) % HALF
    below = col < row
    lowers, crosses, sides, faded, ends = [], [], [], [], []
    for h in range(HB):
        lanes = slice(h * DK, (h + 1) * DK)
        k_h, v_h = keys[:, lanes], values[:, lanes]
        rate_h, cum_h = column(rates, h), column(cums, h)
        grown = rate_h * jnp.exp(cum_h)
        side = jnp.concatenate([grown * k_h, rate_h * v_h], axis=1)
        for c in range(chunks):
            for b in range(2):
                at_row = c * CHUNK + b * HALF
                rows = slice(at_row, at_row + HALF)
                mine = (kh[rows, lanes], kl[rows, lanes])
                sides.append(split(side[rows]))
                spread = cum_h[rows] - dup_ref[h, 2 * c + b : 2 * c + b + 1, :]
                twice = tuple(jnp.concatenate([x, x], axis=0) for x in mine)
                gram = mm3_nt(mine, twice)
                lowers.append(
                    jnp.where(below, rate_h[rows] * jnp.exp(jnp.where(below, spread, 0.0)) * gram, 0.0)
                )
                if b == 1:
                    before = slice(at_row - HALF, at_row)
                    earlier = (kh[before, lanes], kl[before, lanes])
                    twice = tuple(jnp.concatenate([x, x], axis=0) for x in earlier)
                    spread = cum_h[rows] - dup_ref[h, 2 * c : 2 * c + 1, :]
                    crosses.append(rate_h[rows] * jnp.exp(spread) * mm3_nt(mine, twice))
            row_c = row_ref[h, c : c + 1, :]
            end = row_c[:, CHUNK - 1 : CHUNK]
            turned = k_h[c * CHUNK : (c + 1) * CHUNK].T
            faded.append(split(turned * jnp.exp(end - row_c)))
            ends.append(jnp.exp(end))
    inverses = [split(x) for x in block_inverses(lowers)]
    solved = []
    for i, cross in enumerate(crosses):
        top, low = inverses[2 * i], inverses[2 * i + 1]
        upper = mm(lhs_of(top), rhs_of(sides[2 * i]))
        down = mm(lhs_of(split(cross)), rhs_of(split(upper)))
        lower = mm(lhs_of(low), rhs_of(sides[2 * i + 1])) - mm(lhs_of(low), rhs_of(split(down)))
        solved.append(jnp.concatenate([upper, lower], axis=0))
    state = [None] * HB
    for c in range(chunks):
        for h in range(HB):
            i = h * chunks + c
            erase, fresh = solved[i][:, :DK], solved[i][:, DK:]
            if c == 0:
                pseudo = jnp.concatenate([-erase, fresh], axis=1)
                eye = (iota((DK, 2 * DK), 0) == iota((DK, 2 * DK), 1)).astype(F32)
                carried = ends[i] * eye
            else:
                pieces = split(state[h])
                taken = mm3(split(erase), pieces)
                pseudo = jnp.concatenate([-taken[:, :DK], fresh - taken[:, DK:]], axis=1)
                carried = ends[i] * state[h]
            pieces = split(pseudo)
            at_p = slice(c * CHUNK, (c + 1) * CHUNK)
            ph_out[h, at_p, :], pl_out[h, at_p, :] = pieces
            state[h] = carried + mm3(faded[i], pieces)
    for h in range(HB):
        map_out[h] = state[h]


def group_maps(which, key_rows, value_rows, tails, key_kernel, value_kernel, scalars):
    rate_cols, cum_cols, dup_rows, chunk_rows, _ = scalars
    steps, width = key_rows.shape
    heads = width // DK
    group = heads // PLANE
    turns = group // HB
    lanes = HB * DK
    chunks = steps // CHUNK

    def wide(i, g):
        return (0, g[0] * turns + i)

    def per_head(i, g):
        return (g[0] * turns + i, 0, 0)

    def local(i, g):
        return (i, 0, 0)

    return pl.pallas_call(
        maps_kernel,
        grid_spec=pltpu.PrefetchScalarGridSpec(
            num_scalar_prefetch=1,
            grid=(turns,),
            in_specs=[
                pl.BlockSpec((steps, lanes), wide),
                pl.BlockSpec((steps, lanes), wide),
                pl.BlockSpec((tails.shape[0], lanes), wide),
                pl.BlockSpec((4, lanes), wide),
                pl.BlockSpec((4, lanes), wide),
                pl.BlockSpec((1, steps, group), lambda i, g: (g[0], 0, 0)),
                pl.BlockSpec((1, steps, group), lambda i, g: (g[0], 0, 0)),
                pl.BlockSpec((HB, steps // HALF, CHUNK), per_head),
                pl.BlockSpec((HB, chunks, CHUNK), per_head),
            ],
            out_specs=[
                pl.BlockSpec((HB, DK, 2 * DK), local),
                pl.BlockSpec((HB, steps, 2 * DK), local),
                pl.BlockSpec((HB, steps, 2 * DK), local),
            ],
            scratch_shapes=[pltpu.VMEM((steps + 8, lanes), F32)],
        ),
        out_shape=(
            jax.ShapeDtypeStruct((group, DK, 2 * DK), F32),
            jax.ShapeDtypeStruct((group, steps, 2 * DK), BF16),
            jax.ShapeDtypeStruct((group, steps, 2 * DK), BF16),
        ),
        compiler_params=pltpu.CompilerParams(vmem_limit_bytes=VMEM),
        name="maps",
    )(which, key_rows, value_rows, tails, key_kernel, value_kernel, rate_cols, cum_cols, dup_rows, chunk_rows)


def reads_kernel(
    group_ref,
    query_ref,
    tail_ref,
    query_kernel_ref,
    key_ref,
    key_kernel_ref,
    read_ref,
    row_ref,
    ph_ref,
    pl_ref,
    qh_out,
    ql_out,
    own_out,
    scratch,
):
    tokens = query_ref.shape[0]
    window = CHUNK // NH
    chunks = tokens // window
    at = pl.program_id(0)
    queries = conv(scratch, query_ref, tail_ref[0:3, :].astype(F32), query_kernel_ref)
    queries = jnp.concatenate([unit(queries[:, h * DK : (h + 1) * DK]) for h in range(HB)], axis=1)
    keys = conv(scratch, key_ref, tail_ref[3:6, :].astype(F32), key_kernel_ref)
    group = read_ref.shape[2]
    reads = read_ref[0]
    visible = iota((window, CHUNK), 1) <= NH * iota((window, CHUNK), 0) + NH - 1
    for h in range(HB):
        lanes = slice(h * DK, (h + 1) * DK)
        q_h = queries[:, lanes]
        k_h = unit(keys[:, lanes])
        kh, kl = split(k_h)
        read_h = reads[:, h : h + 1]
        for turn in range(1, group // HB):
            read_h = jnp.where(at == turn, reads[:, turn * HB + h : turn * HB + h + 1], read_h)
        lifted = jnp.exp(read_h) * q_h
        for c in range(chunks):
            rows = slice(c * window, (c + 1) * window)
            steps = slice(c * CHUNK, (c + 1) * CHUNK)
            scores = mm3_nt(split(q_h[rows]), (kh[steps], kl[steps]))
            spread = read_h[rows] - row_ref[h, c : c + 1, :]
            inner = jnp.where(visible, jnp.exp(jnp.where(visible, spread, 0.0)) * scores, 0.0)
            pieces = (ph_ref[h, steps, :], pl_ref[h, steps, :])
            got = mm3(split(inner), pieces)
            if c == 0:
                eff, own = got[:, :DK] + lifted[rows], got[:, DK:]
            else:
                got = got + mm3(split(lifted[rows]), split(state))
                eff, own = got[:, :DK], got[:, DK:]
            if c < chunks - 1:
                row_c = row_ref[h, c : c + 1, :]
                end = row_c[:, CHUNK - 1 : CHUNK]
                faded = split(k_h[steps].T * jnp.exp(end - row_c))
                start = (iota((DK, 2 * DK), 0) == iota((DK, 2 * DK), 1)).astype(F32) if c == 0 else state
                state = jnp.exp(end) * start + mm3(faded, pieces)
            qh_out[rows, lanes], ql_out[rows, lanes] = split(eff)
            own_out[rows, lanes] = own


def group_reads(which, query_rows, key_rows, tails, query_kernel, key_kernel, scalars, kept):
    _, _, _, chunk_rows, read_cols = scalars
    high, low = kept
    tokens, width = query_rows.shape
    steps = tokens * NH
    heads = width // DK
    group = heads // PLANE
    turns = group // HB
    lanes = HB * DK
    chunks = steps // CHUNK

    def wide(i, g):
        return (0, g[0] * turns + i)

    def here(i, g):
        return (0, i)

    def local(i, g):
        return (i, 0, 0)

    return pl.pallas_call(
        reads_kernel,
        grid_spec=pltpu.PrefetchScalarGridSpec(
            num_scalar_prefetch=1,
            grid=(turns,),
            in_specs=[
                pl.BlockSpec((tokens, lanes), wide),
                pl.BlockSpec((tails.shape[0], lanes), wide),
                pl.BlockSpec((4, lanes), wide),
                pl.BlockSpec((steps, lanes), wide),
                pl.BlockSpec((4, lanes), wide),
                pl.BlockSpec((1, tokens, group), lambda i, g: (g[0], 0, 0)),
                pl.BlockSpec((HB, chunks, CHUNK), lambda i, g: (g[0] * turns + i, 0, 0)),
                pl.BlockSpec((HB, steps, 2 * DK), local),
                pl.BlockSpec((HB, steps, 2 * DK), local),
            ],
            out_specs=[
                pl.BlockSpec((tokens, lanes), here),
                pl.BlockSpec((tokens, lanes), here),
                pl.BlockSpec((tokens, lanes), here),
            ],
            scratch_shapes=[pltpu.VMEM((steps + 8, lanes), F32)],
        ),
        out_shape=(
            jax.ShapeDtypeStruct((tokens, group * DK), BF16),
            jax.ShapeDtypeStruct((tokens, group * DK), BF16),
            jax.ShapeDtypeStruct((tokens, group * DK), F32),
        ),
        compiler_params=pltpu.CompilerParams(vmem_limit_bytes=VMEM),
        name="reads",
    )(which, query_rows, tails, query_kernel, key_rows, key_kernel, read_cols, chunk_rows, high, low)


def compose_kernel(flag_ref, mine_ref, other_ref, out_ref):
    mine_first = flag_ref[0] == 0
    for h in range(mine_ref.shape[0]):
        mine, other = mine_ref[h], other_ref[h]
        early = jnp.where(mine_first, mine, other)
        late = jnp.where(mine_first, other, mine)
        both = mm3(split(late[:, :DK]), split(early))
        out_ref[h, :, :DK] = both[:, :DK]
        out_ref[h, :, DK:] = both[:, DK:] + late[:, DK:]


def composed(flag, mine, other):
    return pl.pallas_call(
        compose_kernel,
        in_specs=[pl.BlockSpec(memory_space=pltpu.SMEM)] + [pl.BlockSpec(memory_space=pltpu.VMEM)] * 2,
        out_specs=pl.BlockSpec(memory_space=pltpu.VMEM),
        out_shape=jax.ShapeDtypeStruct(mine.shape, F32),
        name="compose",
    )(flag, mine, other)


def apply_kernel(map_ref, state_ref, out_ref):
    for h in range(map_ref.shape[0]):
        out_ref[h] = mm3(split(map_ref[h, :, :DK]), split(state_ref[h])) + map_ref[h, :, DK:]


def applied(maps, state):
    return pl.pallas_call(
        apply_kernel,
        in_specs=[pl.BlockSpec(memory_space=pltpu.VMEM)] * 2,
        out_specs=pl.BlockSpec(memory_space=pltpu.VMEM),
        out_shape=jax.ShapeDtypeStruct(state.shape, F32),
        name="apply",
    )(maps, state)


def branch_kernel(flag_ref, mine_ref, other_ref, entry_ref, keep_out, send_out):
    first = flag_ref[0] == 0
    for h in range(mine_ref.shape[0]):
        early = jnp.where(first, mine_ref[h], other_ref[h])
        entry = entry_ref[h]
        later = mm3(split(early[:, :DK]), split(entry)) + early[:, DK:]
        keep_out[h] = jnp.where(first, entry, later)
        send_out[h] = jnp.where(first, later, entry)


def branched(flag, mine, other, entry):
    return pl.pallas_call(
        branch_kernel,
        in_specs=[pl.BlockSpec(memory_space=pltpu.SMEM)] + [pl.BlockSpec(memory_space=pltpu.VMEM)] * 3,
        out_specs=[pl.BlockSpec(memory_space=pltpu.VMEM)] * 2,
        out_shape=(jax.ShapeDtypeStruct(entry.shape, F32),) * 2,
        name="branch",
    )(flag, mine, other, entry)


def finish_kernel(group_ref, *refs):
    count = (len(refs) - 1) // 4
    out_ref = refs[-1]
    which = pl.program_id(0)
    for turn in range(count):
        qh_ref, ql_ref, own_ref, entry_ref = refs[4 * turn : 4 * turn + 4]

        @pl.when(which == turn)
        def _():
            for h in range(entry_ref.shape[0]):
                lanes = slice(h * DK, (h + 1) * DK)
                got = mm3((qh_ref[:, lanes], ql_ref[:, lanes]), split(entry_ref[h]))
                out_ref[:, lanes] = (own_ref[:, lanes] + got).astype(BF16)


def finished(order, reads, entries):
    tokens, lanes = reads[0][0].shape
    operands, specs = [], []
    for (qh, ql, own), entry in zip(reads, entries):
        operands += [qh, ql, own, entry]
        specs += [pl.BlockSpec((tokens, lanes), lambda i, g: (0, 0))] * 3
        specs += [pl.BlockSpec(entry.shape, lambda i, g: (0, 0, 0))]
    return pl.pallas_call(
        finish_kernel,
        grid_spec=pltpu.PrefetchScalarGridSpec(
            num_scalar_prefetch=1,
            grid=(len(reads),),
            in_specs=specs,
            out_specs=pl.BlockSpec((tokens, lanes), lambda i, g: (0, g[i])),
        ),
        out_shape=jax.ShapeDtypeStruct((tokens, lanes * len(reads)), BF16),
        compiler_params=pltpu.CompilerParams(vmem_limit_bytes=VMEM),
        name="finish",
    )(order, *operands)


def local(
    count,
    query_rows,
    key_rows,
    value_rows,
    write_rate,
    log_gate,
    keep_mask,
    query_kernel,
    key_kernel,
    value_kernel,
):
    tails = lax.ppermute(last_rows(query_rows, key_rows, value_rows), "seq", [(s, s + 1) for s in range(count - 1)])
    scalars = prep(write_rate, log_gate, keep_mask)
    place = lax.axis_index("seq") % PLANE
    core = (place % 2)[None]
    chip = (place // 2)[None]
    pair = [(s, s ^ 1) for s in range(count)]
    across = [(s, s ^ 2) for s in range(count)]
    onward = [(s, s + PLANE) for s in range(count - PLANE)]
    groups = [(place ^ x)[None] for x in (3, 1, 2, 0)]
    made = [group_maps(g, key_rows, value_rows, tails, key_kernel, value_kernel, scalars) for g in groups]
    maps = [m[0] for m in made]
    from_pair = [lax.ppermute(m, "seq", pair) for m in maps[:2]]
    chip_maps = [composed(core, mine, other) for mine, other in zip(maps[2:], from_pair)]
    from_chip = lax.ppermute(chip_maps[0], "seq", across)
    plane_map = composed(chip, chip_maps[1], from_chip)
    plane_map, kept = lax.optimization_barrier((plane_map, [m[1:] for m in made]))

    def read(i):
        return group_reads(
            groups[i], query_rows, key_rows, tails, query_kernel, key_kernel, scalars, kept[i]
        )

    reads = []
    entry = lax.ppermute(plane_map[:, :, DK:], "seq", onward)
    for i in range(count // PLANE - 1):
        if i > 0:
            entry = lax.ppermute(applied(plane_map, entry), "seq", onward)
        if len(reads) < PLANE - 1:
            reads.append(read(i))
            entry, reads[-1] = lax.optimization_barrier((entry, reads[-1]))
    mine, send = branched(chip, chip_maps[1], from_chip, entry)
    theirs = lax.ppermute(send, "seq", across)
    own_entry, own_send = branched(core, maps[3], from_pair[1], mine)
    reads += [read(i) for i in range(len(reads), PLANE)]
    theirs, reads = lax.optimization_barrier((theirs, reads))
    next_entry, next_send = branched(core, maps[2], from_pair[0], theirs)
    far_own = lax.ppermute(own_send, "seq", pair)
    far_next = lax.ppermute(next_send, "seq", pair)
    return finished(jnp.concatenate(groups), reads, [far_next, far_own, next_entry, own_entry])


def solution(mesh):
    rows = P(("groups", "seq"), None)
    return jax.shard_map(
        functools.partial(local, mesh.shape["seq"]),
        mesh=mesh,
        in_specs=(rows, rows, rows, rows, rows, rows, P(), P(), P()),
        out_specs=rows,
        check_vma=False,
    )
```

```python
import functools

import jax
import jax.numpy as jnp
from jax import lax
from jax.experimental import pallas as pl
from jax.experimental.pallas import tpu as pltpu
from jax.sharding import PartitionSpec as P

NH = 2
BLOCK = 16
SPAN = 64
DK = 128
CHUNK = 128
HALF = 64
PLANE = 4
HB = 2
VMEM = 56 << 20

F32 = jnp.float32
BF16 = jnp.bfloat16
NN = (((1,), (0,)), ((), ()))
NT = (((1,), (1,)), ((), ()))


def split(x):
    high = x.astype(BF16)
    low = (x - high.astype(F32)).astype(BF16)
    return high, low


def mm(a, b, dims=NN):
    return lax.dot_general(a, b, dims, preferred_element_type=F32)


def mm3(a, b):
    ah, al = a
    bh, bl = b
    return mm(jnp.concatenate([ah, al], axis=1), jnp.concatenate([bh, bh], axis=0)) + mm(ah, bl)


def mm3_nt(a, b):
    ah, al = a
    bh, bl = b
    return mm(jnp.concatenate([ah, al], axis=1), jnp.concatenate([bh, bh], axis=1), NT) + mm(ah, bl, NT)


def halves(x):
    left = iota(x.shape, 1) < HALF
    zero = jnp.zeros_like(x)
    return jnp.concatenate([jnp.where(left, x, zero), jnp.where(left, zero, x)], axis=0)


def pair_product(x, y):
    return mm3(x, (halves(y[0]), halves(y[1])))


def silu(v):
    return v / (1.0 + jnp.exp(-v))


def load_rows(scratch, rows_ref, tail):
    before = jnp.concatenate([jnp.zeros((13, tail.shape[1]), F32), tail.astype(F32)], axis=0)
    scratch[0:16, :] = before.astype(BF16)
    scratch[16 : 16 + rows_ref.shape[0], :] = rows_ref[...]


def shifter():
    shape = (3 * HALF, HALF + 16)
    row, col = iota(shape, 0), iota(shape, 1)
    return (col == 15 + row % HALF - row // HALF).astype(F32).astype(BF16)


def conv(shifts, scratch, kernel_ref, start, count):
    parts = []
    for at in range(start, start + count, HALF):
        moved = mm(shifts, scratch[at : at + HALF + 16, :])
        total = kernel_ref[3:4, :] * scratch[at + 16 : at + 16 + HALF, :].astype(F32)
        for back in range(1, 4):
            total = total + kernel_ref[3 - back : 4 - back, :] * moved[(back - 1) * HALF : back * HALF]
        parts.append(silu(total))
    return jnp.concatenate(parts, axis=0)


def unit(x):
    return x * lax.rsqrt(jnp.sum(x * x, axis=-1, keepdims=True) + 1e-06)


def iota(shape, dim):
    return lax.broadcasted_iota(jnp.int32, shape, dim)


def prep_kernel(rate_ref, log_ref, mask_ref, rate_out, cum_out, row_out, read_out):
    heads, steps = rate_ref.shape
    tokens = log_ref.shape[1]
    group = heads // PLANE
    subs, blocks = mask_ref.shape
    row_of = (iota((steps, blocks), 0) // SPAN == iota((steps, blocks), 1)).astype(F32)
    picked = mm(row_of, mask_ref[...].astype(F32), NT)
    sub_of = ((iota((steps, subs), 0) % SPAN) // BLOCK == iota((steps, subs), 1)).astype(F32)
    keep = jnp.sum(picked * sub_of, axis=1, keepdims=True)
    rates = rate_ref[...].T * keep
    turned = log_ref[...]
    logs = turned.T
    window = CHUNK // NH

    def upto(token, last):
        return ((token // window == last // window) & (token <= last)).astype(F32)

    high = lax.Precision.HIGHEST
    cum = jnp.dot(
        upto(iota((steps, tokens), 1), iota((steps, tokens), 0) // NH), logs, precision=high, preferred_element_type=F32
    )
    read = jnp.dot(
        upto(iota((tokens, tokens), 1), iota((tokens, tokens), 0)), logs, precision=high, preferred_element_type=F32
    )
    row = jnp.dot(
        turned,
        upto(iota((tokens, steps), 0), iota((tokens, steps), 1) // NH),
        precision=high,
        preferred_element_type=F32,
    )
    for g in range(PLANE):
        rate_out[g] = rates[:, g * group : (g + 1) * group]
        cum_out[g] = cum[:, g * group : (g + 1) * group]
        read_out[g] = read[:, g * group : (g + 1) * group]
    for b in range(steps // CHUNK):
        row_out[:, b, :] = row[:, b * CHUNK : (b + 1) * CHUNK]


def last_rows_kernel(query_ref, key_ref, value_ref, out_ref):
    for i, ref in enumerate((query_ref, key_ref, value_ref)):
        out_ref[3 * i : 3 * i + 3, :] = ref[...].astype(F32)[13:16].astype(BF16)


def last_rows(*arrays):
    width = arrays[0].shape[1]
    return pl.pallas_call(
        last_rows_kernel,
        grid=(1,),
        in_specs=[pl.BlockSpec((16, width), functools.partial(lambda at, i: (at, 0), x.shape[0] // 16 - 1)) for x in arrays],
        out_specs=pl.BlockSpec((9, width), lambda i: (0, 0)),
        out_shape=jax.ShapeDtypeStruct((9, width), BF16),
        name="last_rows",
    )(*arrays)


def prep(write_rate, log_gate, keep_mask):
    steps, heads = write_rate.shape
    tokens = log_gate.shape[0]
    group = heads // PLANE
    return pl.pallas_call(
        prep_kernel,
        out_shape=(
            jax.ShapeDtypeStruct((PLANE, steps, group), F32),
            jax.ShapeDtypeStruct((PLANE, steps, group), F32),
            jax.ShapeDtypeStruct((heads, steps // CHUNK, CHUNK), F32),
            jax.ShapeDtypeStruct((PLANE, tokens, group), F32),
        ),
        compiler_params=pltpu.CompilerParams(vmem_limit_bytes=VMEM),
        name="prep",
    )(write_rate.T, log_gate.T, keep_mask.T)


def block_inverses(lowers, fill):
    row = iota((HALF, CHUNK), 0)
    col = iota((HALF, CHUNK), 1) % HALF
    eye = (row == col).astype(F32)
    near = row // BLOCK == col // BLOCK
    inner = [jnp.where(near, -x, 0.0) for x in lowers]
    outer = [split(jnp.where(near, 0.0, x)) for x in lowers]
    power = [split(x) for x in inner]
    a = [eye + x for x in inner]
    for _ in range(3):
        fill()
        power = [split(pair_product(x, x)) for x in power]
        fill()
        a = [x + pair_product(split(x), y) for x, y in zip(a, power)]
    sa = [split(x) for x in a]
    fill()
    m = [split(pair_product(x, y)) for x, y in zip(sa, outer)]
    fill()
    m2 = [split(pair_product(x, x)) for x in m]
    t = [x - pair_product(y, z) for x, y, z in zip(a, m, sa)]
    return [x + pair_product(y, split(x)) for x, y in zip(t, m2)]


def maps_kernel(
    group_ref,
    key_ref,
    value_ref,
    tail_ref,
    key_kernel_ref,
    value_kernel_ref,
    rate_ref,
    cum_ref,
    row_ref,
    map_out,
    wh_out,
    wl_out,
    mh_out,
    ml_out,
    scratch,
    value_scratch,
):
    steps = key_ref.shape[0]
    chunks = steps // CHUNK
    at = pl.program_id(0)
    load_rows(scratch, key_ref, tail_ref[3:6, :])
    load_rows(value_scratch, value_ref, tail_ref[6:9, :])
    shifts = shifter()
    keys = conv(shifts, scratch, key_kernel_ref, 0, steps)
    keys = jnp.concatenate([unit(keys[:, h * DK : (h + 1) * DK]) for h in range(HB)], axis=1)
    kh, kl = split(keys)
    group = rate_ref.shape[2]
    rates, cums = rate_ref[0], cum_ref[0]

    def column(x, h):
        out = x[:, h : h + 1]
        for turn in range(1, group // HB):
            out = jnp.where(at == turn, x[:, turn * HB + h : turn * HB + h + 1], out)
        return out

    below = iota((CHUNK, CHUNK), 1) < iota((CHUNK, CHUNK), 0)
    left = iota((HALF, CHUNK), 1) < HALF
    items = [(h, c) for h in range(HB) for c in range(chunks)]
    columns = [(column(rates, h), column(cums, h)) for h in range(HB)]
    lowers, crosses, sides, faded, ends = [], [], {}, {}, {}
    for h, c in items:
        lanes = slice(h * DK, (h + 1) * DK)
        rows = slice(c * CHUNK, (c + 1) * CHUNK)
        row_c = row_ref[h, c : c + 1, :]
        rate_c, cum_c = (x[rows] for x in columns[h])
        mine = (kh[rows, lanes], kl[rows, lanes])
        decay = jnp.exp(jnp.where(below, cum_c - row_c, 0.0))
        lower = jnp.where(below, rate_c * decay * mm3_nt(mine, mine), 0.0)
        lowers.append(jnp.where(left, lower[:HALF], lower[HALF:]))
        crosses.append(split(jnp.where(left, lower[HALF:], 0.0)))

    def side(c):
        rows = slice(c * CHUNK, (c + 1) * CHUNK)
        values = conv(shifts, value_scratch, value_kernel_ref, c * CHUNK, CHUNK)
        for h in range(HB):
            lanes = slice(h * DK, (h + 1) * DK)
            rate_c, cum_c = (x[rows] for x in columns[h])
            grown = rate_c * jnp.exp(cum_c) * keys[rows, lanes]
            sides[h, c] = split(jnp.concatenate([grown, rate_c * values[:, lanes]], axis=1))

    def fade(c):
        for h in range(HB):
            row_c = row_ref[h, c : c + 1, :]
            end = row_c[:, CHUNK - 1 : CHUNK]
            k_c = keys[c * CHUNK : (c + 1) * CHUNK, h * DK : (h + 1) * DK]
            faded[h, c] = split(k_c.T * jnp.exp(end - row_c))
            ends[h, c] = jnp.exp(end)

    todo = [functools.partial(f, c) for c in range(chunks) for f in (side, fade)]

    def fill():
        if todo:
            todo.pop(0)()

    eye = (iota((DK, DK), 0) == iota((DK, DK), 1)).astype(F32)
    inverses = block_inverses(lowers, fill)
    while todo:
        fill()
    pieces = [split(x) for x in inverses]
    under = [mm3(y, tuple(jnp.concatenate([z, z], axis=0) for z in x)) for x, y in zip(pieces, crosses)]
    under = [split(jnp.where(left, x, 0.0)) for x in under]
    under = [
        mm3(x, tuple(jnp.concatenate([jnp.zeros_like(z), z], axis=0) for z in y)) for x, y in zip(pieces, under)
    ]
    whole = [
        split(jnp.concatenate([jnp.where(left, x, 0.0), jnp.where(left, -y, x)], axis=0))
        for x, y in zip(inverses, under)
    ]
    solved = [split(mm3(x, sides[i])) for i, x in zip(items, whole)]
    for (h, c), x in zip(items, solved):
        at_w = slice(c * CHUNK, (c + 1) * CHUNK)
        wh_out[h, at_w, :], wl_out[h, at_w, :] = x
    made = [mm3(faded[i], x) for i, x in zip(items, solved)]
    made = [jnp.concatenate([ends[i] * eye - x[:, :DK], x[:, DK:]], axis=1) for i, x in zip(items, made)]

    def then(late, early):
        both = mm3(split(late[:, :DK]), early)
        return jnp.concatenate([both[:, :DK], both[:, DK:] + late[:, DK:]], axis=1)

    assert chunks == 4
    heads = range(HB)
    first, third = ([split(made[h * chunks + c]) for h in heads] for c in (0, 2))
    two = [split(then(made[h * chunks + 1], first[h])) for h in heads]
    last = [then(made[h * chunks + 3], third[h]) for h in heads]
    last = [then(last[h], two[h]) for h in heads]
    for h in heads:
        map_out[h] = last[h]
        for i, x in enumerate((first[h], two[h], third[h])):
            mh_out[h, i * DK : (i + 1) * DK, :], ml_out[h, i * DK : (i + 1) * DK, :] = x


def group_maps(which, key_rows, value_rows, tails, key_kernel, value_kernel, scalars):
    rate_cols, cum_cols, chunk_rows, _ = scalars
    steps, width = key_rows.shape
    heads = width // DK
    group = heads // PLANE
    turns = group // HB
    lanes = HB * DK
    chunks = steps // CHUNK

    def wide(i, g):
        return (0, g[0] * turns + i)

    def per_head(i, g):
        return (g[0] * turns + i, 0, 0)

    def local(i, g):
        return (i, 0, 0)

    return pl.pallas_call(
        maps_kernel,
        grid_spec=pltpu.PrefetchScalarGridSpec(
            num_scalar_prefetch=1,
            grid=(turns,),
            in_specs=[
                pl.BlockSpec((steps, lanes), wide),
                pl.BlockSpec((steps, lanes), wide),
                pl.BlockSpec((tails.shape[0], lanes), wide),
                pl.BlockSpec((4, lanes), wide),
                pl.BlockSpec((4, lanes), wide),
                pl.BlockSpec((1, steps, group), lambda i, g: (g[0], 0, 0)),
                pl.BlockSpec((1, steps, group), lambda i, g: (g[0], 0, 0)),
                pl.BlockSpec((HB, chunks, CHUNK), per_head),
            ],
            out_specs=[
                pl.BlockSpec((HB, DK, 2 * DK), local),
                pl.BlockSpec((HB, steps, 2 * DK), local),
                pl.BlockSpec((HB, steps, 2 * DK), local),
                pl.BlockSpec((HB, 3 * DK, 2 * DK), local),
                pl.BlockSpec((HB, 3 * DK, 2 * DK), local),
            ],
            scratch_shapes=[pltpu.VMEM((steps + 16, lanes), BF16)] * 2,
        ),
        out_shape=(
            jax.ShapeDtypeStruct((group, DK, 2 * DK), F32),
            jax.ShapeDtypeStruct((group, steps, 2 * DK), BF16),
            jax.ShapeDtypeStruct((group, steps, 2 * DK), BF16),
            jax.ShapeDtypeStruct((group, 3 * DK, 2 * DK), BF16),
            jax.ShapeDtypeStruct((group, 3 * DK, 2 * DK), BF16),
        ),
        compiler_params=pltpu.CompilerParams(vmem_limit_bytes=VMEM),
        name="maps",
    )(which, key_rows, value_rows, tails, key_kernel, value_kernel, rate_cols, cum_cols, chunk_rows)


def reads_kernel(
    group_ref,
    query_ref,
    tail_ref,
    query_kernel_ref,
    key_ref,
    key_kernel_ref,
    read_ref,
    row_ref,
    wh_ref,
    wl_ref,
    mh_ref,
    ml_ref,
    qh_out,
    ql_out,
    own_out,
    scratch,
    key_scratch,
):
    tokens = query_ref.shape[0]
    window = CHUNK // NH
    chunks = tokens // window
    at = pl.program_id(0)
    load_rows(scratch, query_ref, tail_ref[0:3, :])
    shifts = shifter()
    queries = conv(shifts, scratch, query_kernel_ref, 0, tokens)
    queries = jnp.concatenate([unit(queries[:, h * DK : (h + 1) * DK]) for h in range(HB)], axis=1)
    load_rows(key_scratch, key_ref, tail_ref[3:6, :])
    keys = conv(shifts, key_scratch, key_kernel_ref, 0, NH * tokens)
    group = read_ref.shape[2]
    reads = read_ref[0]
    visible = iota((window, CHUNK), 1) <= NH * iota((window, CHUNK), 0) + NH - 1
    items = [(h, c) for h in range(HB) for c in range(chunks)]
    pieces, columns, lifted = [], [], []
    for h in range(HB):
        lanes = slice(h * DK, (h + 1) * DK)
        read_h = reads[:, h : h + 1]
        for turn in range(1, group // HB):
            read_h = jnp.where(at == turn, reads[:, turn * HB + h : turn * HB + h + 1], read_h)
        columns.append(read_h)
        lifted.append(jnp.exp(read_h) * queries[:, lanes])
        pieces.append((split(queries[:, lanes]), split(unit(keys[:, lanes]))))

    def tokens_of(c):
        return slice(c * window, (c + 1) * window)

    def steps_of(c):
        return slice(c * CHUNK, (c + 1) * CHUNK)

    scores = [
        mm3_nt(tuple(x[tokens_of(c)] for x in pieces[h][0]), tuple(x[steps_of(c)] for x in pieces[h][1]))
        for h, c in items
    ]
    starts = {}
    for h in range(HB):
        kept = [(mh_ref[h, i * DK : (i + 1) * DK, :], ml_ref[h, i * DK : (i + 1) * DK, :]) for i in range(3)]
        first, two, third = kept
        three = mm3(tuple(x[:, :DK] for x in third), two)
        late = third[0][:, DK:].astype(F32) + third[1][:, DK:].astype(F32)
        three = split(jnp.concatenate([three[:, :DK], three[:, DK:] + late], axis=1))
        starts[h] = [None, first, two, three]
    inner = []
    for (h, c), x in zip(items, scores):
        spread = columns[h][tokens_of(c)] - row_ref[h, c : c + 1, :]
        inner.append(split(jnp.where(visible, jnp.exp(jnp.where(visible, spread, 0.0)) * x, 0.0)))
    got = [mm3(x, (wh_ref[h, steps_of(c), :], wl_ref[h, steps_of(c), :])) for (h, c), x in zip(items, inner)]
    eff = [lifted[h][tokens_of(c)] - x[:, :DK] for (h, c), x in zip(items, got)]
    eff_pieces = [split(x) for x in eff]
    taken = [None if c == 0 else mm3(x, starts[h][c]) for (h, c), x in zip(items, eff_pieces)]
    for (h, c), x, y, z in zip(items, eff_pieces, got, taken):
        at_out = (tokens_of(c), slice(h * DK, (h + 1) * DK))
        qh_out[at_out], ql_out[at_out] = x if c == 0 else split(z[:, :DK])
        own_out[at_out] = y[:, DK:] if c == 0 else y[:, DK:] + z[:, DK:]


def group_reads(which, query_rows, key_rows, tails, query_kernel, key_kernel, scalars, kept):
    _, _, chunk_rows, read_cols = scalars
    tokens, width = query_rows.shape
    steps = tokens * NH
    heads = width // DK
    group = heads // PLANE
    turns = group // HB
    lanes = HB * DK
    chunks = steps // CHUNK

    def wide(i, g):
        return (0, g[0] * turns + i)

    def here(i, g):
        return (0, i)

    def local(i, g):
        return (i, 0, 0)

    return pl.pallas_call(
        reads_kernel,
        grid_spec=pltpu.PrefetchScalarGridSpec(
            num_scalar_prefetch=1,
            grid=(turns,),
            in_specs=[
                pl.BlockSpec((tokens, lanes), wide),
                pl.BlockSpec((tails.shape[0], lanes), wide),
                pl.BlockSpec((4, lanes), wide),
                pl.BlockSpec((steps, lanes), wide),
                pl.BlockSpec((4, lanes), wide),
                pl.BlockSpec((1, tokens, group), lambda i, g: (g[0], 0, 0)),
                pl.BlockSpec((HB, chunks, CHUNK), lambda i, g: (g[0] * turns + i, 0, 0)),
                pl.BlockSpec((HB, steps, 2 * DK), local),
                pl.BlockSpec((HB, steps, 2 * DK), local),
                pl.BlockSpec((HB, 3 * DK, 2 * DK), local),
                pl.BlockSpec((HB, 3 * DK, 2 * DK), local),
            ],
            out_specs=[
                pl.BlockSpec((tokens, lanes), here),
                pl.BlockSpec((tokens, lanes), here),
                pl.BlockSpec((tokens, lanes), here),
            ],
            scratch_shapes=[pltpu.VMEM((tokens + 16, lanes), BF16), pltpu.VMEM((steps + 16, lanes), BF16)],
        ),
        out_shape=(
            jax.ShapeDtypeStruct((tokens, group * DK), BF16),
            jax.ShapeDtypeStruct((tokens, group * DK), BF16),
            jax.ShapeDtypeStruct((tokens, group * DK), F32),
        ),
        compiler_params=pltpu.CompilerParams(vmem_limit_bytes=VMEM),
        name="reads",
    )(which, query_rows, tails, query_kernel, key_rows, key_kernel, read_cols, chunk_rows, *kept)


def small(kernel, flags, operands, outs, name):
    def whole(shape):
        return pl.BlockSpec(shape, lambda i, *_: (0,) * len(shape))

    return pl.pallas_call(
        kernel,
        grid_spec=pltpu.PrefetchScalarGridSpec(
            num_scalar_prefetch=len(flags),
            grid=(1,),
            in_specs=[whole(x.shape) for x in operands],
            out_specs=[whole(shape) for shape in outs],
        ),
        out_shape=[jax.ShapeDtypeStruct(shape, F32) for shape in outs],
        name=name,
    )(*flags, *operands)


def after(first, mine, other):
    early = jnp.where(first, mine, other)
    late = jnp.where(first, other, mine)
    both = mm3(split(late[:, :DK]), split(early))
    return jnp.concatenate([both[:, :DK], both[:, DK:] + late[:, DK:]], axis=1)


def compose_kernel(core_ref, mine_ref, other_ref, out_ref):
    heads = range(mine_ref.shape[0])
    for h, x in enumerate([after(core_ref[0] == 0, mine_ref[h], other_ref[h]) for h in heads]):
        out_ref[h] = x


def composed(core, mine, other):
    return small(compose_kernel, [core], [mine, other], [mine.shape], "compose")[0]


def plane_kernel(core_ref, chip_ref, mine_ref, pair_ref, other_ref, chip_out, plane_out, offset_out):
    heads = range(mine_ref.shape[0])
    chips = [after(core_ref[0] == 0, mine_ref[h], pair_ref[h]) for h in heads]
    planes = [after(chip_ref[0] == 0, chips[h], other_ref[h]) for h in heads]
    for h in heads:
        chip_out[h] = chips[h]
        plane_out[h] = planes[h]
        offset_out[h] = planes[h][:, DK:]


def plane_composed(core, chip, mine, pair, other):
    heads = mine.shape[0]
    return small(
        plane_kernel, [core, chip], [mine, pair, other], [mine.shape, mine.shape, (heads, DK, DK)], "plane"
    )


def apply_kernel(map_ref, state_ref, out_ref):
    heads = range(map_ref.shape[0])
    got = [mm3(split(map_ref[h, :, :DK]), split(state_ref[h])) for h in heads]
    for h in heads:
        out_ref[h] = got[h] + map_ref[h, :, DK:]


def applied(maps, state):
    return small(apply_kernel, [], [maps, state], [state.shape], "apply")[0]


def branches(first, mine, other, entry):
    heads = range(len(entry))
    early = [jnp.where(first, mine[h], other[h]) for h in heads]
    later = [mm3(split(early[h][:, :DK]), split(entry[h])) + early[h][:, DK:] for h in heads]
    own = [jnp.where(first, entry[h], later[h]) for h in heads]
    return own, [jnp.where(first, later[h], entry[h]) for h in heads]


def branch_kernel(core_ref, mine_ref, other_ref, entry_ref, keep_out, send_out):
    refs = (mine_ref, other_ref, entry_ref)
    own, send = branches(core_ref[0] == 0, *([x[h] for h in range(x.shape[0])] for x in refs))
    for h in range(len(own)):
        keep_out[h] = own[h]
        send_out[h] = send[h]


def branched(core, mine, other, entry):
    return small(branch_kernel, [core], [mine, other, entry], [entry.shape] * 2, "branch")


def fork_kernel(core_ref, chip_ref, chip_map_ref, from_chip_ref, map_ref, pair_ref, entry_ref, *outs):
    refs = (chip_map_ref, from_chip_ref, map_ref, pair_ref, entry_ref)
    chip_map, from_chip, mine, pair, entry = ([x[h] for h in range(x.shape[0])] for x in refs)
    own, across = branches(chip_ref[0] == 0, chip_map, from_chip, entry)
    for out_ref, states in zip(outs, (across, *branches(core_ref[0] == 0, mine, pair, own))):
        for h, state in enumerate(states):
            out_ref[h] = state


def forked(core, chip, chip_map, from_chip, mine, pair, entry):
    operands = [chip_map, from_chip, mine, pair, entry]
    return small(fork_kernel, [core, chip], operands, [entry.shape] * 3, "fork")


def finish_kernel(group_ref, *refs):
    out_ref = refs[-1]
    count = (len(refs) - 1) // 4
    for turn in range(count):
        qh_ref, ql_ref, own_ref, entry_ref = refs[4 * turn : 4 * turn + 4]

        @pl.when(pl.program_id(0) == turn)
        def _():
            for h in range(entry_ref.shape[0]):
                lanes = slice(h * DK, (h + 1) * DK)
                got = mm3((qh_ref[:, lanes], ql_ref[:, lanes]), split(entry_ref[h]))
                out_ref[:, lanes] = (own_ref[:, lanes] + got).astype(BF16)


def finished(order, reads, entries, out, width):
    tokens, lanes = reads[0][0].shape
    operands, specs = [], []
    for (qh, ql, own), entry in zip(reads, entries):
        operands += [qh, ql, own, entry]
        specs += [pl.BlockSpec((tokens, lanes), lambda i, g: (0, 0))] * 3
        specs += [pl.BlockSpec(entry.shape, lambda i, g: (0, 0, 0))]
    if out is not None:
        operands.append(out)
        specs.append(pl.BlockSpec(memory_space=pl.ANY))
    return pl.pallas_call(
        finish_kernel,
        grid_spec=pltpu.PrefetchScalarGridSpec(
            num_scalar_prefetch=1,
            grid=(len(reads),),
            in_specs=specs,
            out_specs=pl.BlockSpec((tokens, lanes), lambda i, g: (0, g[i])),
        ),
        out_shape=jax.ShapeDtypeStruct((tokens, width), BF16),
        input_output_aliases={} if out is None else {len(operands): 0},
        name="finish",
    )(order, *operands)


def moved(x, pairs):
    return pltpu.with_memory_space_constraint(lax.ppermute(x, "seq", pairs), pltpu.VMEM)


def local(
    count,
    query_rows,
    key_rows,
    value_rows,
    write_rate,
    log_gate,
    keep_mask,
    query_kernel,
    key_kernel,
    value_kernel,
):
    tails = moved(last_rows(query_rows, key_rows, value_rows), [(s, s + 1) for s in range(count - 1)])
    scalars = prep(write_rate, log_gate, keep_mask)
    place = lax.axis_index("seq") % PLANE
    core = (place % 2)[None]
    chip = (place // 2)[None]
    pair = [(s, s ^ 1) for s in range(count)]
    across = [(s, s ^ 2) for s in range(count)]
    onward = [(s, s + PLANE) for s in range(count - PLANE)]
    groups = [(place ^ x)[None] for x in (3, 1, 2, 0)]
    made = [group_maps(g, key_rows, value_rows, tails, key_kernel, value_kernel, scalars) for g in groups]
    maps = [m[0] for m in made]
    from_pair = [moved(m, pair) for m in maps[:2]]
    next_map = composed(core, maps[2], from_pair[0])
    from_chip = moved(next_map, across)
    chip_map, plane_map, offset = plane_composed(core, chip, maps[3], from_pair[1], from_chip)
    plane_map, offset, kept = lax.optimization_barrier((plane_map, offset, [m[1:] for m in made]))

    def read(i):
        return group_reads(
            groups[i], query_rows, key_rows, tails, query_kernel, key_kernel, scalars, kept[i]
        )

    reads = []
    entry = moved(offset, onward)
    for i in range(count // PLANE - 1):
        if i > 0:
            entry = moved(applied(plane_map, entry), onward)
        if len(reads) < PLANE - 1:
            reads.append(read(i))
            entry, reads[-1] = lax.optimization_barrier((entry, reads[-1]))
    send, own_entry, own_send = forked(core, chip, chip_map, from_chip, maps[3], from_pair[1], entry)
    theirs = moved(send, across)
    far_own = moved(own_send, pair)
    reads += [read(i) for i in range(len(reads), PLANE)]
    width = query_rows.shape[1]
    out = finished(groups[3], reads[3:], [own_entry], None, width)
    out = finished(groups[1], reads[1:2], [far_own], out, width)
    theirs, out = lax.optimization_barrier((theirs, out))
    next_entry, next_send = branched(core, maps[2], from_pair[0], theirs)
    far_next = moved(next_send, pair)
    out = finished(groups[2], reads[2:3], [next_entry], out, width)
    far_next, out = lax.optimization_barrier((far_next, out))
    return finished(groups[0], reads[:1], [far_next], out, width)


def solution(mesh):
    rows = P(("groups", "seq"), None)
    return jax.shard_map(
        functools.partial(local, mesh.shape["seq"]),
        mesh=mesh,
        in_specs=(rows, rows, rows, rows, rows, rows, P(), P(), P()),
        out_specs=rows,
        check_vma=False,
    )
```

```python
import functools

import jax
import jax.numpy as jnp
from jax import lax
from jax.experimental import pallas as pl
from jax.experimental.pallas import tpu as pltpu
from jax.sharding import PartitionSpec as P

NH = 2
BLOCK = 16
SPAN = 64
DK = 128
CHUNK = 128
HALF = 64
PLANE = 4
HB = 2
VMEM = 24 << 20
SMALL = pltpu.CompilerParams(vmem_limit_bytes=8 << 20)

WHOLE = pl.BlockSpec(memory_space=pltpu.VMEM)

F32 = jnp.float32
BF16 = jnp.bfloat16
NN = (((1,), (0,)), ((), ()))
NT = (((1,), (1,)), ((), ()))


def split(x):
    high = x.astype(BF16)
    low = (x - high.astype(F32)).astype(BF16)
    return high, low


def mm(a, b, dims=NN):
    return lax.dot_general(a, b, dims, preferred_element_type=F32)


def mm3(a, b):
    ah, al = a
    bh, bl = b
    return mm(jnp.concatenate([ah, al], axis=1), jnp.concatenate([bh, bh], axis=0)) + mm(ah, bl)


def mm3_nt(a, b):
    ah, al = a
    bh, bl = b
    return mm(jnp.concatenate([ah, al], axis=1), jnp.concatenate([bh, bh], axis=1), NT) + mm(ah, bl, NT)


def halves(x):
    left = iota(x.shape, 1) < HALF
    zero = jnp.zeros_like(x)
    return jnp.concatenate([jnp.where(left, x, zero), jnp.where(left, zero, x)], axis=0)


def pair_product(x, y):
    return mm3(x, (halves(y[0]), halves(y[1])))


def silu(v):
    return v / (1.0 + jnp.exp(-v))


def load_rows(scratch, rows_ref, lanes, tail):
    before = jnp.concatenate([jnp.zeros((13, tail.shape[1]), F32), tail.astype(F32)], axis=0)
    scratch[0:16, :] = before.astype(BF16)
    scratch[16 : 16 + rows_ref.shape[0], :] = rows_ref[:, lanes]


def shifter():
    shape = (3 * HALF, HALF + 16)
    row, col = iota(shape, 0), iota(shape, 1)
    return (col == 15 + row % HALF - row // HALF).astype(F32).astype(BF16)


def conv(shifts, scratch, kernel_ref, start, count):
    parts = []
    for at in range(start, start + count, HALF):
        moved = mm(shifts, scratch[at : at + HALF + 16, :])
        total = kernel_ref[3:4, :] * scratch[at + 16 : at + 16 + HALF, :].astype(F32)
        for back in range(1, 4):
            total = total + kernel_ref[3 - back : 4 - back, :] * moved[(back - 1) * HALF : back * HALF]
        parts.append(silu(total))
    return jnp.concatenate(parts, axis=0)


def unit(x):
    return x * lax.rsqrt(jnp.sum(x * x, axis=-1, keepdims=True) + 1e-06)


CORE, CHIP, GROUPS = 0, 1, 2
FLAGS = jax.ShapeDtypeStruct((8,), jnp.int32)
FLAGS_SPEC = pl.BlockSpec(memory_space=pltpu.SMEM)
TOKEN = pltpu.VMEM((8, 128), jnp.int32)


def hand_on(token_ref, token_out):
    token_out[...] = token_ref[...]


def lanes_at(flags_ref, which, at, group):
    first = flags_ref[GROUPS + which] * group + at * HB
    return pl.ds(pl.multiple_of(first * DK, HB * DK), HB * DK)


def in_hbm(x):
    return pltpu.with_memory_space_constraint(x, pltpu.HBM)


def held(x):
    return pltpu.with_memory_space_constraint(x, pltpu.VMEM)


def iota(shape, dim):
    return lax.broadcasted_iota(jnp.int32, shape, dim)


def prep_kernel(at_ref, rate_ref, log_ref, mask_ref, rate_out, cum_out, row_out, read_out, flags_out, token_out):
    token_out[...] = jnp.zeros_like(token_out)
    place = lax.rem(at_ref[0], PLANE)
    flags_out[CORE] = lax.rem(place, 2)
    flags_out[CHIP] = lax.div(place, 2)
    for i, other in enumerate((3, 1, 2, 0)):
        flags_out[GROUPS + i] = place ^ other
    for i in range(GROUPS + PLANE, FLAGS.shape[0]):
        flags_out[i] = 0
    heads, steps = rate_ref.shape
    tokens = log_ref.shape[1]
    group = heads // PLANE
    subs, blocks = mask_ref.shape
    row_of = (iota((steps, blocks), 0) // SPAN == iota((steps, blocks), 1)).astype(F32)
    picked = mm(row_of, mask_ref[...].astype(F32), NT)
    sub_of = ((iota((steps, subs), 0) % SPAN) // BLOCK == iota((steps, subs), 1)).astype(F32)
    keep = jnp.sum(picked * sub_of, axis=1, keepdims=True)
    rates = rate_ref[...].T * keep
    turned = log_ref[...]
    logs = turned.T
    window = CHUNK // NH

    def upto(token, last):
        return ((token // window == last // window) & (token <= last)).astype(F32)

    high = lax.Precision.HIGHEST
    cum = jnp.dot(
        upto(iota((steps, tokens), 1), iota((steps, tokens), 0) // NH), logs, precision=high, preferred_element_type=F32
    )
    read = jnp.dot(
        upto(iota((tokens, tokens), 1), iota((tokens, tokens), 0)), logs, precision=high, preferred_element_type=F32
    )
    row = jnp.dot(
        turned,
        upto(iota((tokens, steps), 0), iota((tokens, steps), 1) // NH),
        precision=high,
        preferred_element_type=F32,
    )
    for g in range(PLANE):
        rate_out[g] = rates[:, g * group : (g + 1) * group]
        cum_out[g] = cum[:, g * group : (g + 1) * group]
        read_out[g] = read[:, g * group : (g + 1) * group]
    for b in range(steps // CHUNK):
        row_out[:, b, :] = row[:, b * CHUNK : (b + 1) * CHUNK]


def last_rows_kernel(query_ref, key_ref, value_ref, out_ref):
    for i, ref in enumerate((query_ref, key_ref, value_ref)):
        out_ref[3 * i : 3 * i + 3, :] = ref[...].astype(F32)[13:16].astype(BF16)


def last_rows(*arrays):
    width = arrays[0].shape[1]
    return pl.pallas_call(
        last_rows_kernel,
        grid=(1,),
        in_specs=[pl.BlockSpec((16, width), functools.partial(lambda at, i: (at, 0), x.shape[0] // 16 - 1)) for x in arrays],
        out_specs=pl.BlockSpec((9, width), lambda i: (0, 0)),
        out_shape=jax.ShapeDtypeStruct((9, width), BF16),
        compiler_params=SMALL,
        name="last_rows",
    )(*map(in_hbm, arrays))


def prep(at, write_rate, log_gate, keep_mask):
    steps, heads = write_rate.shape
    tokens = log_gate.shape[0]
    group = heads // PLANE
    return pl.pallas_call(
        prep_kernel,
        out_shape=(
            jax.ShapeDtypeStruct((PLANE, steps, group), F32),
            jax.ShapeDtypeStruct((PLANE, steps, group), F32),
            jax.ShapeDtypeStruct((heads, steps // CHUNK, CHUNK), F32),
            jax.ShapeDtypeStruct((PLANE, tokens, group), F32),
            FLAGS,
            TOKEN,
        ),
        in_specs=[FLAGS_SPEC] + [WHOLE] * 3,
        out_specs=[WHOLE] * 4 + [FLAGS_SPEC, WHOLE],
        compiler_params=pltpu.CompilerParams(vmem_limit_bytes=VMEM),
        name="prep",
    )(at, write_rate.T, log_gate.T, keep_mask.T)


def block_inverses(lowers, fill):
    row = iota((HALF, CHUNK), 0)
    col = iota((HALF, CHUNK), 1) % HALF
    eye = (row == col).astype(F32)
    near = row // BLOCK == col // BLOCK
    inner = [jnp.where(near, -x, 0.0) for x in lowers]
    outer = [split(jnp.where(near, 0.0, x)) for x in lowers]
    power = [split(x) for x in inner]
    a = [eye + x for x in inner]
    for _ in range(3):
        fill()
        power = [split(pair_product(x, x)) for x in power]
        fill()
        a = [x + pair_product(split(x), y) for x, y in zip(a, power)]
    sa = [split(x) for x in a]
    fill()
    m = [split(pair_product(x, y)) for x, y in zip(sa, outer)]
    fill()
    m2 = [split(pair_product(x, x)) for x in m]
    t = [x - pair_product(y, z) for x, y, z in zip(a, m, sa)]
    return [x + pair_product(y, split(x)) for x, y in zip(t, m2)]


def maps_kernel(
    which,
    flags_ref,
    key_ref,
    value_ref,
    tail_ref,
    key_kernel_ref,
    value_kernel_ref,
    rate_ref,
    cum_ref,
    row_ref,
    token_ref,
    map_out,
    wh_out,
    wl_out,
    mh_out,
    ml_out,
    token_out,
    scratch,
    value_scratch,
):
    hand_on(token_ref, token_out)
    steps = key_ref.shape[0]
    chunks = steps // CHUNK
    at = pl.program_id(0)
    lanes = lanes_at(flags_ref, which, at, rate_ref.shape[2])
    load_rows(scratch, key_ref, lanes, tail_ref[3:6, :])
    load_rows(value_scratch, value_ref, lanes, tail_ref[6:9, :])
    shifts = shifter()
    keys = conv(shifts, scratch, key_kernel_ref, 0, steps)
    keys = jnp.concatenate([unit(keys[:, h * DK : (h + 1) * DK]) for h in range(HB)], axis=1)
    kh, kl = split(keys)
    group = rate_ref.shape[2]
    rates, cums = rate_ref[0], cum_ref[0]

    def column(x, h):
        out = x[:, h : h + 1]
        for turn in range(1, group // HB):
            out = jnp.where(at == turn, x[:, turn * HB + h : turn * HB + h + 1], out)
        return out

    below = iota((CHUNK, CHUNK), 1) < iota((CHUNK, CHUNK), 0)
    left = iota((HALF, CHUNK), 1) < HALF
    items = [(h, c) for h in range(HB) for c in range(chunks)]
    columns = [(column(rates, h), column(cums, h)) for h in range(HB)]
    lowers, crosses, sides, faded, ends = [], [], {}, {}, {}
    for h, c in items:
        lanes = slice(h * DK, (h + 1) * DK)
        rows = slice(c * CHUNK, (c + 1) * CHUNK)
        row_c = row_ref[h, c : c + 1, :]
        rate_c, cum_c = (x[rows] for x in columns[h])
        mine = (kh[rows, lanes], kl[rows, lanes])
        decay = jnp.exp(jnp.where(below, cum_c - row_c, 0.0))
        lower = jnp.where(below, rate_c * decay * mm3_nt(mine, mine), 0.0)
        lowers.append(jnp.where(left, lower[:HALF], lower[HALF:]))
        crosses.append(split(jnp.where(left, lower[HALF:], 0.0)))

    def side(c):
        rows = slice(c * CHUNK, (c + 1) * CHUNK)
        values = conv(shifts, value_scratch, value_kernel_ref, c * CHUNK, CHUNK)
        for h in range(HB):
            lanes = slice(h * DK, (h + 1) * DK)
            rate_c, cum_c = (x[rows] for x in columns[h])
            grown = rate_c * jnp.exp(cum_c) * keys[rows, lanes]
            sides[h, c] = split(jnp.concatenate([grown, rate_c * values[:, lanes]], axis=1))

    def fade(c):
        for h in range(HB):
            row_c = row_ref[h, c : c + 1, :]
            end = row_c[:, CHUNK - 1 : CHUNK]
            k_c = keys[c * CHUNK : (c + 1) * CHUNK, h * DK : (h + 1) * DK]
            faded[h, c] = split(k_c.T * jnp.exp(end - row_c))
            ends[h, c] = jnp.exp(end)

    todo = [functools.partial(f, c) for c in range(chunks) for f in (side, fade)]

    def fill():
        if todo:
            todo.pop(0)()

    eye = (iota((DK, DK), 0) == iota((DK, DK), 1)).astype(F32)
    inverses = block_inverses(lowers, fill)
    while todo:
        fill()
    pieces = [split(x) for x in inverses]
    under = [mm3(y, tuple(jnp.concatenate([z, z], axis=0) for z in x)) for x, y in zip(pieces, crosses)]
    under = [split(jnp.where(left, x, 0.0)) for x in under]
    under = [
        mm3(x, tuple(jnp.concatenate([jnp.zeros_like(z), z], axis=0) for z in y)) for x, y in zip(pieces, under)
    ]
    whole = [
        split(jnp.concatenate([jnp.where(left, x, 0.0), jnp.where(left, -y, x)], axis=0))
        for x, y in zip(inverses, under)
    ]
    solved = [split(mm3(x, sides[i])) for i, x in zip(items, whole)]
    for (h, c), x in zip(items, solved):
        at_w = slice(c * CHUNK, (c + 1) * CHUNK)
        wh_out[at * HB + h, at_w, :], wl_out[at * HB + h, at_w, :] = x
    made = [mm3(faded[i], x) for i, x in zip(items, solved)]
    made = [jnp.concatenate([ends[i] * eye - x[:, :DK], x[:, DK:]], axis=1) for i, x in zip(items, made)]

    def then(late, early):
        both = mm3(split(late[:, :DK]), early)
        return jnp.concatenate([both[:, :DK], both[:, DK:] + late[:, DK:]], axis=1)

    assert chunks == 4
    heads = range(HB)
    first, third = ([split(made[h * chunks + c]) for h in heads] for c in (0, 2))
    two = [split(then(made[h * chunks + 1], first[h])) for h in heads]
    last = [then(made[h * chunks + 3], third[h]) for h in heads]
    last = [then(last[h], two[h]) for h in heads]
    for h in heads:
        map_out[at * HB + h] = last[h]
        for i, x in enumerate((first[h], two[h], third[h])):
            at_m = slice(i * DK, (i + 1) * DK)
            mh_out[at * HB + h, at_m, :], ml_out[at * HB + h, at_m, :] = x


def group_maps(flags, token, which, key_rows, value_rows, tails, key_kernel, value_kernel, scalars):
    rate_cols, cum_cols, chunk_rows, _ = scalars
    steps, width = key_rows.shape
    heads = width // DK
    group = heads // PLANE
    turns = group // HB
    lanes = HB * DK
    chunks = steps // CHUNK

    def wide(i, g):
        return (0, g[GROUPS + which] * turns + i)

    def per_head(i, g):
        return (g[GROUPS + which] * turns + i, 0, 0)

    return pl.pallas_call(
        functools.partial(maps_kernel, which),
        grid_spec=pltpu.PrefetchScalarGridSpec(
            num_scalar_prefetch=1,
            grid=(turns,),
            in_specs=[
                WHOLE,
                WHOLE,
                pl.BlockSpec((tails.shape[0], lanes), wide),
                pl.BlockSpec((4, lanes), wide),
                pl.BlockSpec((4, lanes), wide),
                pl.BlockSpec((1, steps, group), lambda i, g: (g[GROUPS + which], 0, 0)),
                pl.BlockSpec((1, steps, group), lambda i, g: (g[GROUPS + which], 0, 0)),
                pl.BlockSpec((HB, chunks, CHUNK), per_head),
                WHOLE,
            ],
            out_specs=[
                WHOLE,
                WHOLE,
                WHOLE,
                WHOLE,
                WHOLE,
                WHOLE,
            ],
            scratch_shapes=[pltpu.VMEM((steps + 16, lanes), BF16)] * 2,
        ),
        out_shape=(
            pltpu.VMEM((group, DK, 2 * DK), F32),
            pltpu.VMEM((group, steps, 2 * DK), BF16),
            pltpu.VMEM((group, steps, 2 * DK), BF16),
            pltpu.VMEM((group, 3 * DK, 2 * DK), BF16),
            pltpu.VMEM((group, 3 * DK, 2 * DK), BF16),
            TOKEN,
        ),
        compiler_params=pltpu.CompilerParams(vmem_limit_bytes=VMEM),
        name="maps",
    )(flags, key_rows, value_rows, tails, key_kernel, value_kernel, rate_cols, cum_cols, chunk_rows, held(token))


def reads_kernel(
    which,
    flags_ref,
    query_ref,
    tail_ref,
    query_kernel_ref,
    key_ref,
    key_kernel_ref,
    read_ref,
    row_ref,
    wh_ref,
    wl_ref,
    mh_ref,
    ml_ref,
    token_ref,
    qh_out,
    ql_out,
    own_out,
    token_out,
    scratch,
    key_scratch,
):
    hand_on(token_ref, token_out)
    tokens = query_ref.shape[0]
    window = CHUNK // NH
    chunks = tokens // window
    at = pl.program_id(0)
    lanes = lanes_at(flags_ref, which, at, read_ref.shape[2])
    load_rows(scratch, query_ref, lanes, tail_ref[0:3, :])
    shifts = shifter()
    queries = conv(shifts, scratch, query_kernel_ref, 0, tokens)
    queries = jnp.concatenate([unit(queries[:, h * DK : (h + 1) * DK]) for h in range(HB)], axis=1)
    load_rows(key_scratch, key_ref, lanes, tail_ref[3:6, :])
    keys = conv(shifts, key_scratch, key_kernel_ref, 0, NH * tokens)
    group = read_ref.shape[2]
    reads = read_ref[0]
    visible = iota((window, CHUNK), 1) <= NH * iota((window, CHUNK), 0) + NH - 1
    items = [(h, c) for h in range(HB) for c in range(chunks)]
    pieces, columns, lifted = [], [], []
    for h in range(HB):
        lanes = slice(h * DK, (h + 1) * DK)
        read_h = reads[:, h : h + 1]
        for turn in range(1, group // HB):
            read_h = jnp.where(at == turn, reads[:, turn * HB + h : turn * HB + h + 1], read_h)
        columns.append(read_h)
        lifted.append(jnp.exp(read_h) * queries[:, lanes])
        pieces.append((split(queries[:, lanes]), split(unit(keys[:, lanes]))))

    def tokens_of(c):
        return slice(c * window, (c + 1) * window)

    def steps_of(c):
        return slice(c * CHUNK, (c + 1) * CHUNK)

    scores = [
        mm3_nt(tuple(x[tokens_of(c)] for x in pieces[h][0]), tuple(x[steps_of(c)] for x in pieces[h][1]))
        for h, c in items
    ]
    starts = {}
    for h in range(HB):
        kept = [tuple(x[at * HB + h, i * DK : (i + 1) * DK, :] for x in (mh_ref, ml_ref)) for i in range(3)]
        first, two, third = kept
        three = mm3(tuple(x[:, :DK] for x in third), two)
        late = third[0][:, DK:].astype(F32) + third[1][:, DK:].astype(F32)
        three = split(jnp.concatenate([three[:, :DK], three[:, DK:] + late], axis=1))
        starts[h] = [None, first, two, three]
    inner = []
    for (h, c), x in zip(items, scores):
        spread = columns[h][tokens_of(c)] - row_ref[h, c : c + 1, :]
        inner.append(split(jnp.where(visible, jnp.exp(jnp.where(visible, spread, 0.0)) * x, 0.0)))
    solved = [tuple(x[at * HB + h, steps_of(c), :] for x in (wh_ref, wl_ref)) for h, c in items]
    got = [mm3(x, y) for x, y in zip(inner, solved)]
    eff = [lifted[h][tokens_of(c)] - x[:, :DK] for (h, c), x in zip(items, got)]
    eff_pieces = [split(x) for x in eff]
    taken = [None if c == 0 else mm3(x, starts[h][c]) for (h, c), x in zip(items, eff_pieces)]
    for (h, c), x, y, z in zip(items, eff_pieces, got, taken):
        at_out = (at * HB + h, tokens_of(c))
        qh_out[at_out], ql_out[at_out] = x if c == 0 else split(z[:, :DK])
        own_out[at_out] = y[:, DK:] if c == 0 else y[:, DK:] + z[:, DK:]


def group_reads(flags, token, which, query_rows, key_rows, tails, query_kernel, key_kernel, scalars, kept):
    _, _, chunk_rows, read_cols = scalars
    tokens, width = query_rows.shape
    steps = tokens * NH
    heads = width // DK
    group = heads // PLANE
    turns = group // HB
    lanes = HB * DK
    chunks = steps // CHUNK

    def wide(i, g):
        return (0, g[GROUPS + which] * turns + i)

    return pl.pallas_call(
        functools.partial(reads_kernel, which),
        grid_spec=pltpu.PrefetchScalarGridSpec(
            num_scalar_prefetch=1,
            grid=(turns,),
            in_specs=[
                WHOLE,
                pl.BlockSpec((tails.shape[0], lanes), wide),
                pl.BlockSpec((4, lanes), wide),
                WHOLE,
                pl.BlockSpec((4, lanes), wide),
                pl.BlockSpec((1, tokens, group), lambda i, g: (g[GROUPS + which], 0, 0)),
                pl.BlockSpec((HB, chunks, CHUNK), lambda i, g: (g[GROUPS + which] * turns + i, 0, 0)),
                WHOLE,
                WHOLE,
                WHOLE,
                WHOLE,
                WHOLE,
            ],
            out_specs=[WHOLE] * 4,
            scratch_shapes=[pltpu.VMEM((tokens + 16, lanes), BF16), pltpu.VMEM((steps + 16, lanes), BF16)],
        ),
        out_shape=(
            pltpu.VMEM((group, tokens, DK), BF16),
            pltpu.VMEM((group, tokens, DK), BF16),
            pltpu.VMEM((group, tokens, DK), F32),
            TOKEN,
        ),
        compiler_params=pltpu.CompilerParams(vmem_limit_bytes=VMEM),
        name="reads",
    )(flags, query_rows, tails, query_kernel, key_rows, key_kernel, read_cols, chunk_rows, *map(held, kept), held(token))


def small(kernel, flags, token, operands, outs, name):
    def whole(shape):
        return pl.BlockSpec(shape, lambda i, f: (0,) * len(shape))

    def body(flags_ref, token_ref, *refs):
        hand_on(token_ref, refs[-1])
        kernel(flags_ref, *refs[:-1])

    return pl.pallas_call(
        body,
        grid_spec=pltpu.PrefetchScalarGridSpec(
            num_scalar_prefetch=1,
            grid=(1,),
            in_specs=[WHOLE] + [whole(x.shape) for x in operands],
            out_specs=[whole(shape) for shape in outs] + [WHOLE],
        ),
        out_shape=[jax.ShapeDtypeStruct(shape, F32) for shape in outs] + [TOKEN],
        compiler_params=SMALL,
        name=name,
    )(flags, held(token), *operands)


def after(first, mine, other):
    early = jnp.where(first, mine, other)
    late = jnp.where(first, other, mine)
    both = mm3(split(late[:, :DK]), split(early))
    return jnp.concatenate([both[:, :DK], both[:, DK:] + late[:, DK:]], axis=1)


def compose_kernel(flags_ref, mine_ref, other_ref, out_ref):
    heads = range(mine_ref.shape[0])
    for h, x in enumerate([after(flags_ref[CORE] == 0, mine_ref[h], other_ref[h]) for h in heads]):
        out_ref[h] = x


def composed(flags, token, mine, other):
    return small(compose_kernel, flags, token, [mine, other], [mine.shape], "compose")


def plane_kernel(flags_ref, mine_ref, pair_ref, other_ref, chip_out, plane_out, offset_out):
    heads = range(mine_ref.shape[0])
    chips = [after(flags_ref[CORE] == 0, mine_ref[h], pair_ref[h]) for h in heads]
    planes = [after(flags_ref[CHIP] == 0, chips[h], other_ref[h]) for h in heads]
    for h in heads:
        chip_out[h] = chips[h]
        plane_out[h] = planes[h]
        offset_out[h] = planes[h][:, DK:]


def plane_composed(flags, token, mine, pair, other):
    heads = mine.shape[0]
    return small(
        plane_kernel, flags, token, [mine, pair, other], [mine.shape, mine.shape, (heads, DK, DK)], "plane"
    )


def apply_kernel(flags_ref, map_ref, state_ref, out_ref):
    heads = range(map_ref.shape[0])
    got = [mm3(split(map_ref[h, :, :DK]), split(state_ref[h])) for h in heads]
    for h in heads:
        out_ref[h] = got[h] + map_ref[h, :, DK:]


def applied(flags, token, maps, state):
    return small(apply_kernel, flags, token, [maps, state], [state.shape], "apply")


def branches(first, mine, other, entry):
    heads = range(len(entry))
    early = [jnp.where(first, mine[h], other[h]) for h in heads]
    later = [mm3(split(early[h][:, :DK]), split(entry[h])) + early[h][:, DK:] for h in heads]
    own = [jnp.where(first, entry[h], later[h]) for h in heads]
    return own, [jnp.where(first, later[h], entry[h]) for h in heads]


def branch_kernel(flags_ref, mine_ref, other_ref, entry_ref, keep_out, send_out):
    refs = (mine_ref, other_ref, entry_ref)
    own, send = branches(flags_ref[CORE] == 0, *([x[h] for h in range(x.shape[0])] for x in refs))
    for h in range(len(own)):
        keep_out[h] = own[h]
        send_out[h] = send[h]


def branched(flags, token, mine, other, entry):
    return small(branch_kernel, flags, token, [mine, other, entry], [entry.shape] * 2, "branch")


def fork_kernel(flags_ref, chip_map_ref, from_chip_ref, map_ref, pair_ref, entry_ref, *outs):
    refs = (chip_map_ref, from_chip_ref, map_ref, pair_ref, entry_ref)
    chip_map, from_chip, mine, pair, entry = ([x[h] for h in range(x.shape[0])] for x in refs)
    own, across = branches(flags_ref[CHIP] == 0, chip_map, from_chip, entry)
    for out_ref, states in zip(outs, (across, *branches(flags_ref[CORE] == 0, mine, pair, own))):
        for h, state in enumerate(states):
            out_ref[h] = state


def forked(flags, token, chip_map, from_chip, mine, pair, entry):
    operands = [chip_map, from_chip, mine, pair, entry]
    return small(fork_kernel, flags, token, operands, [entry.shape] * 3, "fork")


def finish_kernel(flags_ref, token_ref, qh_ref, ql_ref, own_ref, entry_ref, *refs):
    out_ref, token_out = refs[-2:]
    hand_on(token_ref, token_out)
    for h in range(entry_ref.shape[0]):
        lanes = slice(h * DK, (h + 1) * DK)
        got = mm3((qh_ref[h], ql_ref[h]), split(entry_ref[h]))
        out_ref[:, lanes] = (own_ref[h] + got).astype(BF16)


def finished(flags, token, which, read, entry, out, width):
    qh, ql, own, _ = read
    group, tokens, _ = qh.shape
    operands = [held(token), held(qh), held(ql), held(own), entry]
    specs = [WHOLE] * 4 + [pl.BlockSpec(entry.shape, lambda i, g: (0, 0, 0))]
    if out is not None:
        operands.append(out)
        specs.append(pl.BlockSpec(memory_space=pl.ANY))
    return pl.pallas_call(
        finish_kernel,
        grid_spec=pltpu.PrefetchScalarGridSpec(
            num_scalar_prefetch=1,
            grid=(1,),
            in_specs=specs,
            out_specs=[pl.BlockSpec((tokens, group * DK), lambda i, g: (0, g[GROUPS + which])), WHOLE],
        ),
        out_shape=[jax.ShapeDtypeStruct((tokens, width), BF16), TOKEN],
        input_output_aliases={} if out is None else {len(operands): 0},
        compiler_params=SMALL,
        name="finish",
    )(flags, *operands)


def moved(x, pairs):
    return pltpu.with_memory_space_constraint(lax.ppermute(x, "seq", pairs), pltpu.VMEM)


def local(
    count,
    query_rows,
    key_rows,
    value_rows,
    write_rate,
    log_gate,
    keep_mask,
    query_kernel,
    key_kernel,
    value_kernel,
):
    tails = moved(last_rows(query_rows, key_rows, value_rows), [(s, s + 1) for s in range(count - 1)])
    query_rows, key_rows, value_rows = held(query_rows), held(key_rows), held(value_rows)
    query_kernel, key_kernel, value_kernel = held(query_kernel), held(key_kernel), held(value_kernel)
    *scalars, flags, token = prep(lax.axis_index("seq")[None], write_rate, log_gate, keep_mask)
    pair = [(s, s ^ 1) for s in range(count)]
    across = [(s, s ^ 2) for s in range(count)]
    onward = [(s, s + PLANE) for s in range(count - PLANE)]
    made, from_pair = [], []
    for i in range(PLANE):
        *one, token = group_maps(flags, token, i, key_rows, value_rows, tails, key_kernel, value_kernel, scalars)
        made.append(one)
        if i < 2:
            from_pair.append(moved(one[0], pair))
        if i == 2:
            next_map, token = composed(flags, token, one[0], from_pair[0])
            from_chip = moved(next_map, across)
    maps = [m[0] for m in made]
    chip_map, plane_map, offset, token = plane_composed(flags, token, maps[3], from_pair[1], from_chip)

    def read(token, i):
        return group_reads(
            flags, token, i, query_rows, key_rows, tails, query_kernel, key_kernel, scalars, made[i][1:]
        )

    reads = []
    entry = moved(offset, onward)
    for i in range(count // PLANE - 1):
        if i > 0:
            exit_state, token = applied(flags, token, plane_map, entry)
            entry = moved(exit_state, onward)
        if len(reads) < PLANE - 1:
            reads.append(read(token, i))
            token = reads[-1][-1]
    send, own_entry, own_send, token = forked(flags, token, chip_map, from_chip, maps[3], from_pair[1], entry)
    theirs = moved(send, across)
    far_own = moved(own_send, pair)
    for i in range(len(reads), PLANE):
        reads.append(read(token, i))
        token = reads[-1][-1]
    width = query_rows.shape[1]
    out, token = finished(flags, token, 3, reads[3], own_entry, None, width)
    out, token = finished(flags, token, 1, reads[1], far_own, out, width)
    next_entry, next_send, token = branched(flags, token, maps[2], from_pair[0], theirs)
    far_next = moved(next_send, pair)
    out, token = finished(flags, token, 2, reads[2], next_entry, out, width)
    return finished(flags, token, 0, reads[0], far_next, out, width)[0]


def solution(mesh):
    rows = P(("groups", "seq"), None)
    return jax.shard_map(
        functools.partial(local, mesh.shape["seq"]),
        mesh=mesh,
        in_specs=(rows, rows, rows, rows, rows, rows, P(), P(), P()),
        out_specs=rows,
        check_vma=False,
    )
```

```python
import functools

import jax
import jax.numpy as jnp
from jax import lax
from jax.experimental import pallas as pl
from jax.experimental.pallas import tpu as pltpu
from jax.sharding import PartitionSpec as P

NH = 2
BLOCK = 16
SPAN = 64
DK = 128
CHUNK = 128
HALF = 64
PLANE = 4
PARTS = 2
HB = 2
VMEM = 24 << 20
SMALL = pltpu.CompilerParams(vmem_limit_bytes=8 << 20)

WHOLE = pl.BlockSpec(memory_space=pltpu.VMEM)

F32 = jnp.float32
BF16 = jnp.bfloat16
NN = (((1,), (0,)), ((), ()))
NT = (((1,), (1,)), ((), ()))


def split(x):
    high = x.astype(BF16)
    low = (x - high.astype(F32)).astype(BF16)
    return high, low


def mm(a, b, dims=NN):
    return lax.dot_general(a, b, dims, preferred_element_type=F32)


def mm3(a, b):
    ah, al = a
    bh, bl = b
    return mm(jnp.concatenate([ah, al], axis=1), jnp.concatenate([bh, bh], axis=0)) + mm(ah, bl)


def mm3_nt(a, b):
    ah, al = a
    bh, bl = b
    return mm(jnp.concatenate([ah, al], axis=1), jnp.concatenate([bh, bh], axis=1), NT) + mm(ah, bl, NT)


def halves(x):
    left = iota(x.shape, 1) < HALF
    zero = jnp.zeros_like(x)
    return jnp.concatenate([jnp.where(left, x, zero), jnp.where(left, zero, x)], axis=0)


def pair_product(x, y):
    return mm3(x, (halves(y[0]), halves(y[1])))


def silu(v):
    return v / (1.0 + jnp.exp(-v))


def load_rows(scratch, rows_ref, lanes, tail):
    before = jnp.concatenate([jnp.zeros((13, tail.shape[1]), F32), tail.astype(F32)], axis=0)
    scratch[0:16, :] = before.astype(BF16)
    scratch[16 : 16 + rows_ref.shape[0], :] = rows_ref[:, lanes]


def shifter():
    shape = (3 * HALF, HALF + 16)
    row, col = iota(shape, 0), iota(shape, 1)
    return (col == 15 + row % HALF - row // HALF).astype(F32).astype(BF16)


def conv(shifts, scratch, kernel_ref, start, count):
    parts = []
    for at in range(start, start + count, HALF):
        moved = mm(shifts, scratch[at : at + HALF + 16, :])
        total = kernel_ref[3:4, :] * scratch[at + 16 : at + 16 + HALF, :].astype(F32)
        for back in range(1, 4):
            total = total + kernel_ref[3 - back : 4 - back, :] * moved[(back - 1) * HALF : back * HALF]
        parts.append(silu(total))
    return jnp.concatenate(parts, axis=0)


def unit(x):
    return x * lax.rsqrt(jnp.sum(x * x, axis=-1, keepdims=True) + 1e-06)


CORE, CHIP, GROUPS = 0, 1, 2
FLAGS = jax.ShapeDtypeStruct((8,), jnp.int32)
FLAGS_SPEC = pl.BlockSpec(memory_space=pltpu.SMEM)
TOKEN = pltpu.VMEM((8, 128), jnp.int32)


def hand_on(token_ref, token_out):
    token_out[...] = token_ref[...]


def lanes_at(flags_ref, which, at, group):
    first = flags_ref[GROUPS + which] * group + at * HB
    return pl.ds(pl.multiple_of(first * DK, HB * DK), HB * DK)


def in_hbm(x):
    return pltpu.with_memory_space_constraint(x, pltpu.HBM)


def held(x):
    return pltpu.with_memory_space_constraint(x, pltpu.VMEM)


def iota(shape, dim):
    return lax.broadcasted_iota(jnp.int32, shape, dim)


def prep_kernel(at_ref, rate_ref, log_ref, mask_ref, rate_out, cum_out, row_out, read_out, flags_out, token_out):
    token_out[...] = jnp.zeros_like(token_out)
    place = lax.rem(at_ref[0], PLANE)
    flags_out[CORE] = lax.rem(place, 2)
    flags_out[CHIP] = lax.div(place, 2)
    for i, other in enumerate((3, 1, 2, 0)):
        flags_out[GROUPS + i] = place ^ other
    for i in range(GROUPS + PLANE, FLAGS.shape[0]):
        flags_out[i] = 0
    heads, steps = rate_ref.shape
    tokens = log_ref.shape[1]
    group = heads // PLANE
    subs, blocks = mask_ref.shape
    row_of = (iota((steps, blocks), 0) // SPAN == iota((steps, blocks), 1)).astype(F32)
    picked = mm(row_of, mask_ref[...].astype(F32), NT)
    sub_of = ((iota((steps, subs), 0) % SPAN) // BLOCK == iota((steps, subs), 1)).astype(F32)
    keep = jnp.sum(picked * sub_of, axis=1, keepdims=True)
    rates = rate_ref[...].T * keep
    turned = log_ref[...]
    logs = turned.T
    window = CHUNK // NH

    def upto(token, last):
        return ((token // window == last // window) & (token <= last)).astype(F32)

    high = lax.Precision.HIGHEST
    cum = jnp.dot(
        upto(iota((steps, tokens), 1), iota((steps, tokens), 0) // NH), logs, precision=high, preferred_element_type=F32
    )
    read = jnp.dot(
        upto(iota((tokens, tokens), 1), iota((tokens, tokens), 0)), logs, precision=high, preferred_element_type=F32
    )
    row = jnp.dot(
        turned,
        upto(iota((tokens, steps), 0), iota((tokens, steps), 1) // NH),
        precision=high,
        preferred_element_type=F32,
    )
    for g in range(PLANE):
        rate_out[g] = rates[:, g * group : (g + 1) * group]
        cum_out[g] = cum[:, g * group : (g + 1) * group]
        read_out[g] = read[:, g * group : (g + 1) * group]
    for b in range(steps // CHUNK):
        row_out[:, b, :] = row[:, b * CHUNK : (b + 1) * CHUNK]


def last_rows_kernel(query_ref, key_ref, value_ref, out_ref):
    for i, ref in enumerate((query_ref, key_ref, value_ref)):
        out_ref[3 * i : 3 * i + 3, :] = ref[...].astype(F32)[13:16].astype(BF16)


def last_rows(*arrays):
    width = arrays[0].shape[1]
    return pl.pallas_call(
        last_rows_kernel,
        grid=(1,),
        in_specs=[pl.BlockSpec((16, width), functools.partial(lambda at, i: (at, 0), x.shape[0] // 16 - 1)) for x in arrays],
        out_specs=pl.BlockSpec((9, width), lambda i: (0, 0)),
        out_shape=jax.ShapeDtypeStruct((9, width), BF16),
        compiler_params=SMALL,
        name="last_rows",
    )(*map(in_hbm, arrays))


def prep(at, write_rate, log_gate, keep_mask):
    steps, heads = write_rate.shape
    tokens = log_gate.shape[0]
    group = heads // PLANE
    return pl.pallas_call(
        prep_kernel,
        out_shape=(
            jax.ShapeDtypeStruct((PLANE, steps, group), F32),
            jax.ShapeDtypeStruct((PLANE, steps, group), F32),
            jax.ShapeDtypeStruct((heads, steps // CHUNK, CHUNK), F32),
            jax.ShapeDtypeStruct((PLANE, tokens, group), F32),
            FLAGS,
            TOKEN,
        ),
        in_specs=[FLAGS_SPEC] + [WHOLE] * 3,
        out_specs=[WHOLE] * 4 + [FLAGS_SPEC, WHOLE],
        compiler_params=pltpu.CompilerParams(vmem_limit_bytes=VMEM),
        name="prep",
    )(at, write_rate.T, log_gate.T, keep_mask.T)


def block_inverses(lowers, fill):
    row = iota((HALF, CHUNK), 0)
    col = iota((HALF, CHUNK), 1) % HALF
    eye = (row == col).astype(F32)
    near = row // BLOCK == col // BLOCK
    inner = [jnp.where(near, -x, 0.0) for x in lowers]
    outer = [split(jnp.where(near, 0.0, x)) for x in lowers]
    power = [split(x) for x in inner]
    a = [eye + x for x in inner]
    for _ in range(3):
        fill()
        power = [split(pair_product(x, x)) for x in power]
        fill()
        a = [x + pair_product(split(x), y) for x, y in zip(a, power)]
    sa = [split(x) for x in a]
    fill()
    m = [split(pair_product(x, y)) for x, y in zip(sa, outer)]
    fill()
    m2 = [split(pair_product(x, x)) for x in m]
    t = [x - pair_product(y, z) for x, y, z in zip(a, m, sa)]
    return [x + pair_product(y, split(x)) for x, y in zip(t, m2)]


def maps_kernel(
    which,
    flags_ref,
    key_ref,
    value_ref,
    tail_ref,
    key_kernel_ref,
    value_kernel_ref,
    rate_ref,
    cum_ref,
    row_ref,
    token_ref,
    map_out,
    wh_out,
    wl_out,
    mh_out,
    ml_out,
    token_out,
    scratch,
    value_scratch,
):
    hand_on(token_ref, token_out)
    steps = key_ref.shape[0]
    chunks = steps // CHUNK
    at = pl.program_id(0)
    lanes = lanes_at(flags_ref, which, at, rate_ref.shape[2])
    load_rows(scratch, key_ref, lanes, tail_ref[3:6, :])
    load_rows(value_scratch, value_ref, lanes, tail_ref[6:9, :])
    shifts = shifter()
    keys = conv(shifts, scratch, key_kernel_ref, 0, steps)
    keys = jnp.concatenate([unit(keys[:, h * DK : (h + 1) * DK]) for h in range(HB)], axis=1)
    kh, kl = split(keys)
    group = rate_ref.shape[2]
    rates, cums = rate_ref[0], cum_ref[0]

    def column(x, h):
        out = x[:, h : h + 1]
        for turn in range(1, group // HB):
            out = jnp.where(at == turn, x[:, turn * HB + h : turn * HB + h + 1], out)
        return out

    below = iota((CHUNK, CHUNK), 1) < iota((CHUNK, CHUNK), 0)
    left = iota((HALF, CHUNK), 1) < HALF
    items = [(h, c) for h in range(HB) for c in range(chunks)]
    columns = [(column(rates, h), column(cums, h)) for h in range(HB)]
    lowers, crosses, sides, faded, ends = [], [], {}, {}, {}
    for h, c in items:
        lanes = slice(h * DK, (h + 1) * DK)
        rows = slice(c * CHUNK, (c + 1) * CHUNK)
        row_c = row_ref[h, c : c + 1, :]
        rate_c, cum_c = (x[rows] for x in columns[h])
        mine = (kh[rows, lanes], kl[rows, lanes])
        decay = jnp.exp(jnp.where(below, cum_c - row_c, 0.0))
        lower = jnp.where(below, rate_c * decay * mm3_nt(mine, mine), 0.0)
        lowers.append(jnp.where(left, lower[:HALF], lower[HALF:]))
        crosses.append(split(jnp.where(left, lower[HALF:], 0.0)))

    def side(c):
        rows = slice(c * CHUNK, (c + 1) * CHUNK)
        values = conv(shifts, value_scratch, value_kernel_ref, c * CHUNK, CHUNK)
        for h in range(HB):
            lanes = slice(h * DK, (h + 1) * DK)
            rate_c, cum_c = (x[rows] for x in columns[h])
            grown = rate_c * jnp.exp(cum_c) * keys[rows, lanes]
            sides[h, c] = split(jnp.concatenate([grown, rate_c * values[:, lanes]], axis=1))

    def fade(c):
        for h in range(HB):
            row_c = row_ref[h, c : c + 1, :]
            end = row_c[:, CHUNK - 1 : CHUNK]
            k_c = keys[c * CHUNK : (c + 1) * CHUNK, h * DK : (h + 1) * DK]
            faded[h, c] = split(k_c.T * jnp.exp(end - row_c))
            ends[h, c] = jnp.exp(end)

    todo = [functools.partial(f, c) for c in range(chunks) for f in (side, fade)]

    def fill():
        if todo:
            todo.pop(0)()

    eye = (iota((DK, DK), 0) == iota((DK, DK), 1)).astype(F32)
    inverses = block_inverses(lowers, fill)
    while todo:
        fill()
    pieces = [split(x) for x in inverses]
    under = [mm3(y, tuple(jnp.concatenate([z, z], axis=0) for z in x)) for x, y in zip(pieces, crosses)]
    under = [split(jnp.where(left, x, 0.0)) for x in under]
    under = [
        mm3(x, tuple(jnp.concatenate([jnp.zeros_like(z), z], axis=0) for z in y)) for x, y in zip(pieces, under)
    ]
    whole = [
        split(jnp.concatenate([jnp.where(left, x, 0.0), jnp.where(left, -y, x)], axis=0))
        for x, y in zip(inverses, under)
    ]
    solved = [split(mm3(x, sides[i])) for i, x in zip(items, whole)]
    for (h, c), x in zip(items, solved):
        at_w = slice(c * CHUNK, (c + 1) * CHUNK)
        wh_out[at * HB + h, at_w, :], wl_out[at * HB + h, at_w, :] = x
    made = [mm3(faded[i], x) for i, x in zip(items, solved)]
    made = [jnp.concatenate([ends[i] * eye - x[:, :DK], x[:, DK:]], axis=1) for i, x in zip(items, made)]

    def then(late, early):
        both = mm3(split(late[:, :DK]), early)
        return jnp.concatenate([both[:, :DK], both[:, DK:] + late[:, DK:]], axis=1)

    assert chunks == 4
    heads = range(HB)
    first, third = ([split(made[h * chunks + c]) for h in heads] for c in (0, 2))
    two = [split(then(made[h * chunks + 1], first[h])) for h in heads]
    last = [then(made[h * chunks + 3], third[h]) for h in heads]
    last = [then(last[h], two[h]) for h in heads]
    for h in heads:
        map_out[at * HB + h] = last[h]
        for i, x in enumerate((first[h], two[h], third[h])):
            at_m = slice(i * DK, (i + 1) * DK)
            mh_out[at * HB + h, at_m, :], ml_out[at * HB + h, at_m, :] = x


def group_maps(flags, token, which, key_rows, value_rows, tails, key_kernel, value_kernel, scalars):
    rate_cols, cum_cols, chunk_rows, _ = scalars
    steps, width = key_rows.shape
    heads = width // DK
    group = heads // PLANE
    turns = group // HB
    lanes = HB * DK
    chunks = steps // CHUNK

    def wide(i, g):
        return (0, g[GROUPS + which] * turns + i)

    def per_head(i, g):
        return (g[GROUPS + which] * turns + i, 0, 0)

    return pl.pallas_call(
        functools.partial(maps_kernel, which),
        grid_spec=pltpu.PrefetchScalarGridSpec(
            num_scalar_prefetch=1,
            grid=(turns,),
            in_specs=[
                WHOLE,
                WHOLE,
                pl.BlockSpec((tails.shape[0], lanes), wide),
                pl.BlockSpec((4, lanes), wide),
                pl.BlockSpec((4, lanes), wide),
                pl.BlockSpec((1, steps, group), lambda i, g: (g[GROUPS + which], 0, 0)),
                pl.BlockSpec((1, steps, group), lambda i, g: (g[GROUPS + which], 0, 0)),
                pl.BlockSpec((HB, chunks, CHUNK), per_head),
                WHOLE,
            ],
            out_specs=[
                WHOLE,
                WHOLE,
                WHOLE,
                WHOLE,
                WHOLE,
                WHOLE,
            ],
            scratch_shapes=[pltpu.VMEM((steps + 16, lanes), BF16)] * 2,
        ),
        out_shape=(
            pltpu.VMEM((group, DK, 2 * DK), F32),
            pltpu.VMEM((group, steps, 2 * DK), BF16),
            pltpu.VMEM((group, steps, 2 * DK), BF16),
            pltpu.VMEM((group, 3 * DK, 2 * DK), BF16),
            pltpu.VMEM((group, 3 * DK, 2 * DK), BF16),
            TOKEN,
        ),
        compiler_params=pltpu.CompilerParams(vmem_limit_bytes=VMEM),
        name="maps",
    )(flags, key_rows, value_rows, tails, key_kernel, value_kernel, rate_cols, cum_cols, chunk_rows, held(token))


def reads_kernel(
    which,
    flags_ref,
    query_ref,
    tail_ref,
    query_kernel_ref,
    key_ref,
    key_kernel_ref,
    read_ref,
    row_ref,
    wh_ref,
    wl_ref,
    mh_ref,
    ml_ref,
    token_ref,
    qh_out,
    ql_out,
    own_out,
    token_out,
    scratch,
    key_scratch,
):
    hand_on(token_ref, token_out)
    tokens = query_ref.shape[0]
    window = CHUNK // NH
    chunks = tokens // window
    at = pl.program_id(0)
    lanes = lanes_at(flags_ref, which, at, read_ref.shape[2])
    load_rows(scratch, query_ref, lanes, tail_ref[0:3, :])
    shifts = shifter()
    queries = conv(shifts, scratch, query_kernel_ref, 0, tokens)
    queries = jnp.concatenate([unit(queries[:, h * DK : (h + 1) * DK]) for h in range(HB)], axis=1)
    load_rows(key_scratch, key_ref, lanes, tail_ref[3:6, :])
    keys = conv(shifts, key_scratch, key_kernel_ref, 0, NH * tokens)
    group = read_ref.shape[2]
    reads = read_ref[0]
    visible = iota((window, CHUNK), 1) <= NH * iota((window, CHUNK), 0) + NH - 1
    items = [(h, c) for h in range(HB) for c in range(chunks)]
    pieces, columns, lifted = [], [], []
    for h in range(HB):
        lanes = slice(h * DK, (h + 1) * DK)
        read_h = reads[:, h : h + 1]
        for turn in range(1, group // HB):
            read_h = jnp.where(at == turn, reads[:, turn * HB + h : turn * HB + h + 1], read_h)
        columns.append(read_h)
        lifted.append(jnp.exp(read_h) * queries[:, lanes])
        pieces.append((split(queries[:, lanes]), split(unit(keys[:, lanes]))))

    def tokens_of(c):
        return slice(c * window, (c + 1) * window)

    def steps_of(c):
        return slice(c * CHUNK, (c + 1) * CHUNK)

    scores = [
        mm3_nt(tuple(x[tokens_of(c)] for x in pieces[h][0]), tuple(x[steps_of(c)] for x in pieces[h][1]))
        for h, c in items
    ]
    starts = {}
    for h in range(HB):
        kept = [tuple(x[at * HB + h, i * DK : (i + 1) * DK, :] for x in (mh_ref, ml_ref)) for i in range(3)]
        first, two, third = kept
        three = mm3(tuple(x[:, :DK] for x in third), two)
        late = third[0][:, DK:].astype(F32) + third[1][:, DK:].astype(F32)
        three = split(jnp.concatenate([three[:, :DK], three[:, DK:] + late], axis=1))
        starts[h] = [None, first, two, three]
    inner = []
    for (h, c), x in zip(items, scores):
        spread = columns[h][tokens_of(c)] - row_ref[h, c : c + 1, :]
        inner.append(split(jnp.where(visible, jnp.exp(jnp.where(visible, spread, 0.0)) * x, 0.0)))
    solved = [tuple(x[at * HB + h, steps_of(c), :] for x in (wh_ref, wl_ref)) for h, c in items]
    got = [mm3(x, y) for x, y in zip(inner, solved)]
    eff = [lifted[h][tokens_of(c)] - x[:, :DK] for (h, c), x in zip(items, got)]
    eff_pieces = [split(x) for x in eff]
    taken = [None if c == 0 else mm3(x, starts[h][c]) for (h, c), x in zip(items, eff_pieces)]
    for (h, c), x, y, z in zip(items, eff_pieces, got, taken):
        at_out = (at * HB + h, tokens_of(c))
        qh_out[at_out], ql_out[at_out] = x if c == 0 else split(z[:, :DK])
        own_out[at_out] = y[:, DK:] if c == 0 else y[:, DK:] + z[:, DK:]


def group_reads(flags, token, which, query_rows, key_rows, tails, query_kernel, key_kernel, scalars, kept):
    _, _, chunk_rows, read_cols = scalars
    tokens, width = query_rows.shape
    steps = tokens * NH
    heads = width // DK
    group = heads // PLANE
    turns = group // HB
    lanes = HB * DK
    chunks = steps // CHUNK

    def wide(i, g):
        return (0, g[GROUPS + which] * turns + i)

    return pl.pallas_call(
        functools.partial(reads_kernel, which),
        grid_spec=pltpu.PrefetchScalarGridSpec(
            num_scalar_prefetch=1,
            grid=(turns,),
            in_specs=[
                WHOLE,
                pl.BlockSpec((tails.shape[0], lanes), wide),
                pl.BlockSpec((4, lanes), wide),
                WHOLE,
                pl.BlockSpec((4, lanes), wide),
                pl.BlockSpec((1, tokens, group), lambda i, g: (g[GROUPS + which], 0, 0)),
                pl.BlockSpec((HB, chunks, CHUNK), lambda i, g: (g[GROUPS + which] * turns + i, 0, 0)),
                WHOLE,
                WHOLE,
                WHOLE,
                WHOLE,
                WHOLE,
            ],
            out_specs=[WHOLE] * 4,
            scratch_shapes=[pltpu.VMEM((tokens + 16, lanes), BF16), pltpu.VMEM((steps + 16, lanes), BF16)],
        ),
        out_shape=(
            pltpu.VMEM((group, tokens, DK), BF16),
            pltpu.VMEM((group, tokens, DK), BF16),
            pltpu.VMEM((group, tokens, DK), F32),
            TOKEN,
        ),
        compiler_params=pltpu.CompilerParams(vmem_limit_bytes=VMEM),
        name="reads",
    )(flags, query_rows, tails, query_kernel, key_rows, key_kernel, read_cols, chunk_rows, *map(held, kept), held(token))


def small(kernel, flags, token, operands, outs, name):
    def whole(shape):
        return pl.BlockSpec(shape, lambda i, f: (0,) * len(shape))

    def body(flags_ref, token_ref, *refs):
        hand_on(token_ref, refs[-1])
        kernel(flags_ref, *refs[:-1])

    return pl.pallas_call(
        body,
        grid_spec=pltpu.PrefetchScalarGridSpec(
            num_scalar_prefetch=1,
            grid=(1,),
            in_specs=[WHOLE] + [whole(x.shape) for x in operands],
            out_specs=[whole(shape) for shape in outs] + [WHOLE],
        ),
        out_shape=[jax.ShapeDtypeStruct(shape, F32) for shape in outs] + [TOKEN],
        compiler_params=SMALL,
        name=name,
    )(flags, held(token), *operands)


def after(first, mine, other):
    early = jnp.where(first, mine, other)
    late = jnp.where(first, other, mine)
    both = mm3(split(late[:, :DK]), split(early))
    return jnp.concatenate([both[:, :DK], both[:, DK:] + late[:, DK:]], axis=1)


def compose_kernel(flags_ref, mine_ref, other_ref, out_ref):
    heads = range(mine_ref.shape[0])
    for h, x in enumerate([after(flags_ref[CORE] == 0, mine_ref[h], other_ref[h]) for h in heads]):
        out_ref[h] = x


def composed(flags, token, mine, other):
    return small(compose_kernel, flags, token, [mine, other], [mine.shape], "compose")


def plane_kernel(flags_ref, mine_ref, pair_ref, other_ref, chip_out, *outs):
    parts = len(outs) // 3
    for zero_out in outs[2 * parts :]:
        zero_out[...] = jnp.zeros_like(zero_out)
    heads = range(mine_ref.shape[0])
    chips = [after(flags_ref[CORE] == 0, mine_ref[h], pair_ref[h]) for h in heads]
    planes = [after(flags_ref[CHIP] == 0, chips[h], other_ref[h]) for h in heads]
    for h in heads:
        chip_out[h] = chips[h]
        part, at = h * parts // len(heads), h % (len(heads) // parts)
        outs[part][at] = planes[h]
        outs[parts + part][at] = planes[h][:, DK:]


def plane_composed(flags, token, mine, pair, other):
    part = mine.shape[0] // PARTS
    shapes = [(part, DK, 2 * DK)] * PARTS + [(part, DK, DK)] * (2 * PARTS)
    chip_map, *outs, token = small(plane_kernel, flags, token, [mine, pair, other], [mine.shape] + shapes, "plane")
    return chip_map, outs[:PARTS], outs[PARTS : 2 * PARTS], outs[2 * PARTS :], token


def apply_kernel(flags_ref, map_ref, held_ref, come_ref, state_out, exit_out):
    heads = range(map_ref.shape[0])
    state = [held_ref[h] + come_ref[h] for h in heads]
    got = [mm3(split(map_ref[h, :, :DK]), split(state[h])) for h in heads]
    for h in heads:
        state_out[h] = state[h]
        exit_out[h] = got[h] + map_ref[h, :, DK:]


def applied(flags, token, maps, state, come):
    return small(apply_kernel, flags, token, [maps, state, come], [state.shape] * 2, "apply")


def branches(first, mine, other, entry):
    heads = range(len(entry))
    early = [jnp.where(first, mine[h], other[h]) for h in heads]
    later = [mm3(split(early[h][:, :DK]), split(entry[h])) + early[h][:, DK:] for h in heads]
    own = [jnp.where(first, entry[h], later[h]) for h in heads]
    return own, [jnp.where(first, later[h], entry[h]) for h in heads]


def branch_kernel(flags_ref, mine_ref, other_ref, entry_ref, keep_out, send_out):
    refs = (mine_ref, other_ref, entry_ref)
    own, send = branches(flags_ref[CORE] == 0, *([x[h] for h in range(x.shape[0])] for x in refs))
    for h in range(len(own)):
        keep_out[h] = own[h]
        send_out[h] = send[h]


def branched(flags, token, mine, other, entry):
    return small(branch_kernel, flags, token, [mine, other, entry], [entry.shape] * 2, "branch")


def fork_kernel(flags_ref, chip_map_ref, from_chip_ref, map_ref, pair_ref, *refs):
    maps = (chip_map_ref, from_chip_ref, map_ref, pair_ref)
    chip_map, from_chip, mine, pair = ([x[h] for h in range(x.shape[0])] for x in maps)
    states, outs = refs[: 2 * PARTS], refs[2 * PARTS :]
    state, come = ([x[h] for x in part for h in range(x.shape[0])] for part in (states[:PARTS], states[PARTS:]))
    entry = [x + y for x, y in zip(state, come)]
    own, across = branches(flags_ref[CHIP] == 0, chip_map, from_chip, entry)
    for out_ref, states in zip(outs, (across, *branches(flags_ref[CORE] == 0, mine, pair, own))):
        for h, state in enumerate(states):
            out_ref[h] = state


def forked(flags, token, chip_map, from_chip, mine, pair, state, come):
    operands = [chip_map, from_chip, mine, pair, *state, *come]
    return small(fork_kernel, flags, token, operands, [(mine.shape[0], DK, DK)] * 3, "fork")


def finish_kernel(flags_ref, token_ref, qh_ref, ql_ref, own_ref, entry_ref, *refs):
    out_ref, token_out = refs[-2:]
    hand_on(token_ref, token_out)
    for h in range(entry_ref.shape[0]):
        lanes = slice(h * DK, (h + 1) * DK)
        got = mm3((qh_ref[h], ql_ref[h]), split(entry_ref[h]))
        out_ref[:, lanes] = (own_ref[h] + got).astype(BF16)


def finished(flags, token, which, read, entry, out, width):
    qh, ql, own, _ = read
    group, tokens, _ = qh.shape
    operands = [held(token), held(qh), held(ql), held(own), entry]
    specs = [WHOLE] * 4 + [pl.BlockSpec(entry.shape, lambda i, g: (0, 0, 0))]
    if out is not None:
        operands.append(out)
        specs.append(pl.BlockSpec(memory_space=pl.ANY))
    return pl.pallas_call(
        finish_kernel,
        grid_spec=pltpu.PrefetchScalarGridSpec(
            num_scalar_prefetch=1,
            grid=(1,),
            in_specs=specs,
            out_specs=[pl.BlockSpec((tokens, group * DK), lambda i, g: (0, g[GROUPS + which])), WHOLE],
        ),
        out_shape=[jax.ShapeDtypeStruct((tokens, width), BF16), TOKEN],
        input_output_aliases={} if out is None else {len(operands): 0},
        compiler_params=SMALL,
        name="finish",
    )(flags, *operands)


def moved(x, pairs):
    return pltpu.with_memory_space_constraint(lax.ppermute(x, "seq", pairs), pltpu.VMEM)


def local(
    count,
    query_rows,
    key_rows,
    value_rows,
    write_rate,
    log_gate,
    keep_mask,
    query_kernel,
    key_kernel,
    value_kernel,
):
    tails = moved(last_rows(query_rows, key_rows, value_rows), [(s, s + 1) for s in range(count - 1)])
    query_rows, key_rows, value_rows = held(query_rows), held(key_rows), held(value_rows)
    query_kernel, key_kernel, value_kernel = held(query_kernel), held(key_kernel), held(value_kernel)
    *scalars, flags, token = prep(lax.axis_index("seq")[None], write_rate, log_gate, keep_mask)
    pair = [(s, s ^ 1) for s in range(count)]
    across = [(s, s ^ 2) for s in range(count)]
    made, from_pair = {}, {}
    for i in (0, 2, 1, 3):
        *one, token = group_maps(flags, token, i, key_rows, value_rows, tails, key_kernel, value_kernel, scalars)
        made[i] = one
        if i < 2:
            from_pair[i] = moved(one[0], pair)
        if i == 2:
            next_map, token = composed(flags, token, one[0], from_pair[0])
            from_chip = moved(next_map, across)
    maps = [made[i][0] for i in range(PLANE)]
    chip_map, plane_maps, offset, state, token = plane_composed(flags, token, maps[3], from_pair[1], from_chip)

    def read(token, i):
        return group_reads(
            flags, token, i, query_rows, key_rows, tails, query_kernel, key_kernel, scalars, made[i][1:]
        )

    reads = []
    for i in range(count // PLANE - 1):
        if i > 0:
            offset = []
            for part in range(PARTS):
                state[part], part_offset, token = applied(flags, token, plane_maps[part], state[part], come[part])
                offset.append(part_offset)
        come = [moved(x, [(s, s + PLANE) for s in range(i * PLANE, (i + 1) * PLANE)]) for x in offset]
        if len(reads) < PLANE - 1:
            reads.append(read(token, i))
            token = reads[-1][-1]
    send, own_entry, own_send, token = forked(flags, token, chip_map, from_chip, maps[3], from_pair[1], state, come)
    theirs = moved(send, across)
    far_own = moved(own_send, pair)
    for i in range(len(reads), PLANE):
        reads.append(read(token, i))
        token = reads[-1][-1]
    width = query_rows.shape[1]
    out, token = finished(flags, token, 3, reads[3], own_entry, None, width)
    out, token = finished(flags, token, 1, reads[1], far_own, out, width)
    next_entry, next_send, token = branched(flags, token, maps[2], from_pair[0], theirs)
    far_next = moved(next_send, pair)
    out, token = finished(flags, token, 2, reads[2], next_entry, out, width)
    return finished(flags, token, 0, reads[0], far_next, out, width)[0]


def solution(mesh):
    rows = P(("groups", "seq"), None)
    return jax.shard_map(
        functools.partial(local, mesh.shape["seq"]),
        mesh=mesh,
        in_specs=(rows, rows, rows, rows, rows, rows, P(), P(), P()),
        out_specs=rows,
        check_vma=False,
    )
```

```python
import functools

import jax
import jax.numpy as jnp
from jax import lax
from jax.experimental import pallas as pl
from jax.experimental.pallas import tpu as pltpu
from jax.sharding import PartitionSpec as P

NH = 2
BLOCK = 16
SPAN = 64
DK = 128
CHUNK = 128
HALF = 64
PLANE = 4
PARTS = 2
HB = 4
VMEM = 28 << 20
SMALL = pltpu.CompilerParams(vmem_limit_bytes=8 << 20)

WHOLE = pl.BlockSpec(memory_space=pltpu.VMEM)

F32 = jnp.float32
BF16 = jnp.bfloat16
NN = (((1,), (0,)), ((), ()))
NT = (((1,), (1,)), ((), ()))


def split(x):
    high = x.astype(BF16)
    low = (x - high.astype(F32)).astype(BF16)
    return high, low


def mm(a, b, dims=NN):
    return lax.dot_general(a, b, dims, preferred_element_type=F32)


def mm3(a, b):
    ah, al = a
    bh, bl = b
    return mm(jnp.concatenate([ah, al], axis=1), jnp.concatenate([bh, bh], axis=0)) + mm(ah, bl)


def mm3_nt(a, b):
    ah, al = a
    bh, bl = b
    return mm(jnp.concatenate([ah, al], axis=1), jnp.concatenate([bh, bh], axis=1), NT) + mm(ah, bl, NT)


def halves(x):
    left = iota(x.shape, 1) < HALF
    zero = jnp.zeros_like(x)
    return jnp.concatenate([jnp.where(left, x, zero), jnp.where(left, zero, x)], axis=0)


def pair_product(x, y):
    return mm3(x, (halves(y[0]), halves(y[1])))


def silu(v):
    return v / (1.0 + jnp.exp(-v))


def load_rows(scratch, rows_ref, lanes, tail):
    before = jnp.concatenate([jnp.zeros((13, tail.shape[1]), F32), tail.astype(F32)], axis=0)
    scratch[0:16, :] = before.astype(BF16)
    scratch[16 : 16 + rows_ref.shape[0], :] = rows_ref[:, lanes]


def shifter():
    shape = (3 * HALF, HALF + 16)
    row, col = iota(shape, 0), iota(shape, 1)
    return (col == 15 + row % HALF - row // HALF).astype(F32).astype(BF16)


def conv(shifts, scratch, kernel_ref, start, count):
    parts = []
    for at in range(start, start + count, HALF):
        moved = mm(shifts, scratch[at : at + HALF + 16, :])
        total = kernel_ref[3:4, :] * scratch[at + 16 : at + 16 + HALF, :].astype(F32)
        for back in range(1, 4):
            total = total + kernel_ref[3 - back : 4 - back, :] * moved[(back - 1) * HALF : back * HALF]
        parts.append(silu(total))
    return jnp.concatenate(parts, axis=0)


def unit(x):
    return x * lax.rsqrt(jnp.sum(x * x, axis=-1, keepdims=True) + 1e-06)


CORE, CHIP, GROUPS = 0, 1, 2
FLAGS = jax.ShapeDtypeStruct((8,), jnp.int32)
FLAGS_SPEC = pl.BlockSpec(memory_space=pltpu.SMEM)
TOKEN = pltpu.VMEM((8, 128), jnp.int32)


def hand_on(token_ref, token_out):
    token_out[...] = token_ref[...]


def lanes_at(flags_ref, which, at, group):
    first = flags_ref[GROUPS + which] * group + at * HB
    return pl.ds(pl.multiple_of(first * DK, HB * DK), HB * DK)


def in_hbm(x):
    return pltpu.with_memory_space_constraint(x, pltpu.HBM)


def held(x):
    return pltpu.with_memory_space_constraint(x, pltpu.VMEM)


def iota(shape, dim):
    return lax.broadcasted_iota(jnp.int32, shape, dim)


def prep_kernel(at_ref, rate_ref, log_ref, mask_ref, *refs):
    rows, outs, sems = refs[:3], refs[3:-1], refs[-1]
    rate_out, cum_out, row_out, read_out, flags_out, token_out = outs[:6]
    loads = [pltpu.make_async_copy(x, y, sems.at[i]) for i, (x, y) in enumerate(zip(rows, outs[6:]))]
    for load in loads:
        load.start()
    token_out[...] = jnp.zeros_like(token_out)
    place = lax.rem(at_ref[0], PLANE)
    flags_out[CORE] = lax.rem(place, 2)
    flags_out[CHIP] = lax.div(place, 2)
    for i, other in enumerate((3, 1, 2, 0)):
        flags_out[GROUPS + i] = place ^ other
    for i in range(GROUPS + PLANE, FLAGS.shape[0]):
        flags_out[i] = 0
    heads, steps = rate_ref.shape
    tokens = log_ref.shape[1]
    group = heads // PLANE
    subs, blocks = mask_ref.shape
    row_of = (iota((steps, blocks), 0) // SPAN == iota((steps, blocks), 1)).astype(F32)
    picked = mm(row_of, mask_ref[...].astype(F32), NT)
    sub_of = ((iota((steps, subs), 0) % SPAN) // BLOCK == iota((steps, subs), 1)).astype(F32)
    keep = jnp.sum(picked * sub_of, axis=1, keepdims=True)
    rates = rate_ref[...].T * keep
    turned = log_ref[...]
    logs = turned.T
    window = CHUNK // NH

    def upto(token, last):
        return ((token // window == last // window) & (token <= last)).astype(F32)

    high = lax.Precision.HIGHEST
    cum = jnp.dot(
        upto(iota((steps, tokens), 1), iota((steps, tokens), 0) // NH), logs, precision=high, preferred_element_type=F32
    )
    read = jnp.dot(
        upto(iota((tokens, tokens), 1), iota((tokens, tokens), 0)), logs, precision=high, preferred_element_type=F32
    )
    row = jnp.dot(
        turned,
        upto(iota((tokens, steps), 0), iota((tokens, steps), 1) // NH),
        precision=high,
        preferred_element_type=F32,
    )
    for g in range(PLANE):
        rate_out[g] = rates[:, g * group : (g + 1) * group]
        cum_out[g] = cum[:, g * group : (g + 1) * group]
        read_out[g] = read[:, g * group : (g + 1) * group]
    for b in range(steps // CHUNK):
        row_out[:, b, :] = row[:, b * CHUNK : (b + 1) * CHUNK]
    for load in loads:
        load.wait()


def last_rows_kernel(query_ref, key_ref, value_ref, out_ref):
    for i, ref in enumerate((query_ref, key_ref, value_ref)):
        out_ref[3 * i : 3 * i + 3, :] = ref[...].astype(F32)[13:16].astype(BF16)


def last_rows(*arrays):
    width = arrays[0].shape[1]
    return pl.pallas_call(
        last_rows_kernel,
        grid=(1,),
        in_specs=[pl.BlockSpec((16, width), functools.partial(lambda at, i: (at, 0), x.shape[0] // 16 - 1)) for x in arrays],
        out_specs=pl.BlockSpec((9, width), lambda i: (0, 0)),
        out_shape=jax.ShapeDtypeStruct((9, width), BF16),
        compiler_params=SMALL,
        name="last_rows",
    )(*map(in_hbm, arrays))


def prep(at, write_rate, log_gate, keep_mask, *rows):
    steps, heads = write_rate.shape
    tokens = log_gate.shape[0]
    group = heads // PLANE
    return pl.pallas_call(
        prep_kernel,
        out_shape=(
            jax.ShapeDtypeStruct((PLANE, steps, group), F32),
            jax.ShapeDtypeStruct((PLANE, steps, group), F32),
            jax.ShapeDtypeStruct((heads, steps // CHUNK, CHUNK), F32),
            jax.ShapeDtypeStruct((PLANE, tokens, group), F32),
            FLAGS,
            TOKEN,
            *(pltpu.VMEM(x.shape, x.dtype) for x in rows),
        ),
        in_specs=[FLAGS_SPEC] + [WHOLE] * 3 + [pl.BlockSpec(memory_space=pltpu.HBM)] * 3,
        out_specs=[WHOLE] * 4 + [FLAGS_SPEC] + [WHOLE] * 4,
        scratch_shapes=[pltpu.SemaphoreType.DMA((3,))],
        compiler_params=pltpu.CompilerParams(vmem_limit_bytes=VMEM),
        name="prep",
    )(at, write_rate.T, log_gate.T, keep_mask.T, *(pltpu.with_memory_space_constraint(x, pltpu.HBM) for x in rows))


def block_inverses(lowers, fill):
    row = iota((HALF, CHUNK), 0)
    col = iota((HALF, CHUNK), 1) % HALF
    eye = (row == col).astype(F32)
    near = row // BLOCK == col // BLOCK
    inner = [jnp.where(near, -x, 0.0) for x in lowers]
    outer = [split(jnp.where(near, 0.0, x)) for x in lowers]
    power = [split(x) for x in inner]
    a = [eye + x for x in inner]
    for _ in range(3):
        fill()
        power = [split(pair_product(x, x)) for x in power]
        fill()
        a = [x + pair_product(split(x), y) for x, y in zip(a, power)]
    sa = [split(x) for x in a]
    fill()
    m = [split(pair_product(x, y)) for x, y in zip(sa, outer)]
    fill()
    m2 = [split(pair_product(x, x)) for x in m]
    t = [x - pair_product(y, z) for x, y, z in zip(a, m, sa)]
    return [x + pair_product(y, split(x)) for x, y in zip(t, m2)]


def maps_kernel(
    which,
    flags_ref,
    key_ref,
    value_ref,
    tail_ref,
    key_kernel_ref,
    value_kernel_ref,
    rate_ref,
    cum_ref,
    row_ref,
    token_ref,
    map_out,
    wh_out,
    wl_out,
    mh_out,
    ml_out,
    token_out,
    scratch,
    value_scratch,
):
    hand_on(token_ref, token_out)
    steps = key_ref.shape[0]
    chunks = steps // CHUNK
    at = pl.program_id(0)
    lanes = lanes_at(flags_ref, which, at, rate_ref.shape[2])
    load_rows(scratch, key_ref, lanes, tail_ref[3:6, :])
    load_rows(value_scratch, value_ref, lanes, tail_ref[6:9, :])
    shifts = shifter()
    keys = conv(shifts, scratch, key_kernel_ref, 0, steps)
    keys = jnp.concatenate([unit(keys[:, h * DK : (h + 1) * DK]) for h in range(HB)], axis=1)
    kh, kl = split(keys)
    group = rate_ref.shape[2]
    rates, cums = rate_ref[0], cum_ref[0]

    def column(x, h):
        out = x[:, h : h + 1]
        for turn in range(1, group // HB):
            out = jnp.where(at == turn, x[:, turn * HB + h : turn * HB + h + 1], out)
        return out

    below = iota((CHUNK, CHUNK), 1) < iota((CHUNK, CHUNK), 0)
    left = iota((HALF, CHUNK), 1) < HALF
    items = [(h, c) for h in range(HB) for c in range(chunks)]
    columns = [(column(rates, h), column(cums, h)) for h in range(HB)]
    lowers, crosses, sides, faded, ends = [], [], {}, {}, {}
    for h, c in items:
        lanes = slice(h * DK, (h + 1) * DK)
        rows = slice(c * CHUNK, (c + 1) * CHUNK)
        row_c = row_ref[h, c : c + 1, :]
        rate_c, cum_c = (x[rows] for x in columns[h])
        mine = (kh[rows, lanes], kl[rows, lanes])
        decay = jnp.exp(jnp.where(below, cum_c - row_c, 0.0))
        lower = jnp.where(below, rate_c * decay * mm3_nt(mine, mine), 0.0)
        lowers.append(jnp.where(left, lower[:HALF], lower[HALF:]))
        crosses.append(split(jnp.where(left, lower[HALF:], 0.0)))

    def side(c):
        rows = slice(c * CHUNK, (c + 1) * CHUNK)
        values = conv(shifts, value_scratch, value_kernel_ref, c * CHUNK, CHUNK)
        for h in range(HB):
            lanes = slice(h * DK, (h + 1) * DK)
            rate_c, cum_c = (x[rows] for x in columns[h])
            grown = rate_c * jnp.exp(cum_c) * keys[rows, lanes]
            sides[h, c] = split(jnp.concatenate([grown, rate_c * values[:, lanes]], axis=1))

    def fade(c):
        for h in range(HB):
            row_c = row_ref[h, c : c + 1, :]
            end = row_c[:, CHUNK - 1 : CHUNK]
            k_c = keys[c * CHUNK : (c + 1) * CHUNK, h * DK : (h + 1) * DK]
            faded[h, c] = split(k_c.T * jnp.exp(end - row_c))
            ends[h, c] = jnp.exp(end)

    todo = [functools.partial(f, c) for c in range(chunks) for f in (side, fade)]

    def fill():
        if todo:
            todo.pop(0)()

    eye = (iota((DK, DK), 0) == iota((DK, DK), 1)).astype(F32)
    inverses = block_inverses(lowers, fill)
    while todo:
        fill()
    pieces = [split(x) for x in inverses]
    under = [mm3(y, tuple(jnp.concatenate([z, z], axis=0) for z in x)) for x, y in zip(pieces, crosses)]
    under = [split(jnp.where(left, x, 0.0)) for x in under]
    under = [
        mm3(x, tuple(jnp.concatenate([jnp.zeros_like(z), z], axis=0) for z in y)) for x, y in zip(pieces, under)
    ]
    whole = [
        split(jnp.concatenate([jnp.where(left, x, 0.0), jnp.where(left, -y, x)], axis=0))
        for x, y in zip(inverses, under)
    ]
    solved = [split(mm3(x, sides[i])) for i, x in zip(items, whole)]
    for (h, c), x in zip(items, solved):
        at_w = slice(c * CHUNK, (c + 1) * CHUNK)
        wh_out[at * HB + h, at_w, :], wl_out[at * HB + h, at_w, :] = x
    made = [mm3(faded[i], x) for i, x in zip(items, solved)]
    made = [jnp.concatenate([ends[i] * eye - x[:, :DK], x[:, DK:]], axis=1) for i, x in zip(items, made)]

    def then(late, early):
        both = mm3(split(late[:, :DK]), early)
        return jnp.concatenate([both[:, :DK], both[:, DK:] + late[:, DK:]], axis=1)

    assert chunks == 4
    heads = range(HB)
    first, third = ([split(made[h * chunks + c]) for h in heads] for c in (0, 2))
    two = [split(then(made[h * chunks + 1], first[h])) for h in heads]
    last = [then(made[h * chunks + 3], third[h]) for h in heads]
    last = [then(last[h], two[h]) for h in heads]
    for h in heads:
        map_out[at * HB + h] = last[h]
        for i, x in enumerate((first[h], two[h], third[h])):
            at_m = slice(i * DK, (i + 1) * DK)
            mh_out[at * HB + h, at_m, :], ml_out[at * HB + h, at_m, :] = x


def group_maps(flags, token, which, key_rows, value_rows, tails, key_kernel, value_kernel, scalars):
    rate_cols, cum_cols, chunk_rows, _ = scalars
    steps, width = key_rows.shape
    heads = width // DK
    group = heads // PLANE
    turns = group // HB
    lanes = HB * DK
    chunks = steps // CHUNK

    def wide(i, g):
        return (0, g[GROUPS + which] * turns + i)

    def per_head(i, g):
        return (g[GROUPS + which] * turns + i, 0, 0)

    return pl.pallas_call(
        functools.partial(maps_kernel, which),
        grid_spec=pltpu.PrefetchScalarGridSpec(
            num_scalar_prefetch=1,
            grid=(turns,),
            in_specs=[
                WHOLE,
                WHOLE,
                pl.BlockSpec((tails.shape[0], lanes), wide),
                pl.BlockSpec((4, lanes), wide),
                pl.BlockSpec((4, lanes), wide),
                pl.BlockSpec((1, steps, group), lambda i, g: (g[GROUPS + which], 0, 0)),
                pl.BlockSpec((1, steps, group), lambda i, g: (g[GROUPS + which], 0, 0)),
                pl.BlockSpec((HB, chunks, CHUNK), per_head),
                WHOLE,
            ],
            out_specs=[
                WHOLE,
                WHOLE,
                WHOLE,
                WHOLE,
                WHOLE,
                WHOLE,
            ],
            scratch_shapes=[pltpu.VMEM((steps + 16, lanes), BF16)] * 2,
        ),
        out_shape=(
            pltpu.VMEM((group, DK, 2 * DK), F32),
            pltpu.VMEM((group, steps, 2 * DK), BF16),
            pltpu.VMEM((group, steps, 2 * DK), BF16),
            pltpu.VMEM((group, 3 * DK, 2 * DK), BF16),
            pltpu.VMEM((group, 3 * DK, 2 * DK), BF16),
            TOKEN,
        ),
        compiler_params=pltpu.CompilerParams(vmem_limit_bytes=VMEM),
        name="maps",
    )(flags, key_rows, value_rows, tails, key_kernel, value_kernel, rate_cols, cum_cols, chunk_rows, held(token))


def reads_kernel(
    which,
    flags_ref,
    query_ref,
    tail_ref,
    query_kernel_ref,
    key_ref,
    key_kernel_ref,
    read_ref,
    row_ref,
    wh_ref,
    wl_ref,
    mh_ref,
    ml_ref,
    token_ref,
    qh_out,
    ql_out,
    own_out,
    token_out,
    scratch,
    key_scratch,
):
    hand_on(token_ref, token_out)
    tokens = query_ref.shape[0]
    window = CHUNK // NH
    chunks = tokens // window
    at = pl.program_id(0)
    lanes = lanes_at(flags_ref, which, at, read_ref.shape[2])
    load_rows(scratch, query_ref, lanes, tail_ref[0:3, :])
    shifts = shifter()
    queries = conv(shifts, scratch, query_kernel_ref, 0, tokens)
    queries = jnp.concatenate([unit(queries[:, h * DK : (h + 1) * DK]) for h in range(HB)], axis=1)
    load_rows(key_scratch, key_ref, lanes, tail_ref[3:6, :])
    keys = conv(shifts, key_scratch, key_kernel_ref, 0, NH * tokens)
    group = read_ref.shape[2]
    reads = read_ref[0]
    visible = iota((window, CHUNK), 1) <= NH * iota((window, CHUNK), 0) + NH - 1
    items = [(h, c) for h in range(HB) for c in range(chunks)]
    pieces, columns, lifted = [], [], []
    for h in range(HB):
        lanes = slice(h * DK, (h + 1) * DK)
        read_h = reads[:, h : h + 1]
        for turn in range(1, group // HB):
            read_h = jnp.where(at == turn, reads[:, turn * HB + h : turn * HB + h + 1], read_h)
        columns.append(read_h)
        lifted.append(jnp.exp(read_h) * queries[:, lanes])
        pieces.append((split(queries[:, lanes]), split(unit(keys[:, lanes]))))

    def tokens_of(c):
        return slice(c * window, (c + 1) * window)

    def steps_of(c):
        return slice(c * CHUNK, (c + 1) * CHUNK)

    scores = [
        mm3_nt(tuple(x[tokens_of(c)] for x in pieces[h][0]), tuple(x[steps_of(c)] for x in pieces[h][1]))
        for h, c in items
    ]
    starts = {}
    for h in range(HB):
        kept = [tuple(x[at * HB + h, i * DK : (i + 1) * DK, :] for x in (mh_ref, ml_ref)) for i in range(3)]
        first, two, third = kept
        three = mm3(tuple(x[:, :DK] for x in third), two)
        late = third[0][:, DK:].astype(F32) + third[1][:, DK:].astype(F32)
        three = split(jnp.concatenate([three[:, :DK], three[:, DK:] + late], axis=1))
        starts[h] = [None, first, two, three]
    inner = []
    for (h, c), x in zip(items, scores):
        spread = columns[h][tokens_of(c)] - row_ref[h, c : c + 1, :]
        inner.append(split(jnp.where(visible, jnp.exp(jnp.where(visible, spread, 0.0)) * x, 0.0)))
    solved = [tuple(x[at * HB + h, steps_of(c), :] for x in (wh_ref, wl_ref)) for h, c in items]
    got = [mm3(x, y) for x, y in zip(inner, solved)]
    eff = [lifted[h][tokens_of(c)] - x[:, :DK] for (h, c), x in zip(items, got)]
    eff_pieces = [split(x) for x in eff]
    taken = [None if c == 0 else mm3(x, starts[h][c]) for (h, c), x in zip(items, eff_pieces)]
    for (h, c), x, y, z in zip(items, eff_pieces, got, taken):
        at_out = (at * HB + h, tokens_of(c))
        qh_out[at_out], ql_out[at_out] = x if c == 0 else split(z[:, :DK])
        own_out[at_out] = y[:, DK:] if c == 0 else y[:, DK:] + z[:, DK:]


def group_reads(flags, token, which, query_rows, key_rows, tails, query_kernel, key_kernel, scalars, kept):
    _, _, chunk_rows, read_cols = scalars
    tokens, width = query_rows.shape
    steps = tokens * NH
    heads = width // DK
    group = heads // PLANE
    turns = group // HB
    lanes = HB * DK
    chunks = steps // CHUNK

    def wide(i, g):
        return (0, g[GROUPS + which] * turns + i)

    return pl.pallas_call(
        functools.partial(reads_kernel, which),
        grid_spec=pltpu.PrefetchScalarGridSpec(
            num_scalar_prefetch=1,
            grid=(turns,),
            in_specs=[
                WHOLE,
                pl.BlockSpec((tails.shape[0], lanes), wide),
                pl.BlockSpec((4, lanes), wide),
                WHOLE,
                pl.BlockSpec((4, lanes), wide),
                pl.BlockSpec((1, tokens, group), lambda i, g: (g[GROUPS + which], 0, 0)),
                pl.BlockSpec((HB, chunks, CHUNK), lambda i, g: (g[GROUPS + which] * turns + i, 0, 0)),
                WHOLE,
                WHOLE,
                WHOLE,
                WHOLE,
                WHOLE,
            ],
            out_specs=[WHOLE] * 4,
            scratch_shapes=[pltpu.VMEM((tokens + 16, lanes), BF16), pltpu.VMEM((steps + 16, lanes), BF16)],
        ),
        out_shape=(
            pltpu.VMEM((group, tokens, DK), BF16),
            pltpu.VMEM((group, tokens, DK), BF16),
            pltpu.VMEM((group, tokens, DK), F32),
            TOKEN,
        ),
        compiler_params=pltpu.CompilerParams(vmem_limit_bytes=VMEM),
        name="reads",
    )(flags, query_rows, tails, query_kernel, key_rows, key_kernel, read_cols, chunk_rows, *map(held, kept), held(token))


def small(kernel, flags, token, operands, outs, name):
    def whole(shape):
        return pl.BlockSpec(shape, lambda i, f: (0,) * len(shape))

    def body(flags_ref, token_ref, *refs):
        hand_on(token_ref, refs[-1])
        kernel(flags_ref, *refs[:-1])

    return pl.pallas_call(
        body,
        grid_spec=pltpu.PrefetchScalarGridSpec(
            num_scalar_prefetch=1,
            grid=(1,),
            in_specs=[WHOLE] + [whole(x.shape) for x in operands],
            out_specs=[whole(shape) for shape in outs] + [WHOLE],
        ),
        out_shape=[jax.ShapeDtypeStruct(shape, F32) for shape in outs] + [TOKEN],
        compiler_params=SMALL,
        name=name,
    )(flags, held(token), *operands)


def after(first, mine, other):
    early = jnp.where(first, mine, other)
    late = jnp.where(first, other, mine)
    both = mm3(split(late[:, :DK]), split(early))
    return jnp.concatenate([both[:, :DK], both[:, DK:] + late[:, DK:]], axis=1)


def compose_kernel(flags_ref, mine_ref, other_ref, out_ref):
    heads = range(mine_ref.shape[0])
    for h, x in enumerate([after(flags_ref[CORE] == 0, mine_ref[h], other_ref[h]) for h in heads]):
        out_ref[h] = x


def composed(flags, token, mine, other):
    return small(compose_kernel, flags, token, [mine, other], [mine.shape], "compose")


def plane_kernel(flags_ref, mine_ref, pair_ref, other_ref, chip_out, *outs):
    parts = len(outs) // 3
    for zero_out in outs[2 * parts :]:
        zero_out[...] = jnp.zeros_like(zero_out)
    heads = range(mine_ref.shape[0])
    chips = [after(flags_ref[CORE] == 0, mine_ref[h], pair_ref[h]) for h in heads]
    planes = [after(flags_ref[CHIP] == 0, chips[h], other_ref[h]) for h in heads]
    for h in heads:
        chip_out[h] = chips[h]
        part, at = h * parts // len(heads), h % (len(heads) // parts)
        outs[part][at] = planes[h]
        outs[parts + part][at] = planes[h][:, DK:]


def plane_composed(flags, token, mine, pair, other):
    part = mine.shape[0] // PARTS
    shapes = [(part, DK, 2 * DK)] * PARTS + [(part, DK, DK)] * (2 * PARTS)
    chip_map, *outs, token = small(plane_kernel, flags, token, [mine, pair, other], [mine.shape] + shapes, "plane")
    return chip_map, outs[:PARTS], outs[PARTS : 2 * PARTS], outs[2 * PARTS :], token


def apply_kernel(flags_ref, map_ref, held_ref, come_ref, state_out, exit_out):
    heads = range(map_ref.shape[0])
    state = [held_ref[h] + come_ref[h] for h in heads]
    got = [mm3(split(map_ref[h, :, :DK]), split(state[h])) for h in heads]
    for h in heads:
        state_out[h] = state[h]
        exit_out[h] = got[h] + map_ref[h, :, DK:]


def applied(flags, token, maps, state, come):
    return small(apply_kernel, flags, token, [maps, state, come], [state.shape] * 2, "apply")


def branches(first, mine, other, entry):
    heads = range(len(entry))
    early = [jnp.where(first, mine[h], other[h]) for h in heads]
    later = [mm3(split(early[h][:, :DK]), split(entry[h])) + early[h][:, DK:] for h in heads]
    own = [jnp.where(first, entry[h], later[h]) for h in heads]
    return own, [jnp.where(first, later[h], entry[h]) for h in heads]


def branch_kernel(flags_ref, mine_ref, other_ref, entry_ref, keep_out, send_out):
    refs = (mine_ref, other_ref, entry_ref)
    own, send = branches(flags_ref[CORE] == 0, *([x[h] for h in range(x.shape[0])] for x in refs))
    for h in range(len(own)):
        keep_out[h] = own[h]
        send_out[h] = send[h]


def branched(flags, token, mine, other, entry):
    return small(branch_kernel, flags, token, [mine, other, entry], [entry.shape] * 2, "branch")


def fork_kernel(flags_ref, chip_map_ref, from_chip_ref, map_ref, pair_ref, *refs):
    maps = (chip_map_ref, from_chip_ref, map_ref, pair_ref)
    chip_map, from_chip, mine, pair = ([x[h] for h in range(x.shape[0])] for x in maps)
    states, outs = refs[: 2 * PARTS], refs[2 * PARTS :]
    state, come = ([x[h] for x in part for h in range(x.shape[0])] for part in (states[:PARTS], states[PARTS:]))
    entry = [x + y for x, y in zip(state, come)]
    own, across = branches(flags_ref[CHIP] == 0, chip_map, from_chip, entry)
    for out_ref, states in zip(outs, (across, *branches(flags_ref[CORE] == 0, mine, pair, own))):
        for h, state in enumerate(states):
            out_ref[h] = state


def forked(flags, token, chip_map, from_chip, mine, pair, state, come):
    operands = [chip_map, from_chip, mine, pair, *state, *come]
    return small(fork_kernel, flags, token, operands, [(mine.shape[0], DK, DK)] * 3, "fork")


def finish_kernel(flags_ref, token_ref, qh_ref, ql_ref, own_ref, entry_ref, *refs):
    out_ref, token_out = refs[-2:]
    hand_on(token_ref, token_out)
    for h in range(entry_ref.shape[0]):
        lanes = slice(h * DK, (h + 1) * DK)
        got = mm3((qh_ref[h], ql_ref[h]), split(entry_ref[h]))
        out_ref[:, lanes] = (own_ref[h] + got).astype(BF16)


def finished(flags, token, which, read, entry, out, width):
    qh, ql, own, _ = read
    group, tokens, _ = qh.shape
    operands = [held(token), held(qh), held(ql), held(own), entry]
    specs = [WHOLE] * 4 + [pl.BlockSpec(entry.shape, lambda i, g: (0, 0, 0))]
    if out is not None:
        operands.append(out)
        specs.append(pl.BlockSpec(memory_space=pl.ANY))
    return pl.pallas_call(
        finish_kernel,
        grid_spec=pltpu.PrefetchScalarGridSpec(
            num_scalar_prefetch=1,
            grid=(1,),
            in_specs=specs,
            out_specs=[pl.BlockSpec((tokens, group * DK), lambda i, g: (0, g[GROUPS + which])), WHOLE],
        ),
        out_shape=[jax.ShapeDtypeStruct((tokens, width), BF16), TOKEN],
        input_output_aliases={} if out is None else {len(operands): 0},
        compiler_params=SMALL,
        name="finish",
    )(flags, *operands)


def moved(x, pairs):
    return pltpu.with_memory_space_constraint(lax.ppermute(x, "seq", pairs), pltpu.VMEM)


def local(
    count,
    query_rows,
    key_rows,
    value_rows,
    write_rate,
    log_gate,
    keep_mask,
    query_kernel,
    key_kernel,
    value_kernel,
):
    tails = moved(last_rows(query_rows, key_rows, value_rows), [(s, s + 1) for s in range(count - 1)])
    query_kernel, key_kernel, value_kernel = held(query_kernel), held(key_kernel), held(value_kernel)
    *scalars, flags, token, query_rows, key_rows, value_rows = prep(
        lax.axis_index("seq")[None], write_rate, log_gate, keep_mask, query_rows, key_rows, value_rows
    )
    query_rows, key_rows, value_rows = held(query_rows), held(key_rows), held(value_rows)
    pair = [(s, s ^ 1) for s in range(count)]
    across = [(s, s ^ 2) for s in range(count)]
    made, from_pair = {}, {}
    for i in (0, 2, 1, 3):
        *one, token = group_maps(flags, token, i, key_rows, value_rows, tails, key_kernel, value_kernel, scalars)
        made[i] = one
        if i < 2:
            from_pair[i] = moved(one[0], pair)
        if i == 2:
            next_map, token = composed(flags, token, one[0], from_pair[0])
            from_chip = moved(next_map, across)
    maps = [made[i][0] for i in range(PLANE)]
    chip_map, plane_maps, offset, state, token = plane_composed(flags, token, maps[3], from_pair[1], from_chip)

    def read(token, i):
        return group_reads(
            flags, token, i, query_rows, key_rows, tails, query_kernel, key_kernel, scalars, made[i][1:]
        )

    reads = []
    for i in range(count // PLANE - 1):
        if i > 0:
            offset = []
            for part in range(PARTS):
                state[part], part_offset, token = applied(flags, token, plane_maps[part], state[part], come[part])
                offset.append(part_offset)
        come = [moved(x, [(s, s + PLANE) for s in range(i * PLANE, (i + 1) * PLANE)]) for x in offset]
        if len(reads) < PLANE - 1:
            reads.append(read(token, i))
            token = reads[-1][-1]
    send, own_entry, own_send, token = forked(flags, token, chip_map, from_chip, maps[3], from_pair[1], state, come)
    theirs = moved(send, across)
    far_own = moved(own_send, pair)
    for i in range(len(reads), PLANE):
        reads.append(read(token, i))
        token = reads[-1][-1]
    width = query_rows.shape[1]
    out, token = finished(flags, token, 3, reads[3], own_entry, None, width)
    out, token = finished(flags, token, 1, reads[1], far_own, out, width)
    next_entry, next_send, token = branched(flags, token, maps[2], from_pair[0], theirs)
    far_next = moved(next_send, pair)
    out, token = finished(flags, token, 2, reads[2], next_entry, out, width)
    return finished(flags, token, 0, reads[0], far_next, out, width)[0]


def solution(mesh):
    rows = P(("groups", "seq"), None)
    return jax.shard_map(
        functools.partial(local, mesh.shape["seq"]),
        mesh=mesh,
        in_specs=(rows, rows, rows, rows, rows, rows, P(), P(), P()),
        out_specs=rows,
        check_vma=False,
    )
```

```python
import functools

import jax
import jax.numpy as jnp
from jax import lax
from jax.experimental import pallas as pl
from jax.experimental.pallas import tpu as pltpu
from jax.sharding import PartitionSpec as P

NH = 2
BLOCK = 16
SPAN = 64
DK = 128
CHUNK = 128
HALF = 64
PLANE = 4
PARTS = 2
HB = 2
READ_HB = 4
VMEM = 24 << 20
SMALL = pltpu.CompilerParams(vmem_limit_bytes=8 << 20)

WHOLE = pl.BlockSpec(memory_space=pltpu.VMEM)

F32 = jnp.float32
BF16 = jnp.bfloat16
NN = (((1,), (0,)), ((), ()))
NT = (((1,), (1,)), ((), ()))


def split(x):
    high = x.astype(BF16)
    low = (x - high.astype(F32)).astype(BF16)
    return high, low


def mm(a, b, dims=NN):
    return lax.dot_general(a, b, dims, preferred_element_type=F32)


def mm3(a, b):
    ah, al = a
    bh, bl = b
    return mm(jnp.concatenate([ah, al], axis=1), jnp.concatenate([bh, bh], axis=0)) + mm(ah, bl)


def mm3_nt(a, b):
    ah, al = a
    bh, bl = b
    return mm(jnp.concatenate([ah, al], axis=1), jnp.concatenate([bh, bh], axis=1), NT) + mm(ah, bl, NT)


def halves(x):
    left = iota(x.shape, 1) < HALF
    zero = jnp.zeros_like(x)
    return jnp.concatenate([jnp.where(left, x, zero), jnp.where(left, zero, x)], axis=0)


def pair_product(x, y):
    return mm3(x, (halves(y[0]), halves(y[1])))


def silu(v):
    return v / (1.0 + jnp.exp(-v))


def load_rows(scratch, rows_ref, lanes, tail):
    before = jnp.concatenate([jnp.zeros((13, tail.shape[1]), F32), tail.astype(F32)], axis=0)
    scratch[0:16, :] = before.astype(BF16)
    scratch[16 : 16 + rows_ref.shape[0], :] = rows_ref[:, lanes]


def shifter():
    shape = (3 * HALF, HALF + 16)
    row, col = iota(shape, 0), iota(shape, 1)
    return (col == 15 + row % HALF - row // HALF).astype(F32).astype(BF16)


def conv(shifts, scratch, kernel_ref, start, count):
    parts = []
    for at in range(start, start + count, HALF):
        moved = mm(shifts, scratch[at : at + HALF + 16, :])
        total = kernel_ref[3:4, :] * scratch[at + 16 : at + 16 + HALF, :].astype(F32)
        for back in range(1, 4):
            total = total + kernel_ref[3 - back : 4 - back, :] * moved[(back - 1) * HALF : back * HALF]
        parts.append(silu(total))
    return jnp.concatenate(parts, axis=0)


def unit(x):
    return x * lax.rsqrt(jnp.sum(x * x, axis=-1, keepdims=True) + 1e-06)


CORE, CHIP, GROUPS = 0, 1, 2
FLAGS = jax.ShapeDtypeStruct((8,), jnp.int32)
FLAGS_SPEC = pl.BlockSpec(memory_space=pltpu.SMEM)
TOKEN = pltpu.VMEM((8, 128), jnp.int32)


def hand_on(token_ref, token_out):
    token_out[...] = token_ref[...]


def lanes_at(flags_ref, which, at, group, heads=HB):
    first = flags_ref[GROUPS + which] * group + at * heads
    return pl.ds(pl.multiple_of(first * DK, heads * DK), heads * DK)


def in_hbm(x):
    return pltpu.with_memory_space_constraint(x, pltpu.HBM)


def held(x):
    return pltpu.with_memory_space_constraint(x, pltpu.VMEM)


def iota(shape, dim):
    return lax.broadcasted_iota(jnp.int32, shape, dim)


def prep_kernel(at_ref, rate_ref, log_ref, mask_ref, *refs):
    rows, outs, sems = refs[:3], refs[3:-1], refs[-1]
    rate_out, cum_out, row_out, read_out, flags_out, token_out = outs[:6]
    loads = [pltpu.make_async_copy(x, y, sems.at[i]) for i, (x, y) in enumerate(zip(rows, outs[6:]))]
    for load in loads:
        load.start()
    token_out[...] = jnp.zeros_like(token_out)
    place = lax.rem(at_ref[0], PLANE)
    flags_out[CORE] = lax.rem(place, 2)
    flags_out[CHIP] = lax.div(place, 2)
    for i, other in enumerate((3, 1, 2, 0)):
        flags_out[GROUPS + i] = place ^ other
    for i in range(GROUPS + PLANE, FLAGS.shape[0]):
        flags_out[i] = 0
    heads, steps = rate_ref.shape
    tokens = log_ref.shape[1]
    group = heads // PLANE
    subs, blocks = mask_ref.shape
    row_of = (iota((steps, blocks), 0) // SPAN == iota((steps, blocks), 1)).astype(F32)
    picked = mm(row_of, mask_ref[...].astype(F32), NT)
    sub_of = ((iota((steps, subs), 0) % SPAN) // BLOCK == iota((steps, subs), 1)).astype(F32)
    keep = jnp.sum(picked * sub_of, axis=1, keepdims=True)
    rates = rate_ref[...].T * keep
    turned = log_ref[...]
    logs = turned.T
    window = CHUNK // NH

    def upto(token, last):
        return ((token // window == last // window) & (token <= last)).astype(F32)

    high = lax.Precision.HIGHEST
    cum = jnp.dot(
        upto(iota((steps, tokens), 1), iota((steps, tokens), 0) // NH), logs, precision=high, preferred_element_type=F32
    )
    read = jnp.dot(
        upto(iota((tokens, tokens), 1), iota((tokens, tokens), 0)), logs, precision=high, preferred_element_type=F32
    )
    row = jnp.dot(
        turned,
        upto(iota((tokens, steps), 0), iota((tokens, steps), 1) // NH),
        precision=high,
        preferred_element_type=F32,
    )
    for g in range(PLANE):
        rate_out[g] = rates[:, g * group : (g + 1) * group]
        cum_out[g] = cum[:, g * group : (g + 1) * group]
        read_out[g] = read[:, g * group : (g + 1) * group]
    for b in range(steps // CHUNK):
        row_out[:, b, :] = row[:, b * CHUNK : (b + 1) * CHUNK]
    for load in loads:
        load.wait()


def last_rows_kernel(query_ref, key_ref, value_ref, out_ref):
    for i, ref in enumerate((query_ref, key_ref, value_ref)):
        out_ref[3 * i : 3 * i + 3, :] = ref[...].astype(F32)[13:16].astype(BF16)


def last_rows(*arrays):
    width = arrays[0].shape[1]
    return pl.pallas_call(
        last_rows_kernel,
        grid=(1,),
        in_specs=[pl.BlockSpec((16, width), functools.partial(lambda at, i: (at, 0), x.shape[0] // 16 - 1)) for x in arrays],
        out_specs=pl.BlockSpec((9, width), lambda i: (0, 0)),
        out_shape=jax.ShapeDtypeStruct((9, width), BF16),
        compiler_params=SMALL,
        name="last_rows",
    )(*map(in_hbm, arrays))


def prep(at, write_rate, log_gate, keep_mask, *rows):
    steps, heads = write_rate.shape
    tokens = log_gate.shape[0]
    group = heads // PLANE
    return pl.pallas_call(
        prep_kernel,
        out_shape=(
            jax.ShapeDtypeStruct((PLANE, steps, group), F32),
            jax.ShapeDtypeStruct((PLANE, steps, group), F32),
            jax.ShapeDtypeStruct((heads, steps // CHUNK, CHUNK), F32),
            jax.ShapeDtypeStruct((PLANE, tokens, group), F32),
            FLAGS,
            TOKEN,
            *(pltpu.VMEM(x.shape, x.dtype) for x in rows),
        ),
        in_specs=[FLAGS_SPEC] + [WHOLE] * 3 + [pl.BlockSpec(memory_space=pltpu.HBM)] * 3,
        out_specs=[WHOLE] * 4 + [FLAGS_SPEC] + [WHOLE] * 4,
        scratch_shapes=[pltpu.SemaphoreType.DMA((3,))],
        compiler_params=pltpu.CompilerParams(vmem_limit_bytes=VMEM),
        name="prep",
    )(at, write_rate.T, log_gate.T, keep_mask.T, *(pltpu.with_memory_space_constraint(x, pltpu.HBM) for x in rows))


def block_inverses(lowers, fill):
    row = iota((HALF, CHUNK), 0)
    col = iota((HALF, CHUNK), 1) % HALF
    eye = (row == col).astype(F32)
    near = row // BLOCK == col // BLOCK
    inner = [jnp.where(near, -x, 0.0) for x in lowers]
    outer = [split(jnp.where(near, 0.0, x)) for x in lowers]
    power = [split(x) for x in inner]
    a = [eye + x for x in inner]
    for _ in range(3):
        fill()
        power = [split(pair_product(x, x)) for x in power]
        fill()
        a = [x + pair_product(split(x), y) for x, y in zip(a, power)]
    sa = [split(x) for x in a]
    fill()
    m = [split(pair_product(x, y)) for x, y in zip(sa, outer)]
    fill()
    m2 = [split(pair_product(x, x)) for x in m]
    t = [x - pair_product(y, z) for x, y, z in zip(a, m, sa)]
    return [x + pair_product(y, split(x)) for x, y in zip(t, m2)]


def maps_kernel(
    which,
    flags_ref,
    key_ref,
    value_ref,
    tail_ref,
    key_kernel_ref,
    value_kernel_ref,
    rate_ref,
    cum_ref,
    row_ref,
    token_ref,
    map_out,
    wh_out,
    wl_out,
    mh_out,
    ml_out,
    token_out,
    scratch,
    value_scratch,
):
    hand_on(token_ref, token_out)
    steps = key_ref.shape[0]
    chunks = steps // CHUNK
    at = pl.program_id(0)
    lanes = lanes_at(flags_ref, which, at, rate_ref.shape[2])
    load_rows(scratch, key_ref, lanes, tail_ref[3:6, :])
    load_rows(value_scratch, value_ref, lanes, tail_ref[6:9, :])
    shifts = shifter()
    keys = conv(shifts, scratch, key_kernel_ref, 0, steps)
    keys = jnp.concatenate([unit(keys[:, h * DK : (h + 1) * DK]) for h in range(HB)], axis=1)
    kh, kl = split(keys)
    group = rate_ref.shape[2]
    rates, cums = rate_ref[0], cum_ref[0]

    def column(x, h):
        out = x[:, h : h + 1]
        for turn in range(1, group // HB):
            out = jnp.where(at == turn, x[:, turn * HB + h : turn * HB + h + 1], out)
        return out

    below = iota((CHUNK, CHUNK), 1) < iota((CHUNK, CHUNK), 0)
    left = iota((HALF, CHUNK), 1) < HALF
    items = [(h, c) for h in range(HB) for c in range(chunks)]
    columns = [(column(rates, h), column(cums, h)) for h in range(HB)]
    lowers, crosses, sides, faded, ends = [], [], {}, {}, {}
    for h, c in items:
        lanes = slice(h * DK, (h + 1) * DK)
        rows = slice(c * CHUNK, (c + 1) * CHUNK)
        row_c = row_ref[h, c : c + 1, :]
        rate_c, cum_c = (x[rows] for x in columns[h])
        mine = (kh[rows, lanes], kl[rows, lanes])
        decay = jnp.exp(jnp.where(below, cum_c - row_c, 0.0))
        lower = jnp.where(below, rate_c * decay * mm3_nt(mine, mine), 0.0)
        lowers.append(jnp.where(left, lower[:HALF], lower[HALF:]))
        crosses.append(split(jnp.where(left, lower[HALF:], 0.0)))

    def side(c):
        rows = slice(c * CHUNK, (c + 1) * CHUNK)
        values = conv(shifts, value_scratch, value_kernel_ref, c * CHUNK, CHUNK)
        for h in range(HB):
            lanes = slice(h * DK, (h + 1) * DK)
            rate_c, cum_c = (x[rows] for x in columns[h])
            grown = rate_c * jnp.exp(cum_c) * keys[rows, lanes]
            sides[h, c] = split(jnp.concatenate([grown, rate_c * values[:, lanes]], axis=1))

    def fade(c):
        for h in range(HB):
            row_c = row_ref[h, c : c + 1, :]
            end = row_c[:, CHUNK - 1 : CHUNK]
            k_c = keys[c * CHUNK : (c + 1) * CHUNK, h * DK : (h + 1) * DK]
            faded[h, c] = split(k_c.T * jnp.exp(end - row_c))
            ends[h, c] = jnp.exp(end)

    todo = [functools.partial(f, c) for c in range(chunks) for f in (side, fade)]

    def fill():
        if todo:
            todo.pop(0)()

    eye = (iota((DK, DK), 0) == iota((DK, DK), 1)).astype(F32)
    inverses = block_inverses(lowers, fill)
    while todo:
        fill()
    pieces = [split(x) for x in inverses]
    under = [mm3(y, tuple(jnp.concatenate([z, z], axis=0) for z in x)) for x, y in zip(pieces, crosses)]
    under = [split(jnp.where(left, x, 0.0)) for x in under]
    under = [
        mm3(x, tuple(jnp.concatenate([jnp.zeros_like(z), z], axis=0) for z in y)) for x, y in zip(pieces, under)
    ]
    whole = [
        split(jnp.concatenate([jnp.where(left, x, 0.0), jnp.where(left, -y, x)], axis=0))
        for x, y in zip(inverses, under)
    ]
    solved = [split(mm3(x, sides[i])) for i, x in zip(items, whole)]
    for (h, c), x in zip(items, solved):
        at_w = slice(c * CHUNK, (c + 1) * CHUNK)
        wh_out[at * HB + h, at_w, :], wl_out[at * HB + h, at_w, :] = x
    made = [mm3(faded[i], x) for i, x in zip(items, solved)]
    made = [jnp.concatenate([ends[i] * eye - x[:, :DK], x[:, DK:]], axis=1) for i, x in zip(items, made)]

    def then(late, early):
        both = mm3(split(late[:, :DK]), early)
        return jnp.concatenate([both[:, :DK], both[:, DK:] + late[:, DK:]], axis=1)

    assert chunks == 4
    heads = range(HB)
    first, third = ([split(made[h * chunks + c]) for h in heads] for c in (0, 2))
    two = [split(then(made[h * chunks + 1], first[h])) for h in heads]
    last = [then(made[h * chunks + 3], third[h]) for h in heads]
    last = [then(last[h], two[h]) for h in heads]
    for h in heads:
        map_out[at * HB + h] = last[h]
        for i, x in enumerate((first[h], two[h], third[h])):
            at_m = slice(i * DK, (i + 1) * DK)
            mh_out[at * HB + h, at_m, :], ml_out[at * HB + h, at_m, :] = x


def group_maps(flags, token, which, key_rows, value_rows, tails, key_kernel, value_kernel, scalars):
    rate_cols, cum_cols, chunk_rows, _ = scalars
    steps, width = key_rows.shape
    heads = width // DK
    group = heads // PLANE
    turns = group // HB
    lanes = HB * DK
    chunks = steps // CHUNK

    def wide(i, g):
        return (0, g[GROUPS + which] * turns + i)

    def per_head(i, g):
        return (g[GROUPS + which] * turns + i, 0, 0)

    return pl.pallas_call(
        functools.partial(maps_kernel, which),
        grid_spec=pltpu.PrefetchScalarGridSpec(
            num_scalar_prefetch=1,
            grid=(turns,),
            in_specs=[
                WHOLE,
                WHOLE,
                pl.BlockSpec((tails.shape[0], lanes), wide),
                pl.BlockSpec((4, lanes), wide),
                pl.BlockSpec((4, lanes), wide),
                pl.BlockSpec((1, steps, group), lambda i, g: (g[GROUPS + which], 0, 0)),
                pl.BlockSpec((1, steps, group), lambda i, g: (g[GROUPS + which], 0, 0)),
                pl.BlockSpec((HB, chunks, CHUNK), per_head),
                WHOLE,
            ],
            out_specs=[
                WHOLE,
                WHOLE,
                WHOLE,
                WHOLE,
                WHOLE,
                WHOLE,
            ],
            scratch_shapes=[pltpu.VMEM((steps + 16, lanes), BF16)] * 2,
        ),
        out_shape=(
            pltpu.VMEM((group, DK, 2 * DK), F32),
            pltpu.VMEM((group, steps, 2 * DK), BF16),
            pltpu.VMEM((group, steps, 2 * DK), BF16),
            pltpu.VMEM((group, 3 * DK, 2 * DK), BF16),
            pltpu.VMEM((group, 3 * DK, 2 * DK), BF16),
            TOKEN,
        ),
        compiler_params=pltpu.CompilerParams(vmem_limit_bytes=VMEM),
        name="maps",
    )(flags, key_rows, value_rows, tails, key_kernel, value_kernel, rate_cols, cum_cols, chunk_rows, held(token))


def reads_kernel(
    which,
    flags_ref,
    query_ref,
    tail_ref,
    query_kernel_ref,
    key_ref,
    key_kernel_ref,
    read_ref,
    row_ref,
    wh_ref,
    wl_ref,
    mh_ref,
    ml_ref,
    token_ref,
    qh_out,
    ql_out,
    own_out,
    token_out,
    scratch,
    key_scratch,
):
    hand_on(token_ref, token_out)
    tokens = query_ref.shape[0]
    window = CHUNK // NH
    chunks = tokens // window
    at = pl.program_id(0)
    lanes = lanes_at(flags_ref, which, at, read_ref.shape[2], READ_HB)
    load_rows(scratch, query_ref, lanes, tail_ref[0:3, :])
    shifts = shifter()
    queries = conv(shifts, scratch, query_kernel_ref, 0, tokens)
    queries = jnp.concatenate([unit(queries[:, h * DK : (h + 1) * DK]) for h in range(READ_HB)], axis=1)
    load_rows(key_scratch, key_ref, lanes, tail_ref[3:6, :])
    keys = conv(shifts, key_scratch, key_kernel_ref, 0, NH * tokens)
    group = read_ref.shape[2]
    reads = read_ref[0]
    visible = iota((window, CHUNK), 1) <= NH * iota((window, CHUNK), 0) + NH - 1
    items = [(h, c) for h in range(READ_HB) for c in range(chunks)]
    pieces, columns, lifted = [], [], []
    for h in range(READ_HB):
        lanes = slice(h * DK, (h + 1) * DK)
        read_h = reads[:, h : h + 1]
        for turn in range(1, group // READ_HB):
            read_h = jnp.where(at == turn, reads[:, turn * READ_HB + h : turn * READ_HB + h + 1], read_h)
        columns.append(read_h)
        lifted.append(jnp.exp(read_h) * queries[:, lanes])
        pieces.append((split(queries[:, lanes]), split(unit(keys[:, lanes]))))

    def tokens_of(c):
        return slice(c * window, (c + 1) * window)

    def steps_of(c):
        return slice(c * CHUNK, (c + 1) * CHUNK)

    scores = [
        mm3_nt(tuple(x[tokens_of(c)] for x in pieces[h][0]), tuple(x[steps_of(c)] for x in pieces[h][1]))
        for h, c in items
    ]
    starts = {}
    for h in range(READ_HB):
        kept = [tuple(x[at * READ_HB + h, i * DK : (i + 1) * DK, :] for x in (mh_ref, ml_ref)) for i in range(3)]
        first, two, third = kept
        three = mm3(tuple(x[:, :DK] for x in third), two)
        late = third[0][:, DK:].astype(F32) + third[1][:, DK:].astype(F32)
        three = split(jnp.concatenate([three[:, :DK], three[:, DK:] + late], axis=1))
        starts[h] = [None, first, two, three]
    inner = []
    for (h, c), x in zip(items, scores):
        spread = columns[h][tokens_of(c)] - row_ref[h, c : c + 1, :]
        inner.append(split(jnp.where(visible, jnp.exp(jnp.where(visible, spread, 0.0)) * x, 0.0)))
    solved = [tuple(x[at * READ_HB + h, steps_of(c), :] for x in (wh_ref, wl_ref)) for h, c in items]
    got = [mm3(x, y) for x, y in zip(inner, solved)]
    eff = [lifted[h][tokens_of(c)] - x[:, :DK] for (h, c), x in zip(items, got)]
    eff_pieces = [split(x) for x in eff]
    taken = [None if c == 0 else mm3(x, starts[h][c]) for (h, c), x in zip(items, eff_pieces)]
    for (h, c), x, y, z in zip(items, eff_pieces, got, taken):
        at_out = (at * READ_HB + h, tokens_of(c))
        qh_out[at_out], ql_out[at_out] = x if c == 0 else split(z[:, :DK])
        own_out[at_out] = y[:, DK:] if c == 0 else y[:, DK:] + z[:, DK:]


def group_reads(flags, token, which, query_rows, key_rows, tails, query_kernel, key_kernel, scalars, kept):
    _, _, chunk_rows, read_cols = scalars
    tokens, width = query_rows.shape
    steps = tokens * NH
    heads = width // DK
    group = heads // PLANE
    turns = group // READ_HB
    lanes = READ_HB * DK
    chunks = steps // CHUNK

    def wide(i, g):
        return (0, g[GROUPS + which] * turns + i)

    return pl.pallas_call(
        functools.partial(reads_kernel, which),
        grid_spec=pltpu.PrefetchScalarGridSpec(
            num_scalar_prefetch=1,
            grid=(turns,),
            in_specs=[
                WHOLE,
                pl.BlockSpec((tails.shape[0], lanes), wide),
                pl.BlockSpec((4, lanes), wide),
                WHOLE,
                pl.BlockSpec((4, lanes), wide),
                pl.BlockSpec((1, tokens, group), lambda i, g: (g[GROUPS + which], 0, 0)),
                pl.BlockSpec((READ_HB, chunks, CHUNK), lambda i, g: (g[GROUPS + which] * turns + i, 0, 0)),
                WHOLE,
                WHOLE,
                WHOLE,
                WHOLE,
                WHOLE,
            ],
            out_specs=[WHOLE] * 4,
            scratch_shapes=[pltpu.VMEM((tokens + 16, lanes), BF16), pltpu.VMEM((steps + 16, lanes), BF16)],
        ),
        out_shape=(
            pltpu.VMEM((group, tokens, DK), BF16),
            pltpu.VMEM((group, tokens, DK), BF16),
            pltpu.VMEM((group, tokens, DK), F32),
            TOKEN,
        ),
        compiler_params=pltpu.CompilerParams(vmem_limit_bytes=VMEM),
        name="reads",
    )(flags, query_rows, tails, query_kernel, key_rows, key_kernel, read_cols, chunk_rows, *map(held, kept), held(token))


def small(kernel, flags, token, operands, outs, name):
    def whole(shape):
        return pl.BlockSpec(shape, lambda i, f: (0,) * len(shape))

    def body(flags_ref, token_ref, *refs):
        hand_on(token_ref, refs[-1])
        kernel(flags_ref, *refs[:-1])

    return pl.pallas_call(
        body,
        grid_spec=pltpu.PrefetchScalarGridSpec(
            num_scalar_prefetch=1,
            grid=(1,),
            in_specs=[WHOLE] + [whole(x.shape) for x in operands],
            out_specs=[whole(shape) for shape in outs] + [WHOLE],
        ),
        out_shape=[jax.ShapeDtypeStruct(shape, F32) for shape in outs] + [TOKEN],
        compiler_params=SMALL,
        name=name,
    )(flags, held(token), *operands)


def after(first, mine, other):
    early = jnp.where(first, mine, other)
    late = jnp.where(first, other, mine)
    both = mm3(split(late[:, :DK]), split(early))
    return jnp.concatenate([both[:, :DK], both[:, DK:] + late[:, DK:]], axis=1)


def compose_kernel(flags_ref, mine_ref, other_ref, out_ref):
    heads = range(mine_ref.shape[0])
    for h, x in enumerate([after(flags_ref[CORE] == 0, mine_ref[h], other_ref[h]) for h in heads]):
        out_ref[h] = x


def composed(flags, token, mine, other):
    return small(compose_kernel, flags, token, [mine, other], [mine.shape], "compose")


def plane_kernel(flags_ref, mine_ref, pair_ref, other_ref, chip_out, *outs):
    parts = len(outs) // 3
    for zero_out in outs[2 * parts :]:
        zero_out[...] = jnp.zeros_like(zero_out)
    heads = range(mine_ref.shape[0])
    chips = [after(flags_ref[CORE] == 0, mine_ref[h], pair_ref[h]) for h in heads]
    planes = [after(flags_ref[CHIP] == 0, chips[h], other_ref[h]) for h in heads]
    for h in heads:
        chip_out[h] = chips[h]
        part, at = h * parts // len(heads), h % (len(heads) // parts)
        outs[part][at] = planes[h]
        outs[parts + part][at] = planes[h][:, DK:]


def plane_composed(flags, token, mine, pair, other):
    part = mine.shape[0] // PARTS
    shapes = [(part, DK, 2 * DK)] * PARTS + [(part, DK, DK)] * (2 * PARTS)
    chip_map, *outs, token = small(plane_kernel, flags, token, [mine, pair, other], [mine.shape] + shapes, "plane")
    return chip_map, outs[:PARTS], outs[PARTS : 2 * PARTS], outs[2 * PARTS :], token


def apply_kernel(flags_ref, map_ref, held_ref, come_ref, state_out, exit_out):
    heads = range(map_ref.shape[0])
    state = [held_ref[h] + come_ref[h] for h in heads]
    got = [mm3(split(map_ref[h, :, :DK]), split(state[h])) for h in heads]
    for h in heads:
        state_out[h] = state[h]
        exit_out[h] = got[h] + map_ref[h, :, DK:]


def applied(flags, token, maps, state, come):
    return small(apply_kernel, flags, token, [maps, state, come], [state.shape] * 2, "apply")


def branches(first, mine, other, entry):
    heads = range(len(entry))
    early = [jnp.where(first, mine[h], other[h]) for h in heads]
    later = [mm3(split(early[h][:, :DK]), split(entry[h])) + early[h][:, DK:] for h in heads]
    own = [jnp.where(first, entry[h], later[h]) for h in heads]
    return own, [jnp.where(first, later[h], entry[h]) for h in heads]


def branch_kernel(flags_ref, mine_ref, other_ref, entry_ref, keep_out, send_out):
    refs = (mine_ref, other_ref, entry_ref)
    own, send = branches(flags_ref[CORE] == 0, *([x[h] for h in range(x.shape[0])] for x in refs))
    for h in range(len(own)):
        keep_out[h] = own[h]
        send_out[h] = send[h]


def branched(flags, token, mine, other, entry):
    return small(branch_kernel, flags, token, [mine, other, entry], [entry.shape] * 2, "branch")


def fork_kernel(flags_ref, chip_map_ref, from_chip_ref, map_ref, pair_ref, *refs):
    maps = (chip_map_ref, from_chip_ref, map_ref, pair_ref)
    chip_map, from_chip, mine, pair = ([x[h] for h in range(x.shape[0])] for x in maps)
    states, outs = refs[: 2 * PARTS], refs[2 * PARTS :]
    state, come = ([x[h] for x in part for h in range(x.shape[0])] for part in (states[:PARTS], states[PARTS:]))
    entry = [x + y for x, y in zip(state, come)]
    own, across = branches(flags_ref[CHIP] == 0, chip_map, from_chip, entry)
    for out_ref, states in zip(outs, (across, *branches(flags_ref[CORE] == 0, mine, pair, own))):
        for h, state in enumerate(states):
            out_ref[h] = state


def forked(flags, token, chip_map, from_chip, mine, pair, state, come):
    operands = [chip_map, from_chip, mine, pair, *state, *come]
    return small(fork_kernel, flags, token, operands, [(mine.shape[0], DK, DK)] * 3, "fork")


def finish_kernel(flags_ref, token_ref, qh_ref, ql_ref, own_ref, entry_ref, *refs):
    out_ref, token_out = refs[-2:]
    hand_on(token_ref, token_out)
    for h in range(entry_ref.shape[0]):
        lanes = slice(h * DK, (h + 1) * DK)
        got = mm3((qh_ref[h], ql_ref[h]), split(entry_ref[h]))
        out_ref[:, lanes] = (own_ref[h] + got).astype(BF16)


def finished(flags, token, which, read, entry, out, width):
    qh, ql, own, _ = read
    group, tokens, _ = qh.shape
    operands = [held(token), held(qh), held(ql), held(own), entry]
    specs = [WHOLE] * 4 + [pl.BlockSpec(entry.shape, lambda i, g: (0, 0, 0))]
    if out is not None:
        operands.append(out)
        specs.append(pl.BlockSpec(memory_space=pl.ANY))
    return pl.pallas_call(
        finish_kernel,
        grid_spec=pltpu.PrefetchScalarGridSpec(
            num_scalar_prefetch=1,
            grid=(1,),
            in_specs=specs,
            out_specs=[pl.BlockSpec((tokens, group * DK), lambda i, g: (0, g[GROUPS + which])), WHOLE],
        ),
        out_shape=[jax.ShapeDtypeStruct((tokens, width), BF16), TOKEN],
        input_output_aliases={} if out is None else {len(operands): 0},
        compiler_params=SMALL,
        name="finish",
    )(flags, *operands)


def moved(x, pairs):
    return pltpu.with_memory_space_constraint(lax.ppermute(x, "seq", pairs), pltpu.VMEM)


def local(
    count,
    query_rows,
    key_rows,
    value_rows,
    write_rate,
    log_gate,
    keep_mask,
    query_kernel,
    key_kernel,
    value_kernel,
):
    tails = moved(last_rows(query_rows, key_rows, value_rows), [(s, s + 1) for s in range(count - 1)])
    query_kernel, key_kernel, value_kernel = held(query_kernel), held(key_kernel), held(value_kernel)
    *scalars, flags, token, query_rows, key_rows, value_rows = prep(
        lax.axis_index("seq")[None], write_rate, log_gate, keep_mask, query_rows, key_rows, value_rows
    )
    query_rows, key_rows, value_rows = held(query_rows), held(key_rows), held(value_rows)
    pair = [(s, s ^ 1) for s in range(count)]
    across = [(s, s ^ 2) for s in range(count)]
    made, from_pair = {}, {}
    for i in (0, 2, 1, 3):
        *one, token = group_maps(flags, token, i, key_rows, value_rows, tails, key_kernel, value_kernel, scalars)
        made[i] = one
        if i < 2:
            from_pair[i] = moved(one[0], pair)
        if i == 2:
            next_map, token = composed(flags, token, one[0], from_pair[0])
            from_chip = moved(next_map, across)
    maps = [made[i][0] for i in range(PLANE)]
    chip_map, plane_maps, offset, state, token = plane_composed(flags, token, maps[3], from_pair[1], from_chip)

    def read(token, i):
        return group_reads(
            flags, token, i, query_rows, key_rows, tails, query_kernel, key_kernel, scalars, made[i][1:]
        )

    reads = []
    for i in range(count // PLANE - 1):
        if i > 0:
            offset = []
            for part in range(PARTS):
                state[part], part_offset, token = applied(flags, token, plane_maps[part], state[part], come[part])
                offset.append(part_offset)
        come = [moved(x, [(s, s + PLANE) for s in range(i * PLANE, (i + 1) * PLANE)]) for x in offset]
        if len(reads) < PLANE - 1:
            reads.append(read(token, i))
            token = reads[-1][-1]
    send, own_entry, own_send, token = forked(flags, token, chip_map, from_chip, maps[3], from_pair[1], state, come)
    theirs = moved(send, across)
    far_own = moved(own_send, pair)
    for i in range(len(reads), PLANE):
        reads.append(read(token, i))
        token = reads[-1][-1]
    width = query_rows.shape[1]
    out, token = finished(flags, token, 3, reads[3], own_entry, None, width)
    out, token = finished(flags, token, 1, reads[1], far_own, out, width)
    next_entry, next_send, token = branched(flags, token, maps[2], from_pair[0], theirs)
    far_next = moved(next_send, pair)
    out, token = finished(flags, token, 2, reads[2], next_entry, out, width)
    return finished(flags, token, 0, reads[0], far_next, out, width)[0]


def solution(mesh):
    rows = P(("groups", "seq"), None)
    return jax.shard_map(
        functools.partial(local, mesh.shape["seq"]),
        mesh=mesh,
        in_specs=(rows, rows, rows, rows, rows, rows, P(), P(), P()),
        out_specs=rows,
        check_vma=False,
    )
```

```python
import functools

import jax
import jax.numpy as jnp
from jax import lax
from jax.experimental import pallas as pl
from jax.experimental.pallas import tpu as pltpu
from jax.sharding import PartitionSpec as P

NH = 2
BLOCK = 16
SPAN = 64
DK = 128
CHUNK = 128
HALF = 64
PLANE = 4
PARTS = 2
HB = 2
READ_HB = 4
VMEM = 24 << 20
SMALL = pltpu.CompilerParams(vmem_limit_bytes=8 << 20)

WHOLE = pl.BlockSpec(memory_space=pltpu.VMEM)

F32 = jnp.float32
BF16 = jnp.bfloat16
NN = (((1,), (0,)), ((), ()))
NT = (((1,), (1,)), ((), ()))


def split(x):
    high = x.astype(BF16)
    low = (x - high.astype(F32)).astype(BF16)
    return high, low


def mm(a, b, dims=NN):
    return lax.dot_general(a, b, dims, preferred_element_type=F32)


def mm3(a, b):
    ah, al = a
    bh, bl = b
    return mm(jnp.concatenate([ah, al], axis=1), jnp.concatenate([bh, bh], axis=0)) + mm(ah, bl)


def mm3_nt(a, b):
    ah, al = a
    bh, bl = b
    return mm(jnp.concatenate([ah, al], axis=1), jnp.concatenate([bh, bh], axis=1), NT) + mm(ah, bl, NT)


def halves(x):
    left = iota(x.shape, 1) < HALF
    zero = jnp.zeros_like(x)
    return jnp.concatenate([jnp.where(left, x, zero), jnp.where(left, zero, x)], axis=0)


def pair_product(x, y):
    return mm3(x, (halves(y[0]), halves(y[1])))


def silu(v):
    return v / (1.0 + jnp.exp(-v))


def load_rows(scratch, rows_ref, lanes, tail):
    before = jnp.concatenate([jnp.zeros((13, tail.shape[1]), F32), tail.astype(F32)], axis=0)
    scratch[0:16, :] = before.astype(BF16)
    scratch[16 : 16 + rows_ref.shape[0], :] = rows_ref[:, lanes]


def shifter():
    shape = (3 * HALF, HALF + 16)
    row, col = iota(shape, 0), iota(shape, 1)
    return (col == 15 + row % HALF - row // HALF).astype(F32).astype(BF16)


def conv(shifts, scratch, kernel_ref, start, count):
    parts = []
    for at in range(start, start + count, HALF):
        moved = mm(shifts, scratch[at : at + HALF + 16, :])
        total = kernel_ref[3:4, :] * scratch[at + 16 : at + 16 + HALF, :].astype(F32)
        for back in range(1, 4):
            total = total + kernel_ref[3 - back : 4 - back, :] * moved[(back - 1) * HALF : back * HALF]
        parts.append(silu(total))
    return jnp.concatenate(parts, axis=0)


def unit(x):
    return x * lax.rsqrt(jnp.sum(x * x, axis=-1, keepdims=True) + 1e-06)


CORE, CHIP, GROUPS = 0, 1, 2
FLAGS = jax.ShapeDtypeStruct((8,), jnp.int32)
FLAGS_SPEC = pl.BlockSpec(memory_space=pltpu.SMEM)
TOKEN = pltpu.VMEM((8, 128), jnp.int32)


def hand_on(token_ref, token_out):
    token_out[...] = token_ref[...]


def lanes_at(flags_ref, which, at, group, heads=HB):
    first = flags_ref[GROUPS + which] * group + at * heads
    return pl.ds(pl.multiple_of(first * DK, heads * DK), heads * DK)


def in_hbm(x):
    return pltpu.with_memory_space_constraint(x, pltpu.HBM)


def held(x):
    return pltpu.with_memory_space_constraint(x, pltpu.VMEM)


def iota(shape, dim):
    return lax.broadcasted_iota(jnp.int32, shape, dim)


def prep_kernel(at_ref, rate_ref, log_ref, mask_ref, *refs):
    rows, outs, sems = refs[:3], refs[3:-1], refs[-1]
    rate_out, cum_out, row_out, read_out, flags_out, token_out = outs[:6]
    loads = [pltpu.make_async_copy(x, y, sems.at[i]) for i, (x, y) in enumerate(zip(rows, outs[6:]))]
    for load in loads:
        load.start()
    token_out[...] = jnp.zeros_like(token_out)
    place = lax.rem(at_ref[0], PLANE)
    flags_out[CORE] = lax.rem(place, 2)
    flags_out[CHIP] = lax.div(place, 2)
    for i, other in enumerate((3, 1, 2, 0)):
        flags_out[GROUPS + i] = place ^ other
    for i in range(GROUPS + PLANE, FLAGS.shape[0]):
        flags_out[i] = 0
    heads, steps = rate_ref.shape
    tokens = log_ref.shape[1]
    group = heads // PLANE
    subs, blocks = mask_ref.shape
    row_of = (iota((steps, blocks), 0) // SPAN == iota((steps, blocks), 1)).astype(F32)
    picked = mm(row_of, mask_ref[...].astype(F32), NT)
    sub_of = ((iota((steps, subs), 0) % SPAN) // BLOCK == iota((steps, subs), 1)).astype(F32)
    keep = jnp.sum(picked * sub_of, axis=1, keepdims=True)
    rates = rate_ref[...].T * keep
    turned = log_ref[...]
    logs = turned.T
    window = CHUNK // NH

    def upto(token, last):
        return ((token // window == last // window) & (token <= last)).astype(F32)

    high = lax.Precision.HIGHEST
    cum = jnp.dot(
        upto(iota((steps, tokens), 1), iota((steps, tokens), 0) // NH), logs, precision=high, preferred_element_type=F32
    )
    read = jnp.dot(
        upto(iota((tokens, tokens), 1), iota((tokens, tokens), 0)), logs, precision=high, preferred_element_type=F32
    )
    row = jnp.dot(
        turned,
        upto(iota((tokens, steps), 0), iota((tokens, steps), 1) // NH),
        precision=high,
        preferred_element_type=F32,
    )
    for g in range(PLANE):
        rate_out[g] = rates[:, g * group : (g + 1) * group]
        cum_out[g] = cum[:, g * group : (g + 1) * group]
        read_out[g] = read[:, g * group : (g + 1) * group]
    for b in range(steps // CHUNK):
        row_out[:, b, :] = row[:, b * CHUNK : (b + 1) * CHUNK]
    for load in loads:
        load.wait()


def last_rows_kernel(query_ref, key_ref, value_ref, out_ref):
    for i, ref in enumerate((query_ref, key_ref, value_ref)):
        out_ref[3 * i : 3 * i + 3, :] = ref[...].astype(F32)[13:16].astype(BF16)


def last_rows(*arrays):
    width = arrays[0].shape[1]
    return pl.pallas_call(
        last_rows_kernel,
        grid=(1,),
        in_specs=[pl.BlockSpec((16, width), functools.partial(lambda at, i: (at, 0), x.shape[0] // 16 - 1)) for x in arrays],
        out_specs=pl.BlockSpec((9, width), lambda i: (0, 0)),
        out_shape=jax.ShapeDtypeStruct((9, width), BF16),
        compiler_params=SMALL,
        name="last_rows",
    )(*map(in_hbm, arrays))


def prep(at, write_rate, log_gate, keep_mask, *rows):
    steps, heads = write_rate.shape
    tokens = log_gate.shape[0]
    group = heads // PLANE
    return pl.pallas_call(
        prep_kernel,
        out_shape=(
            jax.ShapeDtypeStruct((PLANE, steps, group), F32),
            jax.ShapeDtypeStruct((PLANE, steps, group), F32),
            jax.ShapeDtypeStruct((heads, steps // CHUNK, CHUNK), F32),
            jax.ShapeDtypeStruct((PLANE, tokens, group), F32),
            FLAGS,
            TOKEN,
            *(pltpu.VMEM(x.shape, x.dtype) for x in rows),
        ),
        in_specs=[FLAGS_SPEC] + [WHOLE] * 3 + [pl.BlockSpec(memory_space=pltpu.HBM)] * 3,
        out_specs=[WHOLE] * 4 + [FLAGS_SPEC] + [WHOLE] * 4,
        scratch_shapes=[pltpu.SemaphoreType.DMA((3,))],
        compiler_params=pltpu.CompilerParams(vmem_limit_bytes=VMEM),
        name="prep",
    )(at, write_rate.T, log_gate.T, keep_mask.T, *(pltpu.with_memory_space_constraint(x, pltpu.HBM) for x in rows))


def block_inverses(lowers, fill):
    row = iota((HALF, CHUNK), 0)
    col = iota((HALF, CHUNK), 1) % HALF
    eye = (row == col).astype(F32)
    near = row // BLOCK == col // BLOCK
    inner = [jnp.where(near, -x, 0.0) for x in lowers]
    outer = [split(jnp.where(near, 0.0, x)) for x in lowers]
    power = [split(x) for x in inner]
    a = [eye + x for x in inner]
    for _ in range(3):
        fill()
        power = [split(pair_product(x, x)) for x in power]
        fill()
        a = [x + pair_product(split(x), y) for x, y in zip(a, power)]
    sa = [split(x) for x in a]
    fill()
    m = [split(pair_product(x, y)) for x, y in zip(sa, outer)]
    fill()
    m2 = [split(pair_product(x, x)) for x in m]
    t = [x - pair_product(y, z) for x, y, z in zip(a, m, sa)]
    return [x + pair_product(y, split(x)) for x, y in zip(t, m2)]


def maps_kernel(
    which,
    flags_ref,
    key_ref,
    value_ref,
    tail_ref,
    key_kernel_ref,
    value_kernel_ref,
    rate_ref,
    cum_ref,
    row_ref,
    token_ref,
    map_out,
    wh_out,
    wl_out,
    mh_out,
    ml_out,
    token_out,
    scratch,
    value_scratch,
):
    hand_on(token_ref, token_out)
    steps = key_ref.shape[0]
    chunks = steps // CHUNK
    at = pl.program_id(0)
    lanes = lanes_at(flags_ref, which, at, rate_ref.shape[2])
    load_rows(scratch, key_ref, lanes, tail_ref[3:6, :])
    load_rows(value_scratch, value_ref, lanes, tail_ref[6:9, :])
    shifts = shifter()
    keys = conv(shifts, scratch, key_kernel_ref, 0, steps)
    keys = jnp.concatenate([unit(keys[:, h * DK : (h + 1) * DK]) for h in range(HB)], axis=1)
    kh, kl = split(keys)
    group = rate_ref.shape[2]
    rates, cums = rate_ref[0], cum_ref[0]

    def column(x, h):
        out = x[:, h : h + 1]
        for turn in range(1, group // HB):
            out = jnp.where(at == turn, x[:, turn * HB + h : turn * HB + h + 1], out)
        return out

    below = iota((CHUNK, CHUNK), 1) < iota((CHUNK, CHUNK), 0)
    left = iota((HALF, CHUNK), 1) < HALF
    items = [(h, c) for h in range(HB) for c in range(chunks)]
    columns = [(column(rates, h), column(cums, h)) for h in range(HB)]
    lowers, crosses, sides, faded, ends = [], [], {}, {}, {}
    for h, c in items:
        lanes = slice(h * DK, (h + 1) * DK)
        rows = slice(c * CHUNK, (c + 1) * CHUNK)
        row_c = row_ref[h, c : c + 1, :]
        rate_c, cum_c = (x[rows] for x in columns[h])
        mine = (kh[rows, lanes], kl[rows, lanes])
        decay = jnp.exp(jnp.where(below, cum_c - row_c, 0.0))
        lower = jnp.where(below, rate_c * decay * mm3_nt(mine, mine), 0.0)
        lowers.append(jnp.where(left, lower[:HALF], lower[HALF:]))
        crosses.append(split(jnp.where(left, lower[HALF:], 0.0)))

    def side(c):
        rows = slice(c * CHUNK, (c + 1) * CHUNK)
        values = conv(shifts, value_scratch, value_kernel_ref, c * CHUNK, CHUNK)
        for h in range(HB):
            lanes = slice(h * DK, (h + 1) * DK)
            rate_c, cum_c = (x[rows] for x in columns[h])
            grown = rate_c * jnp.exp(cum_c) * keys[rows, lanes]
            sides[h, c] = split(jnp.concatenate([grown, rate_c * values[:, lanes]], axis=1))

    def fade(c):
        for h in range(HB):
            row_c = row_ref[h, c : c + 1, :]
            end = row_c[:, CHUNK - 1 : CHUNK]
            k_c = keys[c * CHUNK : (c + 1) * CHUNK, h * DK : (h + 1) * DK]
            faded[h, c] = split(k_c.T * jnp.exp(end - row_c))
            ends[h, c] = jnp.exp(end)

    todo = [functools.partial(f, c) for c in range(chunks) for f in (side, fade)]

    def fill():
        if todo:
            todo.pop(0)()

    eye = (iota((DK, DK), 0) == iota((DK, DK), 1)).astype(F32)
    inverses = block_inverses(lowers, fill)
    while todo:
        fill()
    pieces = [split(x) for x in inverses]
    under = [mm3(y, tuple(jnp.concatenate([z, z], axis=0) for z in x)) for x, y in zip(pieces, crosses)]
    under = [split(jnp.where(left, x, 0.0)) for x in under]
    under = [
        mm3(x, tuple(jnp.concatenate([jnp.zeros_like(z), z], axis=0) for z in y)) for x, y in zip(pieces, under)
    ]
    whole = [
        split(jnp.concatenate([jnp.where(left, x, 0.0), jnp.where(left, -y, x)], axis=0))
        for x, y in zip(inverses, under)
    ]
    solved = [split(mm3(x, sides[i])) for i, x in zip(items, whole)]
    for (h, c), x in zip(items, solved):
        at_w = slice(c * CHUNK, (c + 1) * CHUNK)
        wh_out[at * HB + h, at_w, :], wl_out[at * HB + h, at_w, :] = x
    made = [mm3(faded[i], x) for i, x in zip(items, solved)]
    made = [jnp.concatenate([ends[i] * eye - x[:, :DK], x[:, DK:]], axis=1) for i, x in zip(items, made)]

    def then(late, early):
        both = mm3(split(late[:, :DK]), early)
        return jnp.concatenate([both[:, :DK], both[:, DK:] + late[:, DK:]], axis=1)

    assert chunks == 4
    heads = range(HB)
    first, third = ([split(made[h * chunks + c]) for h in heads] for c in (0, 2))
    two = [split(then(made[h * chunks + 1], first[h])) for h in heads]
    last = [then(made[h * chunks + 3], third[h]) for h in heads]
    last = [then(last[h], two[h]) for h in heads]
    for h in heads:
        map_out[at * HB + h] = last[h]
        for i, x in enumerate((first[h], two[h], third[h])):
            at_m = slice(i * DK, (i + 1) * DK)
            mh_out[at * HB + h, at_m, :], ml_out[at * HB + h, at_m, :] = x


def group_maps(flags, token, which, key_rows, value_rows, tails, key_kernel, value_kernel, scalars):
    rate_cols, cum_cols, chunk_rows, _ = scalars
    steps, width = key_rows.shape
    heads = width // DK
    group = heads // PLANE
    turns = group // HB
    lanes = HB * DK
    chunks = steps // CHUNK

    def wide(i, g):
        return (0, g[GROUPS + which] * turns + i)

    def per_head(i, g):
        return (g[GROUPS + which] * turns + i, 0, 0)

    return pl.pallas_call(
        functools.partial(maps_kernel, which),
        grid_spec=pltpu.PrefetchScalarGridSpec(
            num_scalar_prefetch=1,
            grid=(turns,),
            in_specs=[
                WHOLE,
                WHOLE,
                pl.BlockSpec((tails.shape[0], lanes), wide),
                pl.BlockSpec((4, lanes), wide),
                pl.BlockSpec((4, lanes), wide),
                pl.BlockSpec((1, steps, group), lambda i, g: (g[GROUPS + which], 0, 0)),
                pl.BlockSpec((1, steps, group), lambda i, g: (g[GROUPS + which], 0, 0)),
                pl.BlockSpec((HB, chunks, CHUNK), per_head),
                WHOLE,
            ],
            out_specs=[
                WHOLE,
                WHOLE,
                WHOLE,
                WHOLE,
                WHOLE,
                WHOLE,
            ],
            scratch_shapes=[pltpu.VMEM((steps + 16, lanes), BF16)] * 2,
        ),
        out_shape=(
            pltpu.VMEM((group, DK, 2 * DK), F32),
            pltpu.VMEM((group, steps, 2 * DK), BF16),
            pltpu.VMEM((group, steps, 2 * DK), BF16),
            pltpu.VMEM((group, 3 * DK, 2 * DK), BF16),
            pltpu.VMEM((group, 3 * DK, 2 * DK), BF16),
            TOKEN,
        ),
        compiler_params=pltpu.CompilerParams(vmem_limit_bytes=VMEM),
        name="maps",
    )(flags, key_rows, value_rows, tails, key_kernel, value_kernel, rate_cols, cum_cols, chunk_rows, held(token))


def reads_kernel(
    which,
    flags_ref,
    query_ref,
    tail_ref,
    query_kernel_ref,
    key_ref,
    key_kernel_ref,
    read_ref,
    row_ref,
    wh_ref,
    wl_ref,
    mh_ref,
    ml_ref,
    token_ref,
    qh_out,
    ql_out,
    own_out,
    token_out,
    scratch,
    key_scratch,
):
    hand_on(token_ref, token_out)
    tokens = query_ref.shape[0]
    window = CHUNK // NH
    chunks = tokens // window
    at = pl.program_id(0)
    lanes = lanes_at(flags_ref, which, at, read_ref.shape[2], READ_HB)
    load_rows(scratch, query_ref, lanes, tail_ref[0:3, :])
    shifts = shifter()
    queries = conv(shifts, scratch, query_kernel_ref, 0, tokens)
    queries = jnp.concatenate([unit(queries[:, h * DK : (h + 1) * DK]) for h in range(READ_HB)], axis=1)
    load_rows(key_scratch, key_ref, lanes, tail_ref[3:6, :])
    keys = conv(shifts, key_scratch, key_kernel_ref, 0, NH * tokens)
    group = read_ref.shape[2]
    reads = read_ref[0]
    visible = iota((window, CHUNK), 1) <= NH * iota((window, CHUNK), 0) + NH - 1
    items = [(h, c) for h in range(READ_HB) for c in range(chunks)]
    pieces, columns, lifted = [], [], []
    for h in range(READ_HB):
        lanes = slice(h * DK, (h + 1) * DK)
        read_h = reads[:, h : h + 1]
        for turn in range(1, group // READ_HB):
            read_h = jnp.where(at == turn, reads[:, turn * READ_HB + h : turn * READ_HB + h + 1], read_h)
        columns.append(read_h)
        lifted.append(jnp.exp(read_h) * queries[:, lanes])
        pieces.append((split(queries[:, lanes]), split(unit(keys[:, lanes]))))

    def tokens_of(c):
        return slice(c * window, (c + 1) * window)

    def steps_of(c):
        return slice(c * CHUNK, (c + 1) * CHUNK)

    scores = [
        mm3_nt(tuple(x[tokens_of(c)] for x in pieces[h][0]), tuple(x[steps_of(c)] for x in pieces[h][1]))
        for h, c in items
    ]
    starts = {}
    for h in range(READ_HB):
        kept = [tuple(x[at * READ_HB + h, i * DK : (i + 1) * DK, :] for x in (mh_ref, ml_ref)) for i in range(3)]
        first, two, third = kept
        three = mm3(tuple(x[:, :DK] for x in third), two)
        late = third[0][:, DK:].astype(F32) + third[1][:, DK:].astype(F32)
        three = split(jnp.concatenate([three[:, :DK], three[:, DK:] + late], axis=1))
        starts[h] = [None, first, two, three]
    inner = []
    for (h, c), x in zip(items, scores):
        spread = columns[h][tokens_of(c)] - row_ref[h, c : c + 1, :]
        inner.append(split(jnp.where(visible, jnp.exp(jnp.where(visible, spread, 0.0)) * x, 0.0)))
    solved = [tuple(x[at * READ_HB + h, steps_of(c), :] for x in (wh_ref, wl_ref)) for h, c in items]
    got = [mm3(x, y) for x, y in zip(inner, solved)]
    eff = [lifted[h][tokens_of(c)] - x[:, :DK] for (h, c), x in zip(items, got)]
    eff_pieces = [split(x) for x in eff]
    taken = [None if c == 0 else mm3(x, starts[h][c]) for (h, c), x in zip(items, eff_pieces)]
    for (h, c), x, y, z in zip(items, eff_pieces, got, taken):
        at_out = (at * READ_HB + h, tokens_of(c))
        qh_out[at_out], ql_out[at_out] = x if c == 0 else split(z[:, :DK])
        own_out[at_out] = y[:, DK:] if c == 0 else y[:, DK:] + z[:, DK:]


def group_reads(flags, token, which, query_rows, key_rows, tails, query_kernel, key_kernel, scalars, kept):
    _, _, chunk_rows, read_cols = scalars
    tokens, width = query_rows.shape
    steps = tokens * NH
    heads = width // DK
    group = heads // PLANE
    turns = group // READ_HB
    lanes = READ_HB * DK
    chunks = steps // CHUNK

    def wide(i, g):
        return (0, g[GROUPS + which] * turns + i)

    return pl.pallas_call(
        functools.partial(reads_kernel, which),
        grid_spec=pltpu.PrefetchScalarGridSpec(
            num_scalar_prefetch=1,
            grid=(turns,),
            in_specs=[
                WHOLE,
                pl.BlockSpec((tails.shape[0], lanes), wide),
                pl.BlockSpec((4, lanes), wide),
                WHOLE,
                pl.BlockSpec((4, lanes), wide),
                pl.BlockSpec((1, tokens, group), lambda i, g: (g[GROUPS + which], 0, 0)),
                pl.BlockSpec((READ_HB, chunks, CHUNK), lambda i, g: (g[GROUPS + which] * turns + i, 0, 0)),
                WHOLE,
                WHOLE,
                WHOLE,
                WHOLE,
                WHOLE,
            ],
            out_specs=[WHOLE] * 4,
            scratch_shapes=[pltpu.VMEM((tokens + 16, lanes), BF16), pltpu.VMEM((steps + 16, lanes), BF16)],
        ),
        out_shape=(
            pltpu.VMEM((group, tokens, DK), BF16),
            pltpu.VMEM((group, tokens, DK), BF16),
            pltpu.VMEM((group, tokens, DK), F32),
            TOKEN,
        ),
        compiler_params=pltpu.CompilerParams(vmem_limit_bytes=VMEM),
        name="reads",
    )(flags, query_rows, tails, query_kernel, key_rows, key_kernel, read_cols, chunk_rows, *map(held, kept), held(token))


def small(kernel, flags, token, operands, outs, name):
    def whole(shape):
        return pl.BlockSpec(shape, lambda i, f: (0,) * len(shape))

    def body(flags_ref, token_ref, *refs):
        hand_on(token_ref, refs[-1])
        kernel(flags_ref, *refs[:-1])

    return pl.pallas_call(
        body,
        grid_spec=pltpu.PrefetchScalarGridSpec(
            num_scalar_prefetch=1,
            grid=(1,),
            in_specs=[WHOLE] + [whole(x.shape) for x in operands],
            out_specs=[whole(shape) for shape in outs] + [WHOLE],
        ),
        out_shape=[jax.ShapeDtypeStruct(shape, F32) for shape in outs] + [TOKEN],
        compiler_params=SMALL,
        name=name,
    )(flags, held(token), *operands)


def after(first, mine, other):
    early = jnp.where(first, mine, other)
    late = jnp.where(first, other, mine)
    both = mm3(split(late[:, :DK]), split(early))
    return jnp.concatenate([both[:, :DK], both[:, DK:] + late[:, DK:]], axis=1)


def compose_kernel(flags_ref, mine_ref, other_ref, out_ref):
    heads = range(mine_ref.shape[0])
    for h, x in enumerate([after(flags_ref[CORE] == 0, mine_ref[h], other_ref[h]) for h in heads]):
        out_ref[h] = x


def composed(flags, token, mine, other):
    return small(compose_kernel, flags, token, [mine, other], [mine.shape], "compose")


def plane_kernel(flags_ref, mine_ref, pair_ref, other_ref, chip_out, *outs):
    parts = len(outs) // 3
    for zero_out in outs[2 * parts :]:
        zero_out[...] = jnp.zeros_like(zero_out)
    heads = range(mine_ref.shape[0])
    chips = [after(flags_ref[CORE] == 0, mine_ref[h], pair_ref[h]) for h in heads]
    planes = [after(flags_ref[CHIP] == 0, chips[h], other_ref[h]) for h in heads]
    for h in heads:
        chip_out[h] = chips[h]
        part, at = h * parts // len(heads), h % (len(heads) // parts)
        outs[part][at] = planes[h]
        outs[parts + part][at] = planes[h][:, DK:]


def plane_composed(flags, token, mine, pair, other):
    part = mine.shape[0] // PARTS
    shapes = [(part, DK, 2 * DK)] * PARTS + [(part, DK, DK)] * (2 * PARTS)
    chip_map, *outs, token = small(plane_kernel, flags, token, [mine, pair, other], [mine.shape] + shapes, "plane")
    return chip_map, outs[:PARTS], outs[PARTS : 2 * PARTS], outs[2 * PARTS :], token


def apply_kernel(flags_ref, map_ref, held_ref, come_ref, state_out, exit_out):
    heads = range(map_ref.shape[0])
    state = [held_ref[h] + come_ref[h] for h in heads]
    got = [mm3(split(map_ref[h, :, :DK]), split(state[h])) for h in heads]
    for h in heads:
        state_out[h] = state[h]
        exit_out[h] = got[h] + map_ref[h, :, DK:]


def applied(flags, token, maps, state, come):
    return small(apply_kernel, flags, token, [maps, state, come], [state.shape] * 2, "apply")


def branches(first, mine, other, entry):
    heads = range(len(entry))
    early = [jnp.where(first, mine[h], other[h]) for h in heads]
    later = [mm3(split(early[h][:, :DK]), split(entry[h])) + early[h][:, DK:] for h in heads]
    own = [jnp.where(first, entry[h], later[h]) for h in heads]
    return own, [jnp.where(first, later[h], entry[h]) for h in heads]


def branch_kernel(flags_ref, mine_ref, other_ref, entry_ref, keep_out, send_out):
    refs = (mine_ref, other_ref, entry_ref)
    own, send = branches(flags_ref[CORE] == 0, *([x[h] for h in range(x.shape[0])] for x in refs))
    for h in range(len(own)):
        keep_out[h] = own[h]
        send_out[h] = send[h]


def branched(flags, token, mine, other, entry):
    return small(branch_kernel, flags, token, [mine, other, entry], [entry.shape] * 2, "branch")


def fork_kernel(flags_ref, chip_map_ref, from_chip_ref, map_ref, pair_ref, *refs):
    maps = (chip_map_ref, from_chip_ref, map_ref, pair_ref)
    chip_map, from_chip, mine, pair = ([x[h] for h in range(x.shape[0])] for x in maps)
    states, outs = refs[: 2 * PARTS], refs[2 * PARTS :]
    state, come = ([x[h] for x in part for h in range(x.shape[0])] for part in (states[:PARTS], states[PARTS:]))
    entry = [x + y for x, y in zip(state, come)]
    own, across = branches(flags_ref[CHIP] == 0, chip_map, from_chip, entry)
    for out_ref, states in zip(outs, (across, *branches(flags_ref[CORE] == 0, mine, pair, own))):
        for h, state in enumerate(states):
            out_ref[h] = state


def forked(flags, token, chip_map, from_chip, mine, pair, state, come):
    operands = [chip_map, from_chip, mine, pair, *state, *come]
    return small(fork_kernel, flags, token, operands, [(mine.shape[0], DK, DK)] * 3, "fork")


def finish_kernel(flags_ref, token_ref, qh_ref, ql_ref, own_ref, entry_ref, *refs):
    out_ref, token_out = refs[-2:]
    hand_on(token_ref, token_out)
    count = out_ref.shape[0]
    rows = pl.ds(pl.multiple_of(pl.program_id(0) * count, count), count)
    for h in range(entry_ref.shape[0]):
        lanes = slice(h * DK, (h + 1) * DK)
        got = mm3((qh_ref[h, rows, :], ql_ref[h, rows, :]), split(entry_ref[h]))
        out_ref[:, lanes] = (own_ref[h, rows, :] + got).astype(BF16)


def finished(flags, token, which, read, entry, out, width):
    qh, ql, own, _ = read
    group, tokens, _ = qh.shape
    operands = [held(token), held(qh), held(ql), held(own), entry]
    specs = [WHOLE] * 4 + [pl.BlockSpec(entry.shape, lambda i, g: (0, 0, 0))]
    if out is not None:
        operands.append(out)
        specs.append(pl.BlockSpec(memory_space=pl.ANY))
    return pl.pallas_call(
        finish_kernel,
        grid_spec=pltpu.PrefetchScalarGridSpec(
            num_scalar_prefetch=1,
            grid=(2,),
            in_specs=specs,
            out_specs=[pl.BlockSpec((tokens // 2, group * DK), lambda i, g: (i, g[GROUPS + which])), WHOLE],
        ),
        out_shape=[jax.ShapeDtypeStruct((tokens, width), BF16), TOKEN],
        input_output_aliases={} if out is None else {len(operands): 0},
        compiler_params=SMALL,
        name="finish",
    )(flags, *operands)


def moved(x, pairs):
    return pltpu.with_memory_space_constraint(lax.ppermute(x, "seq", pairs), pltpu.VMEM)


def local(
    count,
    query_rows,
    key_rows,
    value_rows,
    write_rate,
    log_gate,
    keep_mask,
    query_kernel,
    key_kernel,
    value_kernel,
):
    tails = moved(last_rows(query_rows, key_rows, value_rows), [(s, s + 1) for s in range(count - 1)])
    query_kernel, key_kernel, value_kernel = held(query_kernel), held(key_kernel), held(value_kernel)
    *scalars, flags, token, query_rows, key_rows, value_rows = prep(
        lax.axis_index("seq")[None], write_rate, log_gate, keep_mask, query_rows, key_rows, value_rows
    )
    query_rows, key_rows, value_rows = held(query_rows), held(key_rows), held(value_rows)
    pair = [(s, s ^ 1) for s in range(count)]
    across = [(s, s ^ 2) for s in range(count)]
    made, from_pair = {}, {}
    for i in (0, 2, 1, 3):
        *one, token = group_maps(flags, token, i, key_rows, value_rows, tails, key_kernel, value_kernel, scalars)
        made[i] = one
        if i < 2:
            from_pair[i] = moved(one[0], pair)
        if i == 2:
            next_map, token = composed(flags, token, one[0], from_pair[0])
            from_chip = moved(next_map, across)
    maps = [made[i][0] for i in range(PLANE)]
    chip_map, plane_maps, offset, state, token = plane_composed(flags, token, maps[3], from_pair[1], from_chip)

    def read(token, i):
        return group_reads(
            flags, token, i, query_rows, key_rows, tails, query_kernel, key_kernel, scalars, made[i][1:]
        )

    reads = []
    for i in range(count // PLANE - 1):
        if i > 0:
            offset = []
            for part in range(PARTS):
                state[part], part_offset, token = applied(flags, token, plane_maps[part], state[part], come[part])
                offset.append(part_offset)
        come = [moved(x, [(s, s + PLANE) for s in range(i * PLANE, (i + 1) * PLANE)]) for x in offset]
        if len(reads) < PLANE - 1:
            reads.append(read(token, i))
            token = reads[-1][-1]
    send, own_entry, own_send, token = forked(flags, token, chip_map, from_chip, maps[3], from_pair[1], state, come)
    theirs = moved(send, across)
    far_own = moved(own_send, pair)
    for i in range(len(reads), PLANE):
        reads.append(read(token, i))
        token = reads[-1][-1]
    width = query_rows.shape[1]
    out, token = finished(flags, token, 3, reads[3], own_entry, None, width)
    out, token = finished(flags, token, 1, reads[1], far_own, out, width)
    next_entry, next_send, token = branched(flags, token, maps[2], from_pair[0], theirs)
    far_next = moved(next_send, pair)
    out, token = finished(flags, token, 2, reads[2], next_entry, out, width)
    return finished(flags, token, 0, reads[0], far_next, out, width)[0]


def solution(mesh):
    rows = P(("groups", "seq"), None)
    return jax.shard_map(
        functools.partial(local, mesh.shape["seq"]),
        mesh=mesh,
        in_specs=(rows, rows, rows, rows, rows, rows, P(), P(), P()),
        out_specs=rows,
        check_vma=False,
    )
```
